32 devices in a mesh: dp: 8 (over z, y), chan: 4 (over x, core).
Axes of the slice: x: 2, y: 2, z: 4, core: 2. Of those that a mesh axis runs over, the one named last changes fastest.
Arguments:
- hidden_in: bfloat16 [768, 32768], P('chan', 'dp'), may hold values from -6 to 6
- lengths_short: int32 [128], P('dp'), may hold values from 32 to 128, as said below
- lengths_long: int32 [32], P('dp'), may hold values from 128 to 512, as said below
- qkv_weight: bfloat16 [4, 192, 576], P('chan'), may hold values from -0.4375 to 0.4375
- qv_bias: float32 [4, 384], P('chan'), may hold values from -1.75 to 1.75
- out_weight: bfloat16 [768, 768], P('chan'), may hold values from -2 to 2
- mixer_bias: float32 [768], replicated, may hold values from -3 to 3
- first_gain: float32 [768], replicated, may hold values from 0.5 to 1.5
- first_shift: float32 [768], replicated, may hold values from -3 to 3
- up_weight: bfloat16 [192, 3072], P(None, 'chan'), may hold values from -0.4375 to 0.4375
- up_bias: float32 [3072], P('chan'), may hold values from -1.75 to 1.75
- down_weight: bfloat16 [192, 3072], P(None, 'chan'), may hold values from -0.21875 to 0.21875
- down_bias: float32 [768], replicated, may hold values from -3 to 3
- second_gain: float32 [768], replicated, may hold values from 0.5 to 1.5
- second_shift: float32 [768], replicated, may hold values from -3 to 3
- out_grad: bfloat16 [32768, 768], P(('dp', 'chan')), may hold values from -6 to 6
Outputs:
- layer_out: bfloat16 [32768, 768], P(('dp', 'chan'))
- grad_input: float32 [768, 32768], P('chan', 'dp')
- grad_qkv_weight: float32 [4, 192, 576], P('chan', None, 'dp')
- grad_qv_bias: float32 [4, 384], P('chan')
- grad_out_weight: float32 [768, 768], P('chan', 'dp')
- grad_mixer_bias: float32 [768], P(('dp', 'chan'))
- grad_first_gain: float32 [768], P(('dp', 'chan'))
- grad_first_shift: float32 [768], P(('dp', 'chan'))
- grad_up_weight: float32 [192, 3072], P('dp', 'chan')
- grad_up_bias: float32 [3072], P('chan')
- grad_down_weight: float32 [192, 3072], P('dp', 'chan')
- grad_down_bias: float32 [768], P(('dp', 'chan'))
- grad_second_gain: float32 [768], P(('dp', 'chan'))
- grad_second_shift: float32 [768], P(('dp', 'chan'))
The draws below stay inside these ranges and needn't reach their ends.
Inputs may be any that keep to these rules, and one draw needn't show every extreme that they name: `lengths_short`: tokens of a short sequence at positions under its length are valid keys; at least one short sequence has all 128 valid. `lengths_long`: likewise for the long sequences; at least one has all 512 valid.
All inputs are finite; a program needn't handle non-finite values.
Results may differ from the reference program's by a relative error of at most 0.017.
Values may be sent and summed in bfloat16 or wider, within the bound.
No kernel may reach another device: no remote copies, remote signals or barrier semaphores. Data moves between devices by JAX's collectives and lax.ppermute only.
A program may use at most 192 MiB of HBM per device.

```python
import jax
import jax.numpy as jnp
from jax import lax

HD = 64
FF = 3072
G = 4
LS = 128
LL = 512
NS = 16
NL = 4
D = 768
TOK_DEV = 4096
TOKENS = 32768


def draw_lengths(key, count, length):
    values = jax.random.randint(key, (count,), length // 4, length + 1).astype(jnp.int32)
    return values.at[0].set(length)


def draw_lengths_short(key, part):
    return draw_lengths(jax.random.fold_in(key, 11), TOKENS // TOK_DEV * NS, LS)


def draw_lengths_long(key, part):
    return draw_lengths(jax.random.fold_in(key, 23), TOKENS // TOK_DEV * NL, LL)


def spiked(entries, rng, source, target, blocks, factor):
    owner, partner = [(jnp.arange(entries.shape[dim]) // (entries.shape[dim] // blocks)).reshape([-1 if axis == dim else 1 for axis in range(entries.ndim)]) for dim in (source, target)]
    chosen = jax.random.permutation(rng, blocks)[partner]
    strong = (owner == chosen) | (owner == (partner + blocks // 2) % blocks)
    return jnp.where(strong, factor * entries, entries)


def steps_of(stream_key, dims, pieces, smallest, largest):
    def one(dim, parts):
        heights = jax.random.uniform(jax.random.fold_in(jax.random.fold_in(stream_key, 6), dim), (parts,), jnp.float32, smallest / len(pieces), largest / len(pieces))
        return jnp.repeat(jnp.exp(heights), dims[dim] // parts).reshape((-1,) + (1,) * (len(dims) - dim - 1))

    level = one(*pieces[0])
    for cut in pieces[1:]:
        level = level * one(*cut)
    return level


def scatter_about(stream_key, dims, scale, reach, shards=(), held_as=jnp.bfloat16):
    level = steps_of(stream_key, dims, shards, -0.22, 0.18) if shards else 1.0
    drawn = jax.random.normal(stream_key, dims, jnp.float32) * scale * level
    return jnp.minimum(jnp.maximum(drawn, -reach), reach).astype(held_as)


def gaussian_with(rng, dims, scale, bound, shards, heavy, kind=jnp.bfloat16):
    values = scale * jax.random.normal(rng, dims, jnp.float32)
    if shards:
        values = values * steps_of(rng, dims, shards, -0.22, 0.18)
    return jnp.clip(spiked(values, jax.random.fold_in(rng, 3), *heavy), -bound, bound).astype(kind)


def setup_inputs(seed: int = 0) -> dict:
    streams_of = jax.random.split(jax.random.key(seed), 17)
    return {
        "hidden_in": scatter_about(streams_of[0], (D, TOKENS), 1.0, 6.0, ((0, 4), (1, 8))),
        "lengths_short": draw_lengths_short(jax.random.fold_in(streams_of[16], 71), 0),
        "lengths_long": draw_lengths_long(jax.random.fold_in(streams_of[16], 71), 0),
        "qkv_weight": scatter_about(streams_of[3], (G, D // G, 3 * D // G), (D // G) ** -0.5, 0.4375, ((0, 4),)),
        "qv_bias": scatter_about(streams_of[4], (G, 2 * D // G), 0.3, 1.75, ((0, 4),), jnp.float32),
        "out_weight": scatter_about(streams_of[5], (D, D), (max(D // 96, 2)) ** -0.5, 2.0, ((0, 4),)),
        "mixer_bias": scatter_about(streams_of[6], (D,), 0.5, 3.0, (), jnp.float32),
        "first_gain": jnp.clip(1.0 + 0.1 * jax.random.normal(streams_of[7], (D,), jnp.float32), 0.5, 1.5),
        "first_shift": scatter_about(streams_of[8], (D,), 0.5, 3.0, (), jnp.float32),
        "up_weight": scatter_about(streams_of[9], (D // G, FF), (D // G) ** -0.5, 0.4375, ((1, 4),)),
        "up_bias": scatter_about(streams_of[10], (FF,), 0.3, 1.75, ((0, 4),), jnp.float32),
        "down_weight": scatter_about(streams_of[11], (D // G, FF), (FF // G) ** -0.5, 0.21875, ((1, 4),)),
        "down_bias": scatter_about(streams_of[12], (D,), 0.5, 3.0, (), jnp.float32),
        "second_gain": jnp.clip(1.0 + 0.1 * jax.random.normal(streams_of[13], (D,), jnp.float32), 0.5, 1.5),
        "second_shift": scatter_about(streams_of[14], (D,), 0.5, 3.0, (), jnp.float32),
        "out_grad": gaussian_with(streams_of[15], (TOKENS, D), 1.0, 6.0, ((0, 32),), (0, 1, 32, 2.75)),
    }


EPSILON = 1e-06
PRECISE = lax.Precision.HIGHEST

@jax.custom_vjp
def low(v):
    return lax.optimization_barrier(v.astype(jnp.bfloat16)).astype(jnp.float32)

@jax.custom_vjp
def low_back(v):
    return v

def low_keep(v):
    return (low(v), None)

def low_pass(kept, grad):
    return (grad,)

def back_keep(v):
    return (v, None)

def back_low(kept, grad):
    return (low(grad),)
low.defvjp(low_keep, low_pass)
low_back.defvjp(back_keep, back_low)

def norm_rows(values, gain, shift):
    mean = lax.optimization_barrier(jnp.mean(values, axis=-1, keepdims=True))
    centred = values - mean
    spread = lax.optimization_barrier(jnp.mean(centred * centred, axis=-1, keepdims=True))
    return centred * lax.rsqrt(spread + EPSILON) * gain + shift

def attend_block(query, keys, values, lengths):
    scale = query.shape[-1] ** (-0.5)
    raw = jnp.einsum('plhe,pmhe->phlm', query, keys, precision=PRECISE) * scale
    raw = low_back(raw)
    valid = (jnp.arange(keys.shape[1])[None, :] < lengths[:, None])[:, None, None, :]
    scores = jnp.where(valid, raw, -1000000000.0)
    total = jax.nn.logsumexp(scores, axis=-1, keepdims=True)
    probs = low(jnp.exp(scores - total))
    return jnp.einsum('phlm,pmhe->plhe', probs, values, precision=PRECISE)

def attend_kind(query, keys, values, lengths, per_block):
    count = query.shape[0]
    blocks = count // per_block
    shaped = tuple((a.reshape((blocks, per_block) + a.shape[1:]) for a in (query, keys, values)))
    grouped = lengths.reshape(blocks, per_block)
    step = jax.checkpoint(attend_block)
    result = lax.map(lambda item: step(item[0], item[1], item[2], item[3]), (shaped[0], shaped[1], shaped[2], grouped))
    return result.reshape(query.shape)

def layer(hidden32, params, short_lengths, long_lengths):
    qkv_weight, qv_bias, out_weight, mixer_bias, first_gain, first_shift, up_weight, up_bias, down_weight, down_bias, second_gain, second_shift = params
    tokens = hidden32.shape[0]
    groups, width = (qkv_weight.shape[0], qkv_weight.shape[1])
    model = groups * width
    head_count = model // HD
    hidden_total = up_weight.shape[1]
    units = hidden_total // (groups * groups)
    up_std = up_weight.reshape(width, groups, groups, units).transpose(2, 0, 1, 3).reshape(groups, width, groups * units)
    upb_std = up_bias.reshape(groups, groups, units).transpose(1, 0, 2).reshape(groups, groups * units)
    down_std = down_weight.reshape(width, groups, groups, units).transpose(2, 1, 3, 0).reshape(groups, groups * units, width)
    zeros = jnp.zeros((groups, width), hidden32.dtype)
    bias_all = jnp.concatenate([qv_bias[:, :width], zeros, qv_bias[:, width:]], axis=1)
    projected = jnp.einsum('tgi,gio->tgo', hidden32.reshape(tokens, groups, width), qkv_weight, precision=PRECISE) + bias_all

    def third(slot):
        piece = projected[:, :, slot * width:(slot + 1) * width].reshape(tokens, head_count, HD)
        return low_back(low(piece))
    query, keys, values = (third(0), third(1), third(2))
    short_rows = short_lengths.shape[0] * LS
    short_count = short_lengths.shape[0]
    long_count = long_lengths.shape[0]

    def short_part(arr):
        return arr[:short_rows].reshape(short_count, LS, head_count, HD)

    def long_part(arr):
        return arr[short_rows:].reshape(long_count, LL, head_count, HD)
    ctx_short = attend_kind(short_part(query), short_part(keys), short_part(values), short_lengths, 4)
    ctx_long = attend_kind(long_part(query), long_part(keys), long_part(values), long_lengths, 1)
    context = jnp.concatenate([ctx_short.reshape(short_rows, model), ctx_long.reshape(tokens - short_rows, model)], axis=0)
    context = low_back(low(context))
    pre_first = low_back(hidden32 + jnp.dot(context, out_weight, precision=PRECISE) + mixer_bias)
    normed = norm_rows(pre_first, first_gain, first_shift)
    normed_low = low(normed).reshape(tokens, groups, width)
    pre_act = low_back(jnp.einsum('tgi,gih->tgh', normed_low, up_std, precision=PRECISE) + upb_std)
    activated = low(jax.nn.gelu(pre_act, approximate=False))
    branch = low_back(jnp.einsum('tgh,ghk->tgk', activated, down_std, precision=PRECISE)).reshape(tokens, model)
    pre_second = normed + branch + down_bias
    return norm_rows(pre_second, second_gain, second_shift)

def reference(hidden_in, lengths_short, lengths_long, qkv_weight, qv_bias, out_weight, mixer_bias, first_gain, first_shift, up_weight, up_bias, down_weight, down_bias, second_gain, second_shift, out_grad):
    params = tuple((p.astype(jnp.float32) for p in (qkv_weight, qv_bias, out_weight, mixer_bias, first_gain, first_shift, up_weight, up_bias, down_weight, down_bias, second_gain, second_shift)))
    rows_each = NS * LS + NL * LL
    model = hidden_in.shape[0]
    all_tokens = hidden_in.shape[1]
    blocks = all_tokens // rows_each
    inputs = hidden_in.astype(jnp.float32).T.reshape(blocks, rows_each, model)
    cotangents = out_grad.astype(jnp.float32).reshape(blocks, rows_each, model)
    short_all = lengths_short.reshape(blocks, NS)
    long_all = lengths_long.reshape(blocks, NL)
    totals0 = tuple((jnp.zeros_like(p) for p in params))

    def step(totals, item):
        block_in, short_block, long_block, block_grad = item

        def forward(hidden32, weights):
            return layer(hidden32, weights, short_block, long_block)
        result, pullback = jax.vjp(forward, block_in, params)
        grad_in, grad_params = pullback(block_grad)
        totals = tuple((a + b for a, b in zip(totals, grad_params)))
        return (totals, (result, grad_in))
    totals, (results, grads_in) = lax.scan(step, totals0, (inputs, short_all, long_all, cotangents))
    layer_out = results.reshape(all_tokens, model).astype(jnp.bfloat16)
    grad_qkv, grad_qv, grad_out, grad_mixer, grad_gain1, grad_shift1, grad_up, grad_upb, grad_down, grad_downb, grad_gain2, grad_shift2 = totals
    return (layer_out, grads_in.reshape(all_tokens, model).T, grad_qkv, grad_qv, grad_out, grad_mixer, grad_gain1, grad_shift1, grad_up, grad_upb, grad_down, grad_downb, grad_gain2, grad_shift2)
```

```python
import functools

import jax
import jax.numpy as jnp
from jax import lax
from jax.experimental import pallas as pl
from jax.experimental.pallas import tpu as pltpu
from jax.sharding import PartitionSpec as P

HD = 64
LS = 128
LL = 512
TILE = 256
EPSILON = 1e-06
LOG2E = 1.4426950408889634
F32 = jnp.float32
BF16 = jnp.bfloat16
VMEM_LIMIT = 60 * 1024 * 1024


def dot(a, b, ca, cb):
    return lax.dot_general(a, b, (((ca,), (cb,)), ((), ())), preferred_element_type=F32)


def gelu_parts(v):
    av = jnp.abs(v)
    t = 1.0 / (1.0 + (0.3275911 * 0.7071067811865476) * av)
    e = jnp.exp2((-0.5 * LOG2E) * (v * v))
    poly = t * (
        0.5 * 0.254829592
        + t
        * (
            0.5 * -0.284496736
            + t * (0.5 * 1.421413741 + t * (0.5 * -1.453152027 + t * (0.5 * 1.061405429)))
        )
    )
    tail = poly * e
    phi = jnp.where(v >= 0, 1.0 - tail, tail)
    return phi, phi + v * (0.3989422804014327 * e)


def attn_fwd_kernel(
    half, heads, short_blocks, me, lens_s, lens_l, x, w, b, proj, ctx0, ctx1, ctx2, ctx3, lse, scr
):
    k = pl.program_id(0)
    block = lax.bitwise_xor(me[0], k) * 2 + half
    width = heads * HD
    span = x.shape[1]
    proj[0] = (dot(w[...], x[...], 0, 0) + b[...]).astype(BF16)

    def one(rows, cols, length):
        q = proj[0, rows[0], cols]
        key = proj[0, rows[1], cols]
        val = proj[0, rows[2], cols]
        s = dot(key, q, 0, 0) * (HD**-0.5 * LOG2E)
        pos = lax.broadcasted_iota(jnp.int32, s.shape, 0)
        s = jnp.where(pos < length, s, -1e9)
        m = jnp.max(s, axis=0, keepdims=True)
        e = jnp.exp2(s - m)
        total = jnp.sum(e, axis=0, keepdims=True)
        c = dot(val, e.astype(BF16), 1, 0) * (1.0 / total)
        return c.astype(BF16), m + jnp.log2(total)

    def run(seq_len, lens, first):
        for i in range(span // seq_len):
            cols = slice(i * seq_len, (i + 1) * seq_len)
            length = lens[first + i]
            for h in range(heads):
                rows = [slice(j * width + h * HD, j * width + (h + 1) * HD) for j in range(3)]
                c, total = one(rows, cols, length)
                scr[h * HD : (h + 1) * HD, cols] = c
                lse[0, h : h + 1, cols] = total

    @pl.when(block < short_blocks)
    def _():
        run(LS, lens_s, block * (span // LS))

    @pl.when(block >= short_blocks)
    def _():
        run(LL, lens_l, (block - short_blocks) * (span // LL))

    for i, out in enumerate((ctx0, ctx1, ctx2, ctx3)):

        @pl.when(k == i)
        def _():
            out[...] = scr[...]


def attn_fwd(half, me, lens_s, lens_l, x, w, b):
    width, tokens = x.shape
    span = tokens // 8
    heads = width // HD
    short_blocks = lens_s.shape[0] * LS // span
    fixed = lambda k, *_: (0, 0)
    piece = jax.ShapeDtypeStruct((width, span), BF16)
    return pl.pallas_call(
        functools.partial(attn_fwd_kernel, half, heads, short_blocks),
        grid_spec=pltpu.PrefetchScalarGridSpec(
            num_scalar_prefetch=3,
            grid=(4,),
            in_specs=[
                pl.BlockSpec(
                    (width, span), lambda k, me, *_: (0, lax.bitwise_xor(me[0], k) * 2 + half)
                ),
                pl.BlockSpec(w.shape, fixed),
                pl.BlockSpec(b.shape, fixed),
            ],
            out_specs=[
                pl.BlockSpec((1, 3 * width, span), lambda k, *_: (k, 0, 0)),
                pl.BlockSpec((width, span), fixed),
                pl.BlockSpec((width, span), fixed),
                pl.BlockSpec((width, span), fixed),
                pl.BlockSpec((width, span), fixed),
                pl.BlockSpec((1, heads, span), lambda k, *_: (k, 0, 0)),
            ],
            scratch_shapes=[pltpu.VMEM((width, span), BF16)],
        ),
        out_shape=[
            jax.ShapeDtypeStruct((4, 3 * width, span), BF16),
            piece,
            piece,
            piece,
            piece,
            jax.ShapeDtypeStruct((4, heads, span), F32),
        ],
        compiler_params=pltpu.CompilerParams(vmem_limit_bytes=VMEM_LIMIT),
        name=f"attn_fwd{half}",
    )(me, lens_s, lens_l, x, w, b)


def attn_bwd_kernel(half, heads, short_blocks, me, lens_s, lens_l, *refs):
    if half:
        (x, w, proj, lse, g0, g1, g2, g3, f0, f1, f2, f3, acc_in, bias_in, old) = refs[:15]
        gin, acc, bias, dproj, gsc, fsc = refs[15:]
    else:
        (x, w, proj, lse, g0, g1, g2, g3, f0, f1, f2, f3) = refs[:12]
        gin, acc, bias, dproj, gsc, fsc = refs[12:]
    k = pl.program_id(0)
    block = lax.bitwise_xor(me[0], k) * 2 + half
    width = heads * HD
    span = x.shape[1]
    scale = HD**-0.5
    for i, (g, f) in enumerate(((g0, f0), (g1, f1), (g2, f2), (g3, f3))):

        @pl.when(k == i)
        def _():
            gsc[...] = g[...]
            fsc[...] = f[...]

    def run(seq_len, lens, first):
        for i in range(span // seq_len):
            cols = slice(i * seq_len, (i + 1) * seq_len)
            length = lens[first + i]
            for h in range(heads):
                rq, rk, rv = [
                    slice(j * width + h * HD, j * width + (h + 1) * HD) for j in range(3)
                ]
                q = proj[0, rq, cols]
                key = proj[0, rk, cols]
                val = proj[0, rv, cols]
                go = gsc[h * HD : (h + 1) * HD, cols]
                s = dot(key, q, 0, 0) * (scale * LOG2E)
                pos = lax.broadcasted_iota(jnp.int32, s.shape, 0)
                s = jnp.where(pos < length, s, -1e9)
                p = jnp.exp2(s - lse[0, h : h + 1, cols])
                gp = dot(val, go, 0, 0)
                inner = jnp.sum(p * gp, axis=0, keepdims=True)
                gs = (p * (gp - inner)).astype(BF16)
                dproj[rq, cols] = (dot(key, gs, 1, 0) * scale).astype(BF16)
                dproj[rk, cols] = (dot(q, gs, 1, 1) * scale).astype(BF16)
                dproj[rv, cols] = dot(go, p.astype(BF16), 1, 1).astype(BF16)

    @pl.when(block < short_blocks)
    def _():
        run(LS, lens_s, block * (span // LS))

    @pl.when(block >= short_blocks)
    def _():
        run(LL, lens_l, (block - short_blocks) * (span // LL))

    gin[...] = dot(w[...], dproj[...], 1, 0) + fsc[...].astype(F32)
    part = dot(dproj[...], x[...], 1, 1)
    sums = jnp.sum(dproj[...].astype(F32), axis=1, keepdims=True)

    @pl.when(k == 0)
    def _():
        if half:
            acc[...] = acc_in[...] + part
            bias[...] = bias_in[...] + sums
        else:
            acc[...] = part
            bias[...] = sums

    @pl.when(k > 0)
    def _():
        acc[...] += part
        bias[...] += sums


def attn_bwd(half, me, lens_s, lens_l, x, w, proj, lse, g, f, carry):
    width, tokens = x.shape
    span = tokens // 8
    heads = width // HD
    short_blocks = lens_s.shape[0] * LS // span
    fixed = lambda k, *_: (0, 0)
    here = lambda k, me, *_: (0, lax.bitwise_xor(me[0], k) * 2 + half)
    piece = pl.BlockSpec((width, span), fixed)
    acc_spec = pl.BlockSpec((3 * width, width), fixed)
    bias_spec = pl.BlockSpec((3 * width, 1), fixed)
    in_specs = [
        pl.BlockSpec((width, span), here),
        pl.BlockSpec(w.shape, fixed),
        pl.BlockSpec((1, 3 * width, span), lambda k, *_: (k, 0, 0)),
        pl.BlockSpec((1, heads, span), lambda k, *_: (k, 0, 0)),
    ] + [piece] * 8
    args = [x, w, proj, lse, *g, *f]
    aliases = {}
    if half:
        gin, acc, bias = carry
        in_specs += [acc_spec, bias_spec, pl.BlockSpec(memory_space=pl.ANY)]
        args += [acc, bias, gin]
        aliases = {3 + len(args) - 1: 0}
    return pl.pallas_call(
        functools.partial(attn_bwd_kernel, half, heads, short_blocks),
        grid_spec=pltpu.PrefetchScalarGridSpec(
            num_scalar_prefetch=3,
            grid=(4,),
            in_specs=in_specs,
            out_specs=[pl.BlockSpec((width, span), here), acc_spec, bias_spec],
            scratch_shapes=[
                pltpu.VMEM((3 * width, span), BF16),
                pltpu.VMEM((width, span), BF16),
                pltpu.VMEM((width, span), BF16),
            ],
        ),
        out_shape=[
            jax.ShapeDtypeStruct((width, tokens), F32),
            jax.ShapeDtypeStruct((3 * width, width), F32),
            jax.ShapeDtypeStruct((3 * width, 1), F32),
        ],
        input_output_aliases=aliases,
        compiler_params=pltpu.CompilerParams(vmem_limit_bytes=VMEM_LIMIT),
        name=f"attn_bwd{half}",
    )(me, lens_s, lens_l, *args)


def mid_kernel(half, width, me, *refs):
    ctx, hid = refs[0:4], refs[4:8]
    og = refs[8]
    ow, up, dn = refs[9:13], refs[13:17], refs[17:21]
    cols, ub = refs[21], refs[22]
    at = 23
    if half:
        gow_in, gup_in, gdn_in, vec_in = refs[at : at + 4]
        at += 4
    lo = refs[at]
    gctx, gpf_out = refs[at + 1 : at + 5], refs[at + 5 : at + 9]
    gow, gup, gdn, vec = refs[at + 9 : at + 13]
    upt, dnt, act, slope, first, n1s, gps_s = refs[at + 13 :]
    step = pl.program_id(0)
    model = 4 * width
    inv = 1.0 / model

    @pl.when(step == 0)
    def _():
        for k in range(4):
            ut = up[k][...].T
            dt = dn[k][...].T
            for g in range(4):
                upt[g, k * width : (k + 1) * width, :] = ut[g * width : (g + 1) * width, :]
                dnt[g, k * width : (k + 1) * width, :] = dt[g * width : (g + 1) * width, :]
        if half:
            gow[...] = gow_in[...]
            gup[...] = gup_in[...]
            gdn[...] = gdn_in[...]
            vec[...] = vec_in[...]
        else:
            gow[...] = jnp.zeros_like(gow)
            gup[...] = jnp.zeros_like(gup)
            gdn[...] = jnp.zeros_like(gdn)
            vec[...] = jnp.zeros_like(vec)

    def col(j):
        return cols[:, j : j + 1]

    lane = lax.broadcasted_iota(jnp.int32, (1, vec.shape[1]), 1)

    def add_vec(j, value):
        vec[...] += jnp.where(lane == j, jnp.sum(value, axis=1, keepdims=True), 0.0)

    first[...] = col(0) + sum(dot(ow[k][...], ctx[k][...], 0, 0) for k in range(4))
    for k in range(4):
        rows = pl.ds(pl.multiple_of(lax.bitwise_xor(me[0], k) * width, width), width)
        first[rows, :] += hid[k][...].astype(F32)
    pre = first[...]
    cen = pre - jnp.sum(pre, axis=0, keepdims=True) * inv
    r1 = lax.rsqrt(jnp.sum(cen * cen, axis=0, keepdims=True) * inv + EPSILON)
    n1 = cen * r1
    n1s[...] = n1
    normed = n1 * col(1) + col(2)
    low = normed.astype(BF16)
    for g in range(4):
        rows = slice(g * width, (g + 1) * width)
        branch = jnp.zeros((width, TILE), F32)
        for k in range(4):
            units = slice(k * width, (k + 1) * width)
            pa = dot(upt[g, units, :], low[rows, :], 1, 0) + ub[rows, k : k + 1]
            phi, sl = gelu_parts(pa)
            a = (pa * phi).astype(BF16)
            act[g, units, :] = a
            slope[g, units, :] = sl
            branch += dot(dnt[g, units, :], a, 0, 0)
        first[rows, :] = normed[rows, :] + branch + cols[rows, 3:4]
    pre = first[...]
    cen = pre - jnp.sum(pre, axis=0, keepdims=True) * inv
    r2 = lax.rsqrt(jnp.sum(cen * cen, axis=0, keepdims=True) * inv + EPSILON)
    n2 = cen * r2
    lo[...] = (n2 * col(4) + col(5)).T.astype(BF16)
    ogt = og[...].astype(F32).T
    add_vec(4, ogt * n2)
    add_vec(5, ogt)
    u = ogt * col(4)
    gps = r2 * (
        u
        - jnp.sum(u, axis=0, keepdims=True) * inv
        - n2 * (jnp.sum(u * n2, axis=0, keepdims=True) * inv)
    )
    add_vec(3, gps)
    gdl = gps.astype(BF16)
    gps_s[...] = gps
    for g in range(4):
        rows = slice(g * width, (g + 1) * width)
        gn = gps_s[rows, :]
        gup_sum = []
        for k in range(4):
            units = slice(k * width, (k + 1) * width)
            ga = dot(dnt[g, units, :], gdl[rows, :], 1, 0) * slope[g, units, :]
            gpa = ga.astype(BF16)
            gup_sum.append(jnp.sum(gpa.astype(F32), axis=1, keepdims=True))
            gdn[g, units, :] += dot(act[g, units, :], gdl[rows, :], 1, 1)
            gup[g, units, :] += dot(gpa, low[rows, :], 1, 1)
            gn += dot(upt[g, units, :], gpa, 0, 0)
        vec[...] += jnp.where(lane == 6 + g, jnp.concatenate(gup_sum, axis=0), 0.0)
        gps_s[rows, :] = gn
    gn = gps_s[...]
    n1 = n1s[...]
    add_vec(1, gn * n1)
    add_vec(2, gn)
    u = gn * col(1)
    gpf = r1 * (
        u
        - jnp.sum(u, axis=0, keepdims=True) * inv
        - n1 * (jnp.sum(u * n1, axis=0, keepdims=True) * inv)
    )
    gpl = gpf.astype(BF16)
    first[...] = gpl.astype(F32)
    add_vec(0, first[...])
    for k in range(4):
        rows = pl.ds(pl.multiple_of(lax.bitwise_xor(me[0], k) * width, width), width)
        gpf_out[k][...] = first[rows, :].astype(BF16)
        gctx[k][...] = dot(ow[k][...], gpl, 1, 0).astype(BF16)
        gow[k] += dot(gpl, ctx[k][...], 1, 1)


def mid(half, me, ctx, hid, og, ow, up, dn, cols, ub, carry):
    width, span = ctx[0].shape
    model = 4 * width
    steps = span // TILE
    whole2 = lambda i, *_: (0, 0)
    whole3 = lambda i, *_: (0, 0, 0)
    tile = pl.BlockSpec((width, TILE), lambda i, *_: (0, i))
    row_in = pl.BlockSpec((TILE, model), lambda i, *_: (half * steps + i, 0))
    weight = pl.BlockSpec((width, model), whole2)
    gow_spec = pl.BlockSpec((4, model, width), whole3)
    vec_spec = pl.BlockSpec((model, 16), whole2)
    in_specs = (
        [tile] * 8
        + [row_in]
        + [weight] * 12
        + [pl.BlockSpec(cols.shape, whole2), pl.BlockSpec(ub.shape, whole2)]
    )
    args = [*ctx, *hid, og, *ow, *up, *dn, cols, ub]
    if half:
        in_specs += [gow_spec] * 3 + [vec_spec]
        args += list(carry)
    big = jax.ShapeDtypeStruct((4, model, width), F32)
    piece = jax.ShapeDtypeStruct((width, span), BF16)
    return pl.pallas_call(
        functools.partial(mid_kernel, half, width),
        grid_spec=pltpu.PrefetchScalarGridSpec(
            num_scalar_prefetch=1,
            grid=(steps,),
            in_specs=in_specs,
            out_specs=[pl.BlockSpec((TILE, model), lambda i, *_: (i, 0))]
            + [tile] * 8
            + [gow_spec] * 3
            + [vec_spec],
            scratch_shapes=[
                pltpu.VMEM((4, model, width), BF16),
                pltpu.VMEM((4, model, width), BF16),
                pltpu.VMEM((4, model, TILE), BF16),
                pltpu.VMEM((4, model, TILE), F32),
                pltpu.VMEM((model, TILE), F32),
                pltpu.VMEM((model, TILE), F32),
                pltpu.VMEM((model, TILE), F32),
            ],
        ),
        out_shape=[jax.ShapeDtypeStruct((span, model), BF16)]
        + [piece] * 8
        + [big] * 3
        + [jax.ShapeDtypeStruct((model, 16), F32)],
        compiler_params=pltpu.CompilerParams(vmem_limit_bytes=VMEM_LIMIT),
        name=f"mid{half}",
    )(me, *args)


def swap(value, axis, bit):
    count = lax.axis_size(axis)
    return lax.ppermute(value, axis, [(i, i ^ bit) for i in range(count)])


def to_chan(pieces):
    return [pieces[0]] + [swap(pieces[k], "chan", k) for k in range(1, 4)]


def gather_chan(value):
    near = swap(value, "chan", 1)
    far = swap(value, "chan", 2)
    return [value, near, far, swap(far, "chan", 1)]


def scatter_dp(pieces):
    index = lax.axis_index("dp")
    count = pieces.shape[0]
    step = 1
    while count > 1:
        part = min(8, count)
        digit = (index // step) % part
        view = pieces.reshape((count // part, part) + pieces.shape[1:])
        total = lax.dynamic_index_in_dim(view, digit, 1, keepdims=False).astype(F32)
        for e in range(1, part):
            term = lax.dynamic_index_in_dim(view, digit ^ e, 1, keepdims=False)
            total = total + swap(term, "dp", e * step).astype(F32)
        count //= part
        step *= part
        pieces = total if count == 1 else total.astype(pieces.dtype)
    return pieces[0]


def sum_dp(value):
    bit = 1
    while bit < lax.axis_size("dp"):
        value = value + swap(value, "dp", bit)
        bit *= 2
    return value


def on_device(
    hidden_in,
    lengths_short,
    lengths_long,
    qkv_weight,
    qv_bias,
    out_weight,
    mixer_bias,
    first_gain,
    first_shift,
    up_weight,
    up_bias,
    down_weight,
    down_bias,
    second_gain,
    second_shift,
    out_grad,
):
    width, tokens = hidden_in.shape
    span = tokens // 8
    model = 4 * width
    dp_count = lax.axis_size("dp")
    chan = lax.axis_index("chan").astype(jnp.int32)
    dp = lax.axis_index("dp").astype(jnp.int32)
    me = chan[None]

    def hidden_piece(k, half):
        return lax.dynamic_slice_in_dim(
            hidden_in, (lax.bitwise_xor(chan, k) * 2 + half) * span, span, 1
        )

    ow = gather_chan(out_weight)
    up = gather_chan(up_weight)
    dn = gather_chan(down_weight)
    ub = jnp.stack(gather_chan(up_bias), axis=1)
    cols = jnp.stack(
        [mixer_bias, first_gain, first_shift, down_bias, second_gain, second_shift], axis=1
    )
    bias = jnp.concatenate(
        [qv_bias[0, :width], jnp.zeros((width,), F32), qv_bias[0, width:]]
    )[:, None]
    w = qkv_weight[0]
    hid, proj, ctx, lse = [], [], [], []
    for half in range(2):
        hid.append(to_chan([hidden_piece(k, half) for k in range(4)]))
        p, c0, c1, c2, c3, total = attn_fwd(
            half, me, lengths_short, lengths_long, hidden_in, w, bias
        )
        proj.append(p)
        lse.append(total)
        ctx.append(to_chan([c0, c1, c2, c3]))
    outs, carry, gctx, gpf = [], None, [], []
    for half in range(2):
        res = mid(half, me, ctx[half], hid[half], out_grad, ow, up, dn, cols, ub, carry)
        outs.append(res[0])
        gctx.append(to_chan(res[1:5]))
        gpf.append(to_chan(res[5:9]))
        carry = res[9:13]
    gow, gup, gdn, vec = carry
    carry = None
    for half in range(2):
        carry = attn_bwd(
            half,
            me,
            lengths_short,
            lengths_long,
            hidden_in,
            w,
            proj[half],
            lse[half],
            gctx[half],
            gpf[half],
            carry,
        )
    grad_input, gqkv, gbias = carry

    def by_columns(value):
        return value.reshape(4, 4, width, width).transpose(1, 3, 0, 2).reshape(4, width, model)

    rows = jnp.concatenate([by_columns(gup), by_columns(gdn)], axis=2).astype(BF16)
    flat = gow.astype(BF16)

    def over_chan(value):
        near = value[0::2] + swap(value[1::2], "chan", 1)
        return near[0] + swap(near[1], "chan", 2)

    rows = over_chan(rows)
    flat = over_chan(flat)
    rows = scatter_dp(rows.reshape(dp_count, width // dp_count, 2 * model))
    flat = scatter_dp(flat.reshape(dp_count, model // dp_count, width))
    gq = scatter_dp(gqkv.astype(BF16).reshape(dp_count, 3 * width // dp_count, width))
    grad_qv = sum_dp(gbias[:, 0])
    vec = sum_dp(vec)
    grad_upb = over_chan(vec[:, 6:10].reshape(4, width, 4)).T.reshape(model)
    vec = vec + swap(vec, "chan", 1)
    vec = vec + swap(vec, "chan", 2)
    own = model // (4 * dp_count)
    mine = lax.dynamic_slice_in_dim(vec[:, :6], (dp * 4 + chan) * own, own, 0)
    return (
        jnp.concatenate(outs, axis=0),
        grad_input,
        gq.T[None],
        jnp.concatenate([grad_qv[:width], grad_qv[2 * width :]])[None],
        flat.T,
        mine[:, 0],
        mine[:, 1],
        mine[:, 2],
        rows[:, :model],
        grad_upb,
        rows[:, model:],
        mine[:, 3],
        mine[:, 4],
        mine[:, 5],
    )


def solution(mesh):
    in_specs = (
        P("chan", "dp"),
        P("dp"),
        P("dp"),
        P("chan", None, None),
        P("chan", None),
        P("chan", None),
        P(),
        P(),
        P(),
        P(None, "chan"),
        P("chan"),
        P(None, "chan"),
        P(),
        P(),
        P(),
        P(("dp", "chan"), None),
    )
    out_specs = (
        P(("dp", "chan"), None),
        P("chan", "dp"),
        P("chan", None, "dp"),
        P("chan", None),
        P("chan", "dp"),
        P(("dp", "chan")),
        P(("dp", "chan")),
        P(("dp", "chan")),
        P("dp", "chan"),
        P("chan"),
        P("dp", "chan"),
        P(("dp", "chan")),
        P(("dp", "chan")),
        P(("dp", "chan")),
    )
    return jax.shard_map(
        on_device, mesh=mesh, in_specs=in_specs, out_specs=out_specs, check_vma=False
    )
```

```python
import functools

import jax
import jax.numpy as jnp
from jax import lax
from jax.experimental import pallas as pl
from jax.experimental.pallas import tpu as pltpu
from jax.sharding import PartitionSpec as P

HD = 64
LS = 128
LL = 512
TILE = 256
EPSILON = 1e-06
LOG2E = 1.4426950408889634
F32 = jnp.float32
BF16 = jnp.bfloat16
VMEM_LIMIT = 60 * 1024 * 1024


def COST(us):
    return pl.CostEstimate(
        flops=int(us * 1.0e9), bytes_accessed=int(us * 1.0e6), transcendentals=0
    )


def dot(a, b, ca, cb):
    return lax.dot_general(a, b, (((ca,), (cb,)), ((), ())), preferred_element_type=F32)


def gelu_parts(v):
    av = jnp.abs(v)
    t = 1.0 / (1.0 + (0.3275911 * 0.7071067811865476) * av)
    e = jnp.exp2((-0.5 * LOG2E) * (v * v))
    poly = t * (
        0.5 * 0.254829592
        + t
        * (
            0.5 * -0.284496736
            + t * (0.5 * 1.421413741 + t * (0.5 * -1.453152027 + t * (0.5 * 1.061405429)))
        )
    )
    tail = poly * e
    phi = jnp.where(v >= 0, 1.0 - tail, tail)
    return phi, phi + v * (0.3989422804014327 * e)


def attn_fwd_kernel(
    half, heads, short_blocks, me, lens_s, lens_l, x, w, b, proj, out0, out1, out2, out3, lse, scr
):
    k = pl.program_id(0)
    block = lax.bitwise_xor(me[0], k) * 2 + half
    width = heads * HD
    span = x.shape[1]
    proj[0] = (dot(w[...], x[...], 0, 0) + b[...]).astype(BF16)

    def one(rows, cols, length):
        q = proj[0, rows[0], cols]
        key = proj[0, rows[1], cols]
        val = proj[0, rows[2], cols]
        s = dot(key, q, 0, 0) * (HD**-0.5 * LOG2E)
        pos = lax.broadcasted_iota(jnp.int32, s.shape, 0)
        s = jnp.where(pos < length, s, -1e9)
        m = jnp.max(s, axis=0, keepdims=True)
        e = jnp.exp2(s - m)
        total = jnp.sum(e, axis=0, keepdims=True)
        c = dot(val, e.astype(BF16), 1, 0) * (1.0 / total)
        return c.astype(BF16), m + jnp.log2(total)

    def run(seq_len, lens, first):
        for i in range(span // seq_len):
            cols = slice(i * seq_len, (i + 1) * seq_len)
            length = lens[first + i]
            for h in range(heads):
                rows = [slice(j * width + h * HD, j * width + (h + 1) * HD) for j in range(3)]
                c, total = one(rows, cols, length)
                scr[h * HD : (h + 1) * HD, cols] = c
                lse[0, h : h + 1, cols] = total

    @pl.when(block < short_blocks)
    def _():
        run(LS, lens_s, block * (span // LS))

    @pl.when(block >= short_blocks)
    def _():
        run(LL, lens_l, (block - short_blocks) * (span // LL))

    for i, out in enumerate((out0, out1, out2, out3)):

        @pl.when(k == i)
        def _():
            out[0] = scr[...]
            if half and i:
                out[1] = x[...]


def attn_fwd(half, me, lens_s, lens_l, x, w, b):
    width, tokens = x.shape
    span = tokens // 8
    heads = width // HD
    short_blocks = lens_s.shape[0] * LS // span
    fixed = lambda k, *_: (0, 0)
    parts = [(1 + (half if k else 0), width, span) for k in range(4)]
    return pl.pallas_call(
        functools.partial(attn_fwd_kernel, half, heads, short_blocks),
        grid_spec=pltpu.PrefetchScalarGridSpec(
            num_scalar_prefetch=3,
            grid=(4,),
            in_specs=[
                pl.BlockSpec(
                    (width, span), lambda k, me, *_: (0, lax.bitwise_xor(me[0], k) * 2 + half)
                ),
                pl.BlockSpec(w.shape, fixed),
                pl.BlockSpec(b.shape, fixed),
            ],
            out_specs=[
                pl.BlockSpec((1, 3 * width, span), lambda k, *_: (k, 0, 0)),
                *[pl.BlockSpec(part, lambda k, *_: (0, 0, 0)) for part in parts],
                pl.BlockSpec((1, heads, span), lambda k, *_: (k, 0, 0)),
            ],
            scratch_shapes=[pltpu.VMEM((width, span), BF16)],
        ),
        out_shape=[
            jax.ShapeDtypeStruct((4, 3 * width, span), BF16),
            *[jax.ShapeDtypeStruct(part, BF16) for part in parts],
            jax.ShapeDtypeStruct((4, heads, span), F32),
        ],
        cost_estimate=COST(9.0),
        compiler_params=pltpu.CompilerParams(vmem_limit_bytes=VMEM_LIMIT),
        name=f"attn_fwd{half}",
    )(me, lens_s, lens_l, x, w, b)


def attn_bwd_kernel(half, heads, short_blocks, me, lens_s, lens_l, *refs):
    if half:
        (x, w, proj, lse, g0, g1, g2, g3, acc_in, bias_in, old) = refs[:11]
        gin, out, bias, dproj, gsc, fsc, acc = refs[11:]
    else:
        (x, w, proj, lse, g0, g1, g2, g3) = refs[:8]
        gin, acc, bias, dproj, gsc, fsc = refs[8:]
    k = pl.program_id(0)
    block = lax.bitwise_xor(me[0], k) * 2 + half
    width = heads * HD
    span = x.shape[1]
    scale = HD**-0.5
    for i, g in enumerate((g0, g1, g2, g3)):

        @pl.when(k == i)
        def _():
            gsc[...] = g[0]
            fsc[...] = g[1]

    def run(seq_len, lens, first):
        for i in range(span // seq_len):
            cols = slice(i * seq_len, (i + 1) * seq_len)
            length = lens[first + i]
            for h in range(heads):
                rq, rk, rv = [
                    slice(j * width + h * HD, j * width + (h + 1) * HD) for j in range(3)
                ]
                q = proj[0, rq, cols]
                key = proj[0, rk, cols]
                val = proj[0, rv, cols]
                go = gsc[h * HD : (h + 1) * HD, cols]
                s = dot(key, q, 0, 0) * (scale * LOG2E)
                pos = lax.broadcasted_iota(jnp.int32, s.shape, 0)
                s = jnp.where(pos < length, s, -1e9)
                p = jnp.exp2(s - lse[0, h : h + 1, cols])
                gp = dot(val, go, 0, 0)
                inner = jnp.sum(p * gp, axis=0, keepdims=True)
                gs = (p * (gp - inner)).astype(BF16)
                dproj[rq, cols] = (dot(key, gs, 1, 0) * scale).astype(BF16)
                dproj[rk, cols] = (dot(q, gs, 1, 1) * scale).astype(BF16)
                dproj[rv, cols] = dot(go, p.astype(BF16), 1, 1).astype(BF16)

    @pl.when(block < short_blocks)
    def _():
        run(LS, lens_s, block * (span // LS))

    @pl.when(block >= short_blocks)
    def _():
        run(LL, lens_l, (block - short_blocks) * (span // LL))

    gin[...] = dot(w[...], dproj[...], 1, 0) + fsc[...].astype(F32)
    part = dot(dproj[...], x[...], 1, 1)
    sums = dot(jnp.ones((8, span), BF16), dproj[...], 1, 1)

    @pl.when(k == 0)
    def _():
        if half:
            acc[...] = acc_in[...] + part
            bias[...] = bias_in[...] + sums
        else:
            acc[...] = part
            bias[...] = sums

    @pl.when(k > 0)
    def _():
        acc[...] += part
        bias[...] += sums

    if half:

        @pl.when(k == 3)
        def _():
            rows = out.shape[1]
            for d in range(out.shape[0]):
                out[d] = acc[d * rows : (d + 1) * rows, :].astype(BF16)


def attn_bwd(half, me, lens_s, lens_l, x, w, proj, lse, g, carry, dp_count):
    width, tokens = x.shape
    span = tokens // 8
    heads = width // HD
    short_blocks = lens_s.shape[0] * LS // span
    fixed = lambda k, *_: (0, 0)
    here = lambda k, me, *_: (0, lax.bitwise_xor(me[0], k) * 2 + half)
    piece = pl.BlockSpec((2, width, span), lambda k, *_: (0, 0, 0))
    acc_spec = pl.BlockSpec((3 * width, width), fixed)
    acc_shape = jax.ShapeDtypeStruct((3 * width, width), F32)
    out_spec, out_shape = acc_spec, acc_shape
    bias_spec = pl.BlockSpec((8, 3 * width), fixed)
    scratch = []
    in_specs = [
        pl.BlockSpec((width, span), here),
        pl.BlockSpec(w.shape, fixed),
        pl.BlockSpec((1, 3 * width, span), lambda k, *_: (k, 0, 0)),
        pl.BlockSpec((1, heads, span), lambda k, *_: (k, 0, 0)),
    ] + [piece] * 4
    args = [x, w, proj, lse, *g]
    aliases = {}
    if half:
        gin, acc, bias = carry
        in_specs += [acc_spec, bias_spec, pl.BlockSpec(memory_space=pl.ANY)]
        args += [acc, bias, gin]
        aliases = {3 + len(args) - 1: 0}
        shape = (dp_count, 3 * width // dp_count, width)
        out_spec = pl.BlockSpec(shape, lambda k, *_: (0, 0, 0))
        out_shape = jax.ShapeDtypeStruct(shape, BF16)
        scratch = [pltpu.VMEM((3 * width, width), F32)]
    return pl.pallas_call(
        functools.partial(attn_bwd_kernel, half, heads, short_blocks),
        grid_spec=pltpu.PrefetchScalarGridSpec(
            num_scalar_prefetch=3,
            grid=(4,),
            in_specs=in_specs,
            out_specs=[pl.BlockSpec((width, span), here), out_spec, bias_spec],
            scratch_shapes=[
                pltpu.VMEM((3 * width, span), BF16),
                pltpu.VMEM((width, span), BF16),
                pltpu.VMEM((width, span), BF16),
            ]
            + scratch,
        ),
        out_shape=[
            jax.ShapeDtypeStruct((width, tokens), F32),
            out_shape,
            jax.ShapeDtypeStruct((8, 3 * width), F32),
        ],
        cost_estimate=COST(18.0),
        input_output_aliases=aliases,
        compiler_params=pltpu.CompilerParams(vmem_limit_bytes=VMEM_LIMIT),
        name=f"attn_bwd{half}",
    )(me, lens_s, lens_l, *args)


def mid_kernel(half, width, blocks, me, *refs):
    ctx, hid = refs[0:4], refs[4:8]
    og = refs[8]
    ow, up, dn = refs[9:13], refs[13:17], refs[17:21]
    cols, ub = refs[21], refs[22]
    at = 23
    if half:
        gow_in, gup_in, gdn_in, vec_in = refs[at : at + 4]
        at += 4
    lo = refs[at]
    back = refs[at + 1 : at + 5]
    at += 5
    if half:
        keep, send, vec_out = refs[at : at + 3]
        at += 3
    gow, gup, gdn, vec = refs[at : at + 4]
    upt, dnt, act, slope, first, n1s, gps_s = refs[at + 4 :]
    step = pl.program_id(0)
    model = 4 * width
    inv = 1.0 / model

    @pl.when(step == 0)
    def _():
        for k in range(4):
            ut = up[k][...].T
            dt = dn[k][...].T
            for g in range(4):
                upt[g, k * width : (k + 1) * width, :] = ut[g * width : (g + 1) * width, :]
                dnt[g, k * width : (k + 1) * width, :] = dt[g * width : (g + 1) * width, :]
        if half:
            gow[...] = gow_in[...]
            gup[...] = gup_in[...]
            gdn[...] = gdn_in[...]
            vec[...] = vec_in[...]
        else:
            gow[...] = jnp.zeros_like(gow)
            gup[...] = jnp.zeros_like(gup)
            gdn[...] = jnp.zeros_like(gdn)
            vec[...] = jnp.zeros_like(vec)

    def col(j):
        return cols[:, j : j + 1]

    lane = lax.broadcasted_iota(jnp.int32, (1, 128), 1)

    def add_vec(j, value):
        vec[...] += jnp.where(lane == j, jnp.sum(value, axis=1, keepdims=True), 0.0)

    first[...] = col(0) + sum(dot(ow[k][...], ctx[k][0], 0, 0) for k in range(4))
    for k in range(4):
        rows = pl.ds(pl.multiple_of(lax.bitwise_xor(me[0], k) * width, width), width)
        first[rows, :] += hid[k][...].reshape(width, TILE).astype(F32)
    pre = first[...]
    cen = pre - jnp.sum(pre, axis=0, keepdims=True) * inv
    r1 = lax.rsqrt(jnp.sum(cen * cen, axis=0, keepdims=True) * inv + EPSILON)
    n1 = cen * r1
    n1s[...] = n1
    normed = n1 * col(1) + col(2)
    low = normed.astype(BF16)
    for g in range(4):
        rows = slice(g * width, (g + 1) * width)
        branch = jnp.zeros((width, TILE), F32)
        for k in range(4):
            units = slice(k * width, (k + 1) * width)
            pa = dot(upt[g, units, :], low[rows, :], 1, 0) + ub[rows, k : k + 1]
            phi, sl = gelu_parts(pa)
            a = (pa * phi).astype(BF16)
            act[g, units, :] = a
            slope[g, units, :] = sl
            branch += dot(dnt[g, units, :], a, 0, 0)
        first[rows, :] = normed[rows, :] + branch + cols[rows, 3:4]
    pre = first[...]
    cen = pre - jnp.sum(pre, axis=0, keepdims=True) * inv
    r2 = lax.rsqrt(jnp.sum(cen * cen, axis=0, keepdims=True) * inv + EPSILON)
    n2 = cen * r2
    lo[...] = (n2 * col(4) + col(5)).T.astype(BF16)
    ogt = og[...].astype(F32).T
    add_vec(4, ogt * n2)
    add_vec(5, ogt)
    u = ogt * col(4)
    gps = r2 * (
        u
        - jnp.sum(u, axis=0, keepdims=True) * inv
        - n2 * (jnp.sum(u * n2, axis=0, keepdims=True) * inv)
    )
    add_vec(3, gps)
    gdl = gps.astype(BF16)
    gps_s[...] = gps
    for g in range(4):
        rows = slice(g * width, (g + 1) * width)
        gn = gps_s[rows, :]
        gup_sum = []
        for k in range(4):
            units = slice(k * width, (k + 1) * width)
            ga = dot(dnt[g, units, :], gdl[rows, :], 1, 0) * slope[g, units, :]
            gpa = ga.astype(BF16)
            gup_sum.append(jnp.sum(gpa.astype(F32), axis=1, keepdims=True))
            gdn[g, units, :] += dot(act[g, units, :], gdl[rows, :], 1, 1)
            gup[g, units, :] += dot(gpa, low[rows, :], 1, 1)
            gn += dot(upt[g, units, :], gpa, 0, 0)
        for k in range(4):
            own = pl.ds(pl.multiple_of(lax.bitwise_xor(me[0], k) * width, width), width)
            vec[own, :] += jnp.where(lane == 6 + g, gup_sum[k], 0.0)
        gps_s[rows, :] = gn
    gn = gps_s[...]
    n1 = n1s[...]
    add_vec(1, gn * n1)
    add_vec(2, gn)
    u = gn * col(1)
    gpf = r1 * (
        u
        - jnp.sum(u, axis=0, keepdims=True) * inv
        - n1 * (jnp.sum(u * n1, axis=0, keepdims=True) * inv)
    )
    gpl = gpf.astype(BF16)
    first[...] = gpl.astype(F32)
    add_vec(0, first[...])
    for k in range(4):
        rows = pl.ds(pl.multiple_of(lax.bitwise_xor(me[0], k) * width, width), width)
        back[k][1] = first[rows, :].astype(BF16)
        back[k][0] = dot(ow[k][...], gpl, 1, 0).astype(BF16)
        gow[k] += dot(gpl, ctx[k][0], 1, 1)

    if half:

        @pl.when(step == pl.num_programs(0) - 1)
        def _():
            vec_out[...] = vec[...].T[:16]
            for k in range(4):
                dest = send if k % 2 else keep
                for g in range(4):
                    units = slice(k * width, (k + 1) * width)
                    cols_g = slice(g * width, (g + 1) * width)
                    dest[k // 2, 0, :, cols_g] = gup[g, units, :].T.astype(BF16)
                    dest[k // 2, 1, :, cols_g] = gdn[g, units, :].T.astype(BF16)
                    for d in range(blocks):
                        rows_d = slice(d * width // blocks, (d + 1) * width // blocks)
                        first_row = (d * 4 + g) * width // blocks
                        dest[k // 2, 2, rows_d, cols_g] = gow[
                            k, first_row : first_row + width // blocks, :
                        ].astype(BF16)


def mid(half, me, ctx, hid, og, ow, up, dn, cols, ub, carry, blocks):
    width, span = ctx[0].shape[1:]
    model = 4 * width
    steps = span // TILE
    whole2 = lambda i, *_: (0, 0)
    whole3 = lambda i, *_: (0, 0, 0)
    whole4 = lambda i, *_: (0, 0, 0, 0)
    ctx_tile = pl.BlockSpec((1, width, TILE), lambda i, *_: (0, 0, i))
    hid_own = pl.BlockSpec((width, TILE), lambda i, me: (0, (me[0] * 2 + half) * steps + i))
    hid_tile = pl.BlockSpec((1, width, TILE), lambda i, *_: (half, 0, i))
    back_tile = pl.BlockSpec((2, width, TILE), lambda i, *_: (0, 0, i))
    row_in = pl.BlockSpec((TILE, model), lambda i, *_: (half * steps + i, 0))
    weight = pl.BlockSpec((width, model), whole2)
    wslot = lambda j: pl.BlockSpec((width, model), lambda i, *_: (j, 0))
    gow_spec = pl.BlockSpec((4, model, width), whole3)
    vec_spec = pl.BlockSpec((model, 128), whole2)
    in_specs = (
        [ctx_tile] * 4
        + [hid_own]
        + [hid_tile] * 3
        + [row_in]
        + [wslot(0)] * 4
        + [wslot(1)] * 4
        + [wslot(2)] * 4
        + [pl.BlockSpec(cols.shape, whole2), pl.BlockSpec(ub.shape, whole2)]
    )
    args = [*ctx, *hid, og, *ow, *up, *dn, cols, ub]
    big = jax.ShapeDtypeStruct((4, model, width), F32)
    vec_shape = jax.ShapeDtypeStruct((model, 128), F32)
    piece = jax.ShapeDtypeStruct((2, width, span), BF16)
    scratch = [
        pltpu.VMEM((4, model, width), BF16),
        pltpu.VMEM((4, model, width), BF16),
        pltpu.VMEM((4, model, TILE), BF16),
        pltpu.VMEM((4, model, TILE), F32),
        pltpu.VMEM((model, TILE), F32),
        pltpu.VMEM((model, TILE), F32),
        pltpu.VMEM((model, TILE), F32),
    ]
    if half:
        in_specs += [gow_spec] * 3 + [vec_spec]
        args += list(carry)
        totals = jax.ShapeDtypeStruct((2, 3, width, model), BF16)
        totals_spec = pl.BlockSpec((2, 3, width, model), whole4)
        tail_specs = [totals_spec, totals_spec, pl.BlockSpec((16, model), whole2)]
        tail_shapes = [totals, totals, jax.ShapeDtypeStruct((16, model), F32)]
        scratch = [pltpu.VMEM(big.shape, F32)] * 3 + [pltpu.VMEM(vec_shape.shape, F32)] + scratch
    else:
        tail_specs = [gow_spec] * 3 + [vec_spec]
        tail_shapes = [big] * 3 + [vec_shape]
    return pl.pallas_call(
        functools.partial(mid_kernel, half, width, blocks),
        grid_spec=pltpu.PrefetchScalarGridSpec(
            num_scalar_prefetch=1,
            grid=(steps,),
            in_specs=in_specs,
            out_specs=[pl.BlockSpec((TILE, model), lambda i, *_: (i, 0))]
            + [back_tile] * 4
            + tail_specs,
            scratch_shapes=scratch,
        ),
        out_shape=[jax.ShapeDtypeStruct((span, model), BF16)] + [piece] * 4 + tail_shapes,
        cost_estimate=COST(30.0),
        compiler_params=pltpu.CompilerParams(vmem_limit_bytes=VMEM_LIMIT),
        name=f"mid{half}",
    )(me, *args)


def combine_kernel(size, outer, inner, last, index, keep, recv, extra, *refs):
    raw = len(refs) == (3 if last else 4)
    if raw:
        erecv, refs = refs[0], refs[1:]
    rows = extra.shape[0]
    if raw:
        more = extra[...] + erecv[...]
    else:
        more = extra[...] + (recv[size, :rows].astype(F32) + recv[size + 1, :rows].astype(F32))
    if last:
        out, extra_out = refs
        out[...] = keep[...].astype(F32) + recv[:size].astype(F32)
        extra_out[...] = more
        return
    kept, sent, extra_out = refs
    extra_out[...] = more
    hi = more.astype(BF16)
    sent[size // 2, :rows] = hi
    sent[size // 2 + 1, :rows] = (more - hi.astype(F32)).astype(BF16)
    mine = index[0]
    for o in range(outer):
        a = pl.ds((o * 2 + mine) * inner, inner)
        b = pl.ds((o * 2 + 1 - mine) * inner, inner)
        c = slice(o * inner, (o + 1) * inner)
        kept[c] = (keep[a].astype(F32) + recv[a].astype(F32)).astype(BF16)
        sent[c] = (keep[b].astype(F32) + recv[b].astype(F32)).astype(BF16)


def combine(index, keep, recv, extra, erecv, outer, inner, last, name):
    size, rows, lanes = keep.shape
    args = [keep, recv, extra] + ([] if erecv is None else [erecv])
    vmem = pl.BlockSpec(memory_space=pltpu.VMEM)
    if last:
        shapes = [jax.ShapeDtypeStruct(keep.shape, F32), jax.ShapeDtypeStruct(extra.shape, F32)]
    else:
        shapes = [
            jax.ShapeDtypeStruct((size // 2, rows, lanes), BF16),
            jax.ShapeDtypeStruct((size // 2 + 2, rows, lanes), BF16),
            jax.ShapeDtypeStruct(extra.shape, F32),
        ]
    return pl.pallas_call(
        functools.partial(combine_kernel, size, outer, inner, last),
        in_specs=[pl.BlockSpec(memory_space=pltpu.SMEM)] + [vmem] * len(args),
        out_specs=[vmem] * len(shapes),
        out_shape=shapes,
        cost_estimate=COST(1.0),
        compiler_params=pltpu.CompilerParams(vmem_limit_bytes=VMEM_LIMIT),
        name=name,
    )(index, *args)


def swap(value, axis, bit):
    count = lax.axis_size(axis)
    return lax.ppermute(value, axis, [(i, i ^ bit) for i in range(count)])


def to_chan(pieces):
    return [pieces[0]] + [swap(pieces[k], "chan", k) for k in range(1, 4)]


def gather_chan(value):
    near = swap(value, "chan", 1)
    far = swap(value, "chan", 2)
    return [value, near, far, swap(far, "chan", 1)]


def scatter_dp(pieces):
    index = lax.axis_index("dp")
    count, bit = pieces.shape[0], 1
    while count > 1:
        view = pieces.reshape((count // 2, 2) + pieces.shape[1:])
        digit = (index // bit) % 2
        mine = lax.dynamic_index_in_dim(view, digit, 1, keepdims=False).astype(F32)
        other = lax.dynamic_index_in_dim(view, 1 - digit, 1, keepdims=False)
        total = mine + swap(other, "dp", bit).astype(F32)
        count, bit = count // 2, bit * 2
        pieces = total if count == 1 else total.astype(pieces.dtype)
    return pieces[0]


def sum_dp(value):
    bit = 1
    while bit < lax.axis_size("dp"):
        value = value + swap(value, "dp", bit)
        bit *= 2
    return value


def hidden_kernel(me, x, out1, out2, out3):
    for i, out in enumerate((out1, out2, out3)):

        @pl.when(pl.program_id(0) == i)
        def _():
            out[0] = x[...]


def hidden_pieces(me, x, span):
    width = x.shape[0]
    shape = (1, width, span)
    return pl.pallas_call(
        hidden_kernel,
        grid_spec=pltpu.PrefetchScalarGridSpec(
            num_scalar_prefetch=1,
            grid=(3,),
            in_specs=[
                pl.BlockSpec((width, span), lambda k, me: (0, lax.bitwise_xor(me[0], k + 1) * 2))
            ],
            out_specs=[pl.BlockSpec(shape, lambda k, me: (0, 0, 0))] * 3,
        ),
        out_shape=[jax.ShapeDtypeStruct(shape, BF16)] * 3,
        cost_estimate=COST(1.0),
        name="hidden",
    )(me, x)


def reduce_weights(dp, keep, send, vec, dp_count):
    groups, sections, width, model = keep.shape
    rows = width // dp_count
    bits = dp_count.bit_length() - 1
    if rows < 16 or bits < 2:
        keep = keep + swap(send, "chan", 1)
        keep = keep[0] + swap(keep[1], "chan", 2)
        last = keep[2].reshape(width, 4, width).transpose(1, 0, 2).reshape(width, model)
        last = last.reshape(dp_count, 4, rows, width).transpose(0, 2, 1, 3)
        keep = jnp.stack([keep[0], keep[1], last.reshape(width, model)])
        keep = keep.reshape(sections, dp_count, rows, model).transpose(1, 0, 2, 3)
        vec = vec + swap(vec, "chan", 1)
        vec = sum_dp(vec + swap(vec, "chan", 2))
        return scatter_dp(keep), vec
    size = groups * sections * dp_count
    recv = swap(send, "chan", 1).reshape(size, rows, model)
    erecv = swap(vec, "chan", 1)
    keep = keep.reshape(size, rows, model)
    zero = jnp.zeros((1,), jnp.int32)
    digit = lambda b: ((dp >> b) & 1)[None]
    stages = [("dp", 0)] + [("chan", 1)] + [("dp", b) for b in range(1, bits)]
    for axis, b in stages:
        size = keep.shape[0]
        outer, inner = (size // 2, 1) if axis == "dp" else (1, size // 2)
        index = digit(b) if axis == "dp" else zero
        keep, send, vec = combine(
            index, keep, recv, vec, erecv, outer, inner, False, f"combine_{axis}{b}"
        )
        recv, erecv = swap(send, axis, 1 << b), None
    return combine(zero, keep, recv, vec, None, 1, 1, True, "combine_end")


def on_device(
    hidden_in,
    lengths_short,
    lengths_long,
    qkv_weight,
    qv_bias,
    out_weight,
    mixer_bias,
    first_gain,
    first_shift,
    up_weight,
    up_bias,
    down_weight,
    down_bias,
    second_gain,
    second_shift,
    out_grad,
):
    width, tokens = hidden_in.shape
    span = tokens // 8
    model = 4 * width
    dp_count = lax.axis_size("dp")
    chan = lax.axis_index("chan").astype(jnp.int32)
    dp = lax.axis_index("dp").astype(jnp.int32)
    me = chan[None]
    bar = lax.optimization_barrier

    far_hidden = to_chan([hidden_in] + list(hidden_pieces(me, hidden_in, span)))
    weights = gather_chan(jnp.concatenate([out_weight, up_weight, down_weight], axis=0))
    ub = jnp.stack(gather_chan(up_bias), axis=1)
    cols = jnp.stack(
        [mixer_bias, first_gain, first_shift, down_bias, second_gain, second_shift], axis=1
    )
    bias = jnp.concatenate(
        [qv_bias[0, :width], jnp.zeros((width,), F32), qv_bias[0, width:]]
    )[:, None]
    w = qkv_weight[0]
    proj, parts, lse = [], [], []
    for half in range(2):
        p, c0, c1, c2, c3, total = attn_fwd(
            half, me, lengths_short, lengths_long, hidden_in, w, bias
        )
        proj.append(p)
        lse.append(total)
        parts.append(to_chan([c0, c1, c2, c3]))
    outs, carry, back = [], None, []
    for half in range(2):
        hid = parts[half] if half else far_hidden
        res = mid(
            half,
            me,
            parts[half],
            [hidden_in] + hid[1:],
            out_grad,
            weights,
            weights,
            weights,
            cols,
            ub,
            carry,
            dp_count if width // dp_count >= 16 else 1,
        )
        outs.append(res[0])
        back.append(to_chan(res[1:5]))
        carry = res[5:]
    keep, send, vec = carry
    sums, vec = reduce_weights(dp, keep, send, vec, dp_count)
    carry = None
    for half in range(2):
        carry = attn_bwd(
            half,
            me,
            lengths_short,
            lengths_long,
            hidden_in,
            w,
            proj[half],
            lse[half],
            back[half],
            carry,
            dp_count,
        )
    grad_input, gq, gbias = carry
    gq, gbias = scatter_dp(gq), sum_dp(gbias[0])
    own = model // (4 * dp_count)
    mine = lax.dynamic_slice_in_dim(vec[:6], (dp * 4 + chan) * own, own, 1)
    grad_upb = lax.dynamic_slice_in_dim(vec[6:10], chan * width, width, 1).reshape(model)
    return (
        jnp.concatenate(outs, axis=0),
        grad_input,
        gq.T[None],
        jnp.concatenate([gbias[:width], gbias[2 * width :]])[None],
        sums[2].reshape(-1, 4, width).transpose(1, 0, 2).reshape(model // dp_count, width).T,
        mine[0],
        mine[1],
        mine[2],
        sums[0],
        grad_upb,
        sums[1],
        mine[3],
        mine[4],
        mine[5],
    )


def solution(mesh):
    in_specs = (
        P("chan", "dp"),
        P("dp"),
        P("dp"),
        P("chan", None, None),
        P("chan", None),
        P("chan", None),
        P(),
        P(),
        P(),
        P(None, "chan"),
        P("chan"),
        P(None, "chan"),
        P(),
        P(),
        P(),
        P(("dp", "chan"), None),
    )
    out_specs = (
        P(("dp", "chan"), None),
        P("chan", "dp"),
        P("chan", None, "dp"),
        P("chan", None),
        P("chan", "dp"),
        P(("dp", "chan")),
        P(("dp", "chan")),
        P(("dp", "chan")),
        P("dp", "chan"),
        P("chan"),
        P("dp", "chan"),
        P(("dp", "chan")),
        P(("dp", "chan")),
        P(("dp", "chan")),
    )
    return jax.shard_map(
        on_device, mesh=mesh, in_specs=in_specs, out_specs=out_specs, check_vma=False
    )
```

```python
import functools

import jax
import jax.numpy as jnp
from jax import lax
from jax.experimental import pallas as pl
from jax.experimental.pallas import tpu as pltpu
from jax.sharding import PartitionSpec as P

HD = 64
LS = 128
LL = 512
TILE = 256
EPSILON = 1e-06
LOG2E = 1.4426950408889634
F32 = jnp.float32
BF16 = jnp.bfloat16
VMEM_LIMIT = 67043328


def COST(us):
    return pl.CostEstimate(
        flops=int(us * 1.0e9), bytes_accessed=int(us * 1.0e6), transcendentals=0
    )


def dot(a, b, ca, cb):
    return lax.dot_general(a, b, (((ca,), (cb,)), ((), ())), preferred_element_type=F32)


def gelu_parts(v):
    av = jnp.abs(v)
    t = 1.0 / (1.0 + (0.3275911 * 0.7071067811865476) * av)
    e = jnp.exp2((-0.5 * LOG2E) * (v * v))
    poly = t * (
        0.5 * 0.254829592
        + t
        * (
            0.5 * -0.284496736
            + t * (0.5 * 1.421413741 + t * (0.5 * -1.453152027 + t * (0.5 * 1.061405429)))
        )
    )
    tail = poly * e
    phi = jnp.where(v >= 0, 1.0 - tail, tail)
    return phi, phi + v * (0.3989422804014327 * e)


def score_operands(heads, span, seq_len, lens, first, q, key, qa, ka):
    width = heads * HD
    scaled = q.astype(F32) * (HD**-0.5 * LOG2E)
    high = scaled.astype(BF16)
    low = (scaled - high.astype(F32)).astype(BF16)
    pos = lax.broadcasted_iota(jnp.int32, (16, seq_len), 1)
    row = lax.broadcasted_iota(jnp.int32, (16, seq_len), 0)
    for h in range(heads):
        rows = slice(h * HD, (h + 1) * HD)
        qa[h, 0:HD, :] = high[rows]
        qa[h, HD : 2 * HD, :] = low[rows]
        ka[h, 0:HD, :] = key[rows]
        ka[h, HD : 2 * HD, :] = key[rows]
    for i in range(span // seq_len):
        bad = (row == 0) & (pos >= lens[first + i])
        mask = jnp.where(bad, -1e9, 0.0).astype(BF16)
        for h in range(heads):
            ka[h, 2 * HD :, i * seq_len : (i + 1) * seq_len] = mask


def one_rows(qa):
    row = lax.broadcasted_iota(jnp.int32, (16, qa.shape[2]), 0)
    ones = jnp.where(row == 0, 1.0, 0.0).astype(BF16)
    for h in range(qa.shape[0]):
        qa[h, 2 * HD :, :] = ones


def attn_fwd_kernel(half, heads, short_blocks, me, lens_s, lens_l, x, w, b, *refs):
    proj, out0, out1, out2, out3, lse, scr, qa, ka, bcol = refs
    k = pl.program_id(0)
    block = lax.bitwise_xor(me[0], k) * 2 + half
    width = heads * HD
    span = x.shape[1]

    @pl.when(k == 0)
    def _():
        t = jnp.broadcast_to(b[...], (8, 2 * width)).T
        bcol[:width] = t[:width]
        bcol[width : 2 * width] = jnp.zeros((width, 8), F32)
        bcol[2 * width :] = t[width:]
        one_rows(qa)

    proj[0] = (dot(w[...], x[...], 0, 0) + bcol[:, 0:1]).astype(BF16)

    def run(seq_len, lens, first):
        score_operands(
            heads, span, seq_len, lens, first, proj[0, :width], proj[0, width : 2 * width], qa, ka
        )
        items = [(i, h) for i in range(span // seq_len) for h in range(heads)]

        def score(i, h):
            cols = slice(i * seq_len, (i + 1) * seq_len)
            return dot(ka[h, :, cols], qa[h, :, cols], 0, 0)

        s = score(*items[0])
        for n, (i, h) in enumerate(items):
            later = score(*items[n + 1]) if n + 1 < len(items) else None
            cols = slice(i * seq_len, (i + 1) * seq_len)
            m = jnp.max(s, axis=0, keepdims=True)
            e = jnp.exp2(s - m)
            total = jnp.sum(e, axis=0, keepdims=True)
            val = proj[0, 2 * width + h * HD : 2 * width + (h + 1) * HD, cols]
            c = dot(val, e.astype(BF16), 1, 0) * (1.0 / total)
            scr[h * HD : (h + 1) * HD, cols] = c.astype(BF16)
            lse[0, h : h + 1, cols] = m + jnp.log2(total)
            s = later

    @pl.when(block < short_blocks)
    def _():
        run(LS, lens_s, block * (span // LS))

    @pl.when(block >= short_blocks)
    def _():
        run(LL, lens_l, (block - short_blocks) * (span // LL))

    for i, out in enumerate((out0, out1, out2, out3)):

        @pl.when(k == i)
        def _():
            out[0] = scr[...]
            if i:
                out[1] = x[...]


def attn_fwd(half, me, lens_s, lens_l, x, w, b):
    width, tokens = x.shape
    span = tokens // 8
    heads = width // HD
    short_blocks = lens_s.shape[0] * LS // span
    fixed = lambda k, *_: (0, 0)
    parts = [(2 if k else 1, width, span) for k in range(4)]
    return pl.pallas_call(
        functools.partial(attn_fwd_kernel, half, heads, short_blocks),
        grid_spec=pltpu.PrefetchScalarGridSpec(
            num_scalar_prefetch=3,
            grid=(4,),
            in_specs=[
                pl.BlockSpec(
                    (width, span), lambda k, me, *_: (0, lax.bitwise_xor(me[0], k) * 2 + half)
                ),
                pl.BlockSpec(w.shape, fixed),
                pl.BlockSpec(b.shape, fixed),
            ],
            out_specs=[
                pl.BlockSpec((1, 3 * width, span), lambda k, *_: (k, 0, 0)),
                *[pl.BlockSpec(part, lambda k, *_: (0, 0, 0)) for part in parts],
                pl.BlockSpec((1, heads, span), lambda k, *_: (k, 0, 0)),
            ],
            scratch_shapes=[
                pltpu.VMEM((width, span), BF16),
                pltpu.VMEM((heads, 2 * HD + 16, span), BF16),
                pltpu.VMEM((heads, 2 * HD + 16, span), BF16),
                pltpu.VMEM((3 * width, 8), F32),
            ],
        ),
        out_shape=[
            jax.ShapeDtypeStruct((4, 3 * width, span), BF16),
            *[jax.ShapeDtypeStruct(part, BF16) for part in parts],
            jax.ShapeDtypeStruct((4, heads, span), F32),
        ],
        cost_estimate=COST(8.0),
        compiler_params=pltpu.CompilerParams(vmem_limit_bytes=VMEM_LIMIT),
        name=f"attn_fwd{half}",
    )(me, lens_s, lens_l, x, w, b)


def attn_bwd_kernel(half, base, stride, heads, short_blocks, first_call, split, *refs):
    me, lens_s, lens_l, x, w, proj, lse = refs[:7]
    count = 4 // stride
    gs = refs[7 : 7 + count]
    refs = refs[7 + count :]
    if not first_call:
        acc_in, bias_in = refs[:2]
        refs = refs[3:]
    gin = refs[0]
    if split == 0:
        acc, bias = refs[1:3]
        refs = refs[3:]
    elif split == 1:
        out, bias = refs[1:3]
        acc = refs[-1]
        refs = refs[3:-1]
    else:
        keep, send, extra = refs[1:4]
        bias, acc = refs[-2:]
        refs = refs[4:-2]
    dproj, gsc, qa, ka = refs
    step = pl.program_id(0)
    block = lax.bitwise_xor(me[0], base + stride * step) * 2 + half
    width = heads * HD
    span = x.shape[1]
    scale = HD**-0.5

    @pl.when(step == 0)
    def _():
        one_rows(qa)

    for i, g in enumerate(gs):

        @pl.when(step == i)
        def _():
            gsc[...] = g[...]

    def run(seq_len, lens, first):
        score_operands(
            heads, span, seq_len, lens, first, proj[0, :width], proj[0, width : 2 * width], qa, ka
        )
        items = [(i, h) for i in range(span // seq_len) for h in range(heads)]

        def score(i, h):
            cols = slice(i * seq_len, (i + 1) * seq_len)
            val = proj[0, 2 * width + h * HD : 2 * width + (h + 1) * HD, cols]
            go = gsc[0, h * HD : (h + 1) * HD, cols]
            return dot(ka[h, :, cols], qa[h, :, cols], 0, 0), dot(val, go, 0, 0)

        pair = score(*items[0])
        for n, (i, h) in enumerate(items):
            later = score(*items[n + 1]) if n + 1 < len(items) else None
            cols = slice(i * seq_len, (i + 1) * seq_len)
            rq, rk, rv = [slice(j * width + h * HD, j * width + (h + 1) * HD) for j in range(3)]
            q = proj[0, rq, cols]
            key = proj[0, rk, cols]
            go = gsc[0, h * HD : (h + 1) * HD, cols]
            s, gp = pair
            p = jnp.exp2(s - lse[0, h : h + 1, cols])
            inner = jnp.sum(p * gp, axis=0, keepdims=True)
            g = (p * (gp - inner)).astype(BF16)
            dproj[rq, cols] = (dot(key, g, 1, 0) * scale).astype(BF16)
            dproj[rk, cols] = (dot(q, g, 1, 1) * scale).astype(BF16)
            dproj[rv, cols] = dot(go, p.astype(BF16), 1, 1).astype(BF16)
            pair = later

    @pl.when(block < short_blocks)
    def _():
        run(LS, lens_s, block * (span // LS))

    @pl.when(block >= short_blocks)
    def _():
        run(LL, lens_l, (block - short_blocks) * (span // LL))

    gin[...] = dot(w[...], dproj[...], 1, 0) + gsc[1].astype(F32)
    part = dot(dproj[...], x[...], 1, 1)
    sums = dot(jnp.ones((8, span), BF16), dproj[...], 1, 1)

    @pl.when(step == 0)
    def _():
        if first_call:
            acc[...] = part
            bias[...] = sums
        else:
            acc[...] = acc_in[...] + part
            bias[...] = bias_in[...] + sums

    @pl.when(step > 0)
    def _():
        acc[...] += part
        bias[...] += sums

    if split == 1:

        @pl.when(step == count - 1)
        def _():
            rows = out.shape[1]
            for d in range(out.shape[0]):
                out[d] = acc[d * rows : (d + 1) * rows, :].astype(BF16)

    if split == 2:

        @pl.when(step == count - 1)
        def _():
            pairs, rows = keep.shape[:2]
            mine = me[1]
            for d in range(pairs):
                a = pl.ds(pl.multiple_of((2 * d + mine) * rows, 8), rows)
                c = pl.ds(pl.multiple_of((2 * d + 1 - mine) * rows, 8), rows)
                keep[d] = acc[a, :].astype(BF16)
                send[d] = acc[c, :].astype(BF16)
            total = jnp.concatenate(
                [bias[:, i * width : (i + 1) * width] for i in range(3)], axis=0
            )
            extra[...] = total
            high = total.astype(BF16)
            send[pairs, :24] = high
            send[pairs + 1, :24] = (total - high.astype(F32)).astype(BF16)


def attn_bwd(half, base, stride, me, lens_s, lens_l, x, w, proj, lse, g, carry, dp_count, split):
    width, tokens = x.shape
    span = tokens // 8
    heads = width // HD
    short_blocks = lens_s.shape[0] * LS // span
    fixed = lambda k, *_: (0, 0)
    fixed3 = lambda k, *_: (0, 0, 0)
    here = lambda k, me, *_: (0, lax.bitwise_xor(me[0], base + stride * k) * 2 + half)
    slot = lambda k, *_: (base + stride * k, 0, 0)
    first_call = carry is None
    acc_spec = pl.BlockSpec((3 * width, width), fixed)
    bias_spec = pl.BlockSpec((8, 3 * width), fixed)
    acc_shape = jax.ShapeDtypeStruct((3 * width, width), F32)
    bias_shape = jax.ShapeDtypeStruct((8, 3 * width), F32)
    mine = [g[base + stride * k] for k in range(4 // stride)]
    in_specs = [
        pl.BlockSpec((width, span), here),
        pl.BlockSpec(w.shape, fixed),
        pl.BlockSpec((1, 3 * width, span), slot),
        pl.BlockSpec((1, heads, span), slot),
    ] + [pl.BlockSpec((2, width, span), fixed3)] * len(mine)
    args = [x, w, proj, lse, *mine]
    aliases = {}
    if not first_call:
        gin, acc, bias = carry
        in_specs += [acc_spec, bias_spec, pl.BlockSpec(memory_space=pl.ANY)]
        args += [acc, bias, gin]
        aliases = {3 + len(args) - 1: 0}
    rows = 3 * width // dp_count
    scratch = []
    if split == 0:
        tail = [(acc_spec, acc_shape), (bias_spec, bias_shape)]
    elif split == 1:
        shape = (dp_count, rows, width)
        tail = [
            (pl.BlockSpec(shape, fixed3), jax.ShapeDtypeStruct(shape, BF16)),
            (bias_spec, bias_shape),
        ]
        scratch = [pltpu.VMEM(acc_shape.shape, F32)]
    else:
        keep = (dp_count // 2, rows, width)
        send = (dp_count // 2 + 2, rows, width)
        tail = [
            (pl.BlockSpec(keep, fixed3), jax.ShapeDtypeStruct(keep, BF16)),
            (pl.BlockSpec(send, fixed3), jax.ShapeDtypeStruct(send, BF16)),
            (pl.BlockSpec((24, width), fixed), jax.ShapeDtypeStruct((24, width), F32)),
        ]
        scratch = [pltpu.VMEM(bias_shape.shape, F32), pltpu.VMEM(acc_shape.shape, F32)]
    return pl.pallas_call(
        functools.partial(
            attn_bwd_kernel, half, base, stride, heads, short_blocks, first_call, split
        ),
        grid_spec=pltpu.PrefetchScalarGridSpec(
            num_scalar_prefetch=3,
            grid=(4 // stride,),
            in_specs=in_specs,
            out_specs=[pl.BlockSpec((width, span), here)] + [t[0] for t in tail],
            scratch_shapes=[
                pltpu.VMEM((3 * width, span), BF16),
                pltpu.VMEM((2, width, span), BF16),
                pltpu.VMEM((heads, 2 * HD + 16, span), BF16),
                pltpu.VMEM((heads, 2 * HD + 16, span), BF16),
            ]
            + scratch,
        ),
        out_shape=[jax.ShapeDtypeStruct((width, tokens), F32)] + [t[1] for t in tail],
        input_output_aliases=aliases,
        cost_estimate=COST(16.0 / stride),
        compiler_params=pltpu.CompilerParams(vmem_limit_bytes=VMEM_LIMIT),
        name=f"attn_bwd{half}{base}",
    )(me, lens_s, lens_l, *args)


def prep_kernel(w0, w1, w2, w3, *refs):
    params = refs[:6]
    owt, upt, dnt, upn, dnn, ub, cols, ow = refs[6:]
    weights = (w0, w1, w2, w3)
    model = owt.shape[0]
    width = model // 4

    def eye(n):
        a = lax.broadcasted_iota(jnp.int32, (n, n), 0)
        b = lax.broadcasted_iota(jnp.int32, (n, n), 1)
        return jnp.where(a == b, 1.0, 0.0).astype(BF16)

    big, small = eye(256), eye(width)
    for k, w in enumerate(weights):
        ks = slice(k * width, (k + 1) * width)
        ow[ks, :] = w[:width, :]
        for at in range(0, model, 256):
            lanes = slice(at, at + 256)
            for ref, first in ((upt, width), (dnt, 2 * width)):
                t = dot(big, w[first : first + width, lanes], 1, 1).astype(BF16)
                for g in range(4):
                    low, high = max(at, g * width), min(at + 256, (g + 1) * width)
                    if low < high:
                        start = k * width + low - g * width
                        ref[g, start : start + high - low, :] = t[low - at : high - at, :]
        bt = w[3 * width :, :].astype(F32).T
        ub[:, k : k + 1] = (bt[:, 2:3] + bt[:, 1:2]) + bt[:, 0:1]
    for at in range(0, model, 256):
        owt[at : at + 256, :] = dot(big, ow[:, at : at + 256], 1, 1).astype(BF16)
    for g in range(4):
        upn[g] = dot(small, upt[g], 1, 1).astype(BF16)
        dnn[g] = dot(small, dnt[g], 1, 1).astype(BF16)
    for j, p in enumerate(params):
        cols[:, j : j + 1] = jnp.broadcast_to(p[...], (8, model)).T[:, 0:1]


def prep(weights, params):
    model = weights[0].shape[1]
    width = model // 4
    vmem = pl.BlockSpec(memory_space=pltpu.VMEM)
    shapes = [
        jax.ShapeDtypeStruct((model, model), BF16),
        jax.ShapeDtypeStruct((4, model, width), BF16),
        jax.ShapeDtypeStruct((4, model, width), BF16),
        jax.ShapeDtypeStruct((4, width, model), BF16),
        jax.ShapeDtypeStruct((4, width, model), BF16),
        jax.ShapeDtypeStruct((model, 8), F32),
        jax.ShapeDtypeStruct((model, 8), F32),
        jax.ShapeDtypeStruct((model, model), BF16),
    ]
    return pl.pallas_call(
        prep_kernel,
        in_specs=[vmem] * 10,
        out_specs=[vmem] * len(shapes),
        out_shape=shapes,
        cost_estimate=COST(4.0),
        compiler_params=pltpu.CompilerParams(vmem_limit_bytes=VMEM_LIMIT),
        name="prep",
    )(*weights, *params)


def mid_kernel(half, width, blocks, me, *refs):
    ctx, hid = refs[0:4], refs[4:8]
    og, ub, cols = refs[8:11]
    given = refs[11:17]
    at = 17
    if half:
        acc_hbm, vec_in = refs[at : at + 3], refs[at + 3]
        at += 4
    lo = refs[at]
    back = refs[at + 1 : at + 5]
    at += 5
    if half:
        keep, send, vec_out = refs[at : at + 3]
        at += 3
    else:
        acc_hbm, vec = refs[at : at + 3], refs[at + 3]
        at += 4
    (gow, gup, gdn, owt, upt, dnt, upn, dnn, ow) = refs[at : at + 9]
    at += 9
    (sums, act, slope, first, n1s, gps_s, cats, lows, sem, acc_sem) = refs[at : at + 10]
    if half:
        vec = refs[at + 10]
    accs = (gow, gup, gdn)
    step = pl.program_id(0)
    last = pl.num_programs(0) - 1
    model = 4 * width
    inv = 1.0 / model
    held = (owt, upt, dnn, dnt, upn, ow)

    def own(k):
        return pl.ds(pl.multiple_of(lax.bitwise_xor(me[0], k) * width, width), width)

    def fetch(i):
        return pltpu.make_async_copy(given[i], held[i], sem.at[i])

    def ready(i):
        @pl.when(step == 0)
        def _():
            fetch(i).wait()

    def acc_copy(i):
        if half:
            return pltpu.make_async_copy(acc_hbm[i], accs[i], acc_sem.at[i])
        return pltpu.make_async_copy(accs[i], acc_hbm[i], acc_sem.at[i])

    @pl.when(step == 0)
    def _():
        for i in range(6):
            fetch(i).start()
        if half:
            for i in range(3):
                acc_copy(i).start()
        row = lax.broadcasted_iota(jnp.int32, (16, TILE), 0)
        for g in range(4):
            lows[g, width:, :] = jnp.where(row == 0, 1.0, 0.0).astype(BF16)
        sums[...] = jnp.zeros_like(sums)

    def before(value):
        return value if half else jnp.where(step == 0, 0.0, value)

    def acc_ready(i):
        if half:

            @pl.when(step == 0)
            def _():
                acc_copy(i).wait()

    def acc_done(i):
        if not half:

            @pl.when(step == last)
            def _():
                acc_copy(i).start()

    def col(j):
        return cols[:, j : j + 1]

    def add_sum(j, value):
        sums[j] += sum(value[:, i : i + 128] for i in range(0, TILE, 128))

    for k in range(4):
        cats[k * width : (k + 1) * width, :] = ctx[k][0]
    ready(0)
    first[...] = dot(owt[...], cats[...], 1, 0) + col(0)
    for k in range(4):
        first[own(k), :] += hid[k][...].reshape(width, TILE).astype(F32)
    pre = first[...]
    cen = pre - jnp.sum(pre, axis=0, keepdims=True) * inv
    r1 = lax.rsqrt(jnp.sum(cen * cen, axis=0, keepdims=True) * inv + EPSILON)
    n1 = cen * r1
    n1s[...] = n1
    normed = n1 * col(1) + col(2)
    first[...] = normed
    low = normed.astype(BF16)
    for g in range(4):
        lows[g, :width, :] = low[g * width : (g + 1) * width, :]
    ready(1)
    ready(2)

    def pre_act(g):
        return dot(upt[g], lows[g, :width, :], 1, 0)

    later = pre_act(0)
    for g in range(4):
        rows = slice(g * width, (g + 1) * width)
        raw = later
        if g < 3:
            later = pre_act(g + 1)
        for k in range(4):
            units = slice(k * width, (k + 1) * width)
            pa = raw[units, :] + ub[rows, k : k + 1]
            phi, sl = gelu_parts(pa)
            act[g, units, :] = (pa * phi).astype(BF16)
            slope[g, units, :] = sl
        first[rows, :] += dot(dnn[g], act[g], 1, 0) + cols[rows, 3:4]
    pre = first[...]
    cen = pre - jnp.sum(pre, axis=0, keepdims=True) * inv
    r2 = lax.rsqrt(jnp.sum(cen * cen, axis=0, keepdims=True) * inv + EPSILON)
    n2 = cen * r2
    lo[...] = (n2 * col(4) + col(5)).astype(BF16).T
    ogt = og[...].T.astype(F32)
    add_sum(4, ogt * n2)
    add_sum(5, ogt)
    u = ogt * col(4)
    gps = r2 * (
        u
        - jnp.sum(u, axis=0, keepdims=True) * inv
        - n2 * (jnp.sum(u * n2, axis=0, keepdims=True) * inv)
    )
    add_sum(3, gps)
    gdl = gps.astype(BF16)
    gps_s[...] = gps
    ready(3)
    ready(4)
    acc_ready(1)
    acc_ready(2)

    def grad_act(g):
        return dot(dnt[g], gdl[g * width : (g + 1) * width, :], 1, 0)

    later = grad_act(0)
    for g in range(4):
        rows = slice(g * width, (g + 1) * width)
        raw = later
        if g < 3:
            later = grad_act(g + 1)
        gdn[g] = before(gdn[g]) + dot(act[g], gdl[rows, :], 1, 1)
        gpa = (raw * slope[g]).astype(BF16)
        gup[g] = before(gup[g]) + dot(gpa, lows[g], 1, 1)
        gps_s[rows, :] += dot(upn[g], gpa, 1, 0)
    acc_done(1)
    acc_done(2)
    gn = gps_s[...]
    n1 = n1s[...]
    add_sum(1, gn * n1)
    add_sum(2, gn)
    u = gn * col(1)
    gpf = r1 * (
        u
        - jnp.sum(u, axis=0, keepdims=True) * inv
        - n1 * (jnp.sum(u * n1, axis=0, keepdims=True) * inv)
    )
    gpl = gpf.astype(BF16)
    first[...] = gpl.astype(F32)
    add_sum(0, first[...])
    ready(5)
    acc_ready(0)
    gow[...] = before(gow[...]) + dot(gpl, cats[...], 1, 1)
    acc_done(0)
    for k in range(4):
        back[k][1] = first[own(k), :].astype(BF16)
        back[k][0] = dot(ow[k * width : (k + 1) * width, :], gpl, 1, 0).astype(BF16)

    @pl.when(step == last)
    def _():
        lane = lax.broadcasted_iota(jnp.int32, (1, 128), 1)
        total = vec_in[...] if half else jnp.zeros((model, 128), F32)
        for j in range(6):
            total += jnp.where(lane == j, jnp.sum(sums[j], axis=1, keepdims=True), 0.0)
        vec[...] = total
        if half:
            for g in range(4):
                for k in range(4):
                    vec[own(k), :] += jnp.where(
                        lane == 6 + g, gup[g, k * width : (k + 1) * width, width : width + 1], 0.0
                    )
            more = vec[...].T[:16]
            vec_out[...] = more
            for k in range(4):
                dest = send if k % 2 else keep
                base = (k // 2) * 3 * width
                units = slice(k * width, (k + 1) * width)
                for g in range(4):
                    lanes = slice(g * width, (g + 1) * width)
                    dest[base : base + width, lanes] = gup[g, units, :width].T.astype(BF16)
                    dest[base + width : base + 2 * width, lanes] = gdn[g, units, :].T.astype(BF16)
                    for d in range(blocks):
                        part = width // blocks
                        start = (d * 4 + g) * part
                        to = base + 2 * width + d * part
                        dest[to : to + part, lanes] = gow[start : start + part, units].astype(BF16)
            if blocks > 1:
                part = width // blocks
                high = more.astype(BF16)
                send[6 * width : 6 * width + 16, :] = high
                send[6 * width + part : 6 * width + part + 16, :] = (
                    more - high.astype(F32)
                ).astype(BF16)
        else:
            for i in range(3):
                acc_copy(i).wait()


def mid(half, me, ctx, hid, og, ready, carry, blocks):
    width, span = ctx[0].shape[1:]
    model = 4 * width
    steps = span // TILE
    whole2 = lambda i, *_: (0, 0)
    ctx_tile = pl.BlockSpec((1, width, TILE), lambda i, *_: (0, 0, i))
    hid_own = pl.BlockSpec((width, TILE), lambda i, me: (0, (me[0] * 2 + half) * steps + i))
    hid_tile = pl.BlockSpec((1, width, TILE), lambda i, *_: (1, 0, i))
    back_tile = pl.BlockSpec((2, width, TILE), lambda i, *_: (0, 0, i))
    row_in = pl.BlockSpec((TILE, model), lambda i, *_: (half * steps + i, 0))
    hbm = pl.BlockSpec(memory_space=pl.ANY)
    column = pl.BlockSpec((model, 8), whole2)
    vec_spec = pl.BlockSpec((model, 128), whole2)
    owt, upt, dnt, upn, dnn, ub, cols, ow = ready
    in_specs = [ctx_tile] * 4 + [hid_own] + [hid_tile] * 3 + [row_in, column, column] + [hbm] * 6
    args = [*ctx, *hid, og, ub, cols, owt, upt, dnn, dnt, upn, ow]
    accs = [(model, model), (4, model, width + 16), (4, model, width)]
    piece = jax.ShapeDtypeStruct((2, width, span), BF16)
    scratch = [pltpu.VMEM(a, F32) for a in accs] + [
        pltpu.VMEM((model, model), BF16),
        pltpu.VMEM((4, model, width), BF16),
        pltpu.VMEM((4, model, width), BF16),
        pltpu.VMEM((4, width, model), BF16),
        pltpu.VMEM((4, width, model), BF16),
        pltpu.VMEM((model, model), BF16),
        pltpu.VMEM((6, model, 128), F32),
        pltpu.VMEM((4, model, TILE), BF16),
        pltpu.VMEM((4, model, TILE), F32),
        pltpu.VMEM((model, TILE), F32),
        pltpu.VMEM((model, TILE), F32),
        pltpu.VMEM((model, TILE), F32),
        pltpu.VMEM((model, TILE), BF16),
        pltpu.VMEM((4, width + 16, TILE), BF16),
        pltpu.SemaphoreType.DMA((6,)),
        pltpu.SemaphoreType.DMA((3,)),
    ]
    if half:
        in_specs += [hbm] * 3 + [vec_spec]
        args += list(carry)
        extra = 2 * (width // blocks) if blocks > 1 else 0
        rows = [6 * width, 6 * width + extra]
        tail_specs = [pl.BlockSpec((r, model), whole2) for r in rows + [16]]
        tail_shapes = [jax.ShapeDtypeStruct((r, model), BF16) for r in rows]
        tail_shapes += [jax.ShapeDtypeStruct((16, model), F32)]
        scratch += [pltpu.VMEM((model, 128), F32)]
    else:
        tail_specs = [hbm] * 3 + [vec_spec]
        tail_shapes = [jax.ShapeDtypeStruct(a, F32) for a in accs + [(model, 128)]]
    return pl.pallas_call(
        functools.partial(mid_kernel, half, width, blocks),
        grid_spec=pltpu.PrefetchScalarGridSpec(
            num_scalar_prefetch=1,
            grid=(steps,),
            in_specs=in_specs,
            out_specs=[pl.BlockSpec((TILE, model), lambda i, *_: (i, 0))]
            + [back_tile] * 4
            + tail_specs,
            scratch_shapes=scratch,
        ),
        out_shape=[jax.ShapeDtypeStruct((span, model), BF16)] + [piece] * 4 + tail_shapes,
        cost_estimate=COST(25.0),
        compiler_params=pltpu.CompilerParams(vmem_limit_bytes=VMEM_LIMIT),
        name=f"mid{half}",
    )(me, *args)


def combine_kernel(size, outer, inner, last, index, keep, recv, extra, *refs):
    rows = extra.shape[0]
    more = extra[...] + (recv[size, :rows].astype(F32) + recv[size + 1, :rows].astype(F32))
    if last:
        out, extra_out = refs
        out[...] = keep[...].astype(F32) + recv[:size].astype(F32)
        extra_out[...] = more
        return
    kept, sent, extra_out = refs
    extra_out[...] = more
    hi = more.astype(BF16)
    sent[size // 2, :rows] = hi
    sent[size // 2 + 1, :rows] = (more - hi.astype(F32)).astype(BF16)
    mine = index[0]
    for o in range(outer):
        a = pl.ds((o * 2 + mine) * inner, inner)
        b = pl.ds((o * 2 + 1 - mine) * inner, inner)
        c = slice(o * inner, (o + 1) * inner)
        kept[c] = (keep[a].astype(F32) + recv[a].astype(F32)).astype(BF16)
        sent[c] = (keep[b].astype(F32) + recv[b].astype(F32)).astype(BF16)


def combine(index, keep, recv, extra, outer, inner, last, name):
    size, rows, lanes = keep.shape
    args = [keep, recv, extra]
    vmem = pl.BlockSpec(memory_space=pltpu.VMEM)
    if last:
        shapes = [jax.ShapeDtypeStruct(keep.shape, F32), jax.ShapeDtypeStruct(extra.shape, F32)]
    else:
        shapes = [
            jax.ShapeDtypeStruct((size // 2, rows, lanes), BF16),
            jax.ShapeDtypeStruct((size // 2 + 2, rows, lanes), BF16),
            jax.ShapeDtypeStruct(extra.shape, F32),
        ]
    return pl.pallas_call(
        functools.partial(combine_kernel, size, outer, inner, last),
        in_specs=[pl.BlockSpec(memory_space=pltpu.SMEM)] + [vmem] * len(args),
        out_specs=[vmem] * len(shapes),
        out_shape=shapes,
        cost_estimate=COST(1.0),
        compiler_params=pltpu.CompilerParams(vmem_limit_bytes=VMEM_LIMIT),
        name=name,
    )(index, *args)


def swap(value, axis, bit):
    count = lax.axis_size(axis)
    return lax.ppermute(value, axis, [(i, i ^ bit) for i in range(count)])


def to_chan(pieces):
    return [pieces[0]] + [swap(pieces[k], "chan", k) for k in range(1, 4)]


def gather_chan(value):
    near = swap(value, "chan", 1)
    far = swap(value, "chan", 2)
    return [value, near, far, swap(far, "chan", 1)]


def scatter_dp(pieces):
    index = lax.axis_index("dp")
    count, bit = pieces.shape[0], 1
    while count > 1:
        view = pieces.reshape((count // 2, 2) + pieces.shape[1:])
        digit = (index // bit) % 2
        mine = lax.dynamic_index_in_dim(view, digit, 1, keepdims=False).astype(F32)
        other = lax.dynamic_index_in_dim(view, 1 - digit, 1, keepdims=False)
        total = mine + swap(other, "dp", bit).astype(F32)
        count, bit = count // 2, bit * 2
        pieces = total if count == 1 else total.astype(pieces.dtype)
    return pieces[0]


def sum_dp(value):
    bit = 1
    while bit < lax.axis_size("dp"):
        value = value + swap(value, "dp", bit)
        bit *= 2
    return value


def pack_kernel(ow, up, dn, ub, weights):
    width = ow.shape[0]
    for i, w in enumerate((ow, up, dn)):
        weights[i * width : (i + 1) * width, :] = w[...]
    whole = jnp.broadcast_to(ub[...], (16, ub.shape[1]))
    high = whole.astype(BF16)
    rest = whole - high.astype(F32)
    middle = rest.astype(BF16)
    low = (rest - middle.astype(F32)).astype(BF16)
    row = lax.broadcasted_iota(jnp.int32, whole.shape, 0)
    terms = jnp.where(
        row == 0,
        high.astype(F32),
        jnp.where(row == 1, middle.astype(F32), low.astype(F32)),
    )
    weights[3 * width :, :] = terms.astype(BF16)


def pack(ow, up, dn, ub):
    width, model = ow.shape
    vmem = pl.BlockSpec(memory_space=pltpu.VMEM)
    return pl.pallas_call(
        pack_kernel,
        in_specs=[vmem] * 4,
        out_specs=vmem,
        out_shape=jax.ShapeDtypeStruct((3 * width + 16, model), BF16),
        cost_estimate=COST(1.0),
        compiler_params=pltpu.CompilerParams(vmem_limit_bytes=VMEM_LIMIT),
        name="pack",
    )(ow, up, dn, ub)


def digit(value, b):
    return ((value >> b) & 1)[None]


def reduce_plain(keep, send, vec, dp_count):
    width, model = keep.shape[0] // 6, keep.shape[1]
    sections = 3
    keep = keep.reshape(2, 3, width, model)
    send = send[: 6 * width].reshape(2, 3, width, model)
    rows = width // dp_count
    keep = keep + swap(send, "chan", 1)
    keep = keep[0] + swap(keep[1], "chan", 2)
    if rows < 16:
        last = keep[2].reshape(width, 4, width).transpose(1, 0, 2).reshape(width, model)
        last = last.reshape(dp_count, 4, rows, width).transpose(0, 2, 1, 3)
        keep = jnp.stack([keep[0], keep[1], last.reshape(width, model)])
    keep = keep.reshape(sections, dp_count, rows, model).transpose(1, 0, 2, 3)
    vec = vec + swap(vec, "chan", 1)
    vec = sum_dp(vec + swap(vec, "chan", 2))
    return scatter_dp(keep), vec


def on_device(
    hidden_in,
    lengths_short,
    lengths_long,
    qkv_weight,
    qv_bias,
    out_weight,
    mixer_bias,
    first_gain,
    first_shift,
    up_weight,
    up_bias,
    down_weight,
    down_bias,
    second_gain,
    second_shift,
    out_grad,
):
    width, tokens = hidden_in.shape
    span = tokens // 8
    model = 4 * width
    dp_count = lax.axis_size("dp")
    chan = lax.axis_index("chan").astype(jnp.int32)
    dp = lax.axis_index("dp").astype(jnp.int32)
    me = chan[None]
    bar = lax.optimization_barrier
    fine = width // dp_count >= 16 and dp_count >= 4
    lengths = (lengths_short, lengths_long)
    w = qkv_weight[0]

    packed = pack(out_weight, up_weight, down_weight, up_bias[None])
    params = [
        p[None]
        for p in (mixer_bias, first_gain, first_shift, down_bias, second_gain, second_shift)
    ]
    far = swap(packed, "chan", 2)
    near = swap(packed, "chan", 1)
    x, _ = bar((hidden_in, packed))
    proj, parts, lse = [], [], []
    for half in range(2):
        p, c0, c1, c2, c3, total = attn_fwd(half, me, *lengths, x, w, qv_bias)
        x, p = bar((x, p))
        proj.append(p)
        lse.append(total)
        parts.append([c0, c1, c2, c3])
    first = to_chan(parts[0])
    far, near, first[1], p = bar((far, near, first[1], p))
    weights = [packed, near, far, swap(far, "chan", 1)]
    ready = prep(weights, params)
    second = to_chan(parts[1])
    blocks = dp_count if fine else 1
    hid = [hidden_in] + first[1:]
    lo0, *rest = mid(0, me, first, hid, out_grad, ready, None, blocks)
    g0, carry = rest[:4], rest[4:]
    g0, carry, second = bar((g0, carry, second))
    back0 = to_chan(g0)
    hid = [hidden_in] + second[1:]
    lo1, *rest = mid(1, me, second, hid, out_grad, ready, carry, blocks)
    rest, back0 = bar((rest, back0))
    g1, (keep, send, vec) = rest[:4], rest[4:]
    recv = swap(send, "chan", 1)
    back = [back0, to_chan(g1)]
    ids = jnp.stack([chan, dp & 1])

    def backward(half, base, stride, x, carry, split):
        return attn_bwd(
            half,
            base,
            stride,
            ids,
            *lengths,
            x,
            w,
            proj[half],
            lse[half],
            back[half],
            carry,
            dp_count,
            split,
        )

    if not fine:
        sums, vec = reduce_plain(keep, send, vec, dp_count)
        carry = backward(0, 0, 1, hidden_in, None, 0)
        grad_input, gq, gbias = backward(1, 0, 1, hidden_in, carry, 1)
        gq, gbias = scatter_dp(gq), sum_dp(gbias[0])
    else:
        rows = width // dp_count
        size = 6 * dp_count
        zero = jnp.zeros((1,), jnp.int32)
        recv = recv.reshape(size + 2, rows, model)
        keep = keep.reshape(size, rows, model)

        def stage(index, recv, chan_next, name):
            size = keep.shape[0]
            outer, inner = (1, size // 2) if chan_next else (size // 2, 1)
            return combine(index, keep, recv, vec, outer, inner, False, name)

        keep, send, vec = stage(digit(dp, 0), recv, False, "combine0")
        recv = swap(send, "dp", 1)
        x, keep = bar((hidden_in, keep))
        carry = backward(0, 0, 1, x, None, 0)
        carry, back[1] = bar((carry, back[1]))
        carry = backward(1, 0, 2, x, carry, 0)
        recv, carry = bar((recv, carry))
        keep, send, vec = stage(zero, recv, True, "combine1")
        recv = swap(send, "chan", 2)
        x, keep = bar((x, keep))
        grad_input, gk, gs, gbias = backward(1, 1, 2, x, carry, 2)
        recv, gk, gs = bar((recv, gk, gs))
        grecv = swap(gs, "dp", 1)
        b = 1
        while b < dp_count.bit_length() - 1:
            keep, send, vec = stage(digit(dp, b), recv, False, f"combine_w{b}")
            recv = swap(send, "dp", 1 << b)
            grecv, keep = bar((grecv, keep))
            gk, gs, gbias = combine(
                digit(dp, b),
                gk,
                grecv,
                gbias,
                gk.shape[0] // 2,
                1,
                False,
                f"combine_q{b}",
            )
            grecv = swap(gs, "dp", 1 << b)
            recv, gk = bar((recv, gk))
            b += 1
        sums, vec = combine(zero, keep, recv, vec, 1, 1, True, "combine_w")
        grecv, vec = bar((grecv, vec))
        gq, gbias = combine(zero, gk, grecv, gbias, 1, 1, True, "combine_q")
        gq, gbias = gq[0], gbias[0::8].reshape(3 * width)
    outs = [lo0, lo1]
    own = model // (4 * dp_count)
    mine = lax.dynamic_slice_in_dim(vec[:6], (dp * 4 + chan) * own, own, 1)
    grad_upb = lax.dynamic_slice_in_dim(vec[6:10], chan * width, width, 1).reshape(model)
    return (
        jnp.concatenate(outs, axis=0),
        grad_input,
        gq.T[None],
        jnp.concatenate([gbias[:width], gbias[2 * width :]])[None],
        sums[2].reshape(-1, 4, width).transpose(1, 0, 2).reshape(model // dp_count, width).T,
        mine[0],
        mine[1],
        mine[2],
        sums[0],
        grad_upb,
        sums[1],
        mine[3],
        mine[4],
        mine[5],
    )


def solution(mesh):
    in_specs = (
        P("chan", "dp"),
        P("dp"),
        P("dp"),
        P("chan", None, None),
        P("chan", None),
        P("chan", None),
        P(),
        P(),
        P(),
        P(None, "chan"),
        P("chan"),
        P(None, "chan"),
        P(),
        P(),
        P(),
        P(("dp", "chan"), None),
    )
    out_specs = (
        P(("dp", "chan"), None),
        P("chan", "dp"),
        P("chan", None, "dp"),
        P("chan", None),
        P("chan", "dp"),
        P(("dp", "chan")),
        P(("dp", "chan")),
        P(("dp", "chan")),
        P("dp", "chan"),
        P("chan"),
        P("dp", "chan"),
        P(("dp", "chan")),
        P(("dp", "chan")),
        P(("dp", "chan")),
    )
    return jax.shard_map(
        on_device, mesh=mesh, in_specs=in_specs, out_specs=out_specs, check_vma=False
    )
```

```python
import functools

import jax
import jax.numpy as jnp
from jax import lax
from jax.experimental import pallas as pl
from jax.experimental.pallas import tpu as pltpu
from jax.sharding import PartitionSpec as P

HD = 64
LS = 128
LL = 512
TILE = 256
EPSILON = 1e-06
LOG2E = 1.4426950408889634
F32 = jnp.float32
BF16 = jnp.bfloat16
VMEM_LIMIT = 67043328
VMEM_SMALL = 8388608


def COST(us):
    return pl.CostEstimate(
        flops=int(us * 1.0e9), bytes_accessed=int(us * 1.0e6), transcendentals=0
    )


def dot(a, b, ca, cb):
    return lax.dot_general(a, b, (((ca,), (cb,)), ((), ())), preferred_element_type=F32)


def gelu_parts(v):
    av = jnp.abs(v)
    t = 1.0 / (1.0 + (0.3275911 * 0.7071067811865476) * av)
    e = jnp.exp2((-0.5 * LOG2E) * (v * v))
    poly = t * (
        0.5 * 0.254829592
        + t
        * (
            0.5 * -0.284496736
            + t * (0.5 * 1.421413741 + t * (0.5 * -1.453152027 + t * (0.5 * 1.061405429)))
        )
    )
    tail = poly * e
    phi = jnp.where(v >= 0, 1.0 - tail, tail)
    return phi, phi + v * (0.3989422804014327 * e)


def score_operands(heads, span, seq_len, lens, first, q, key, qa, ka):
    width = heads * HD
    scaled = q.astype(F32) * (HD**-0.5 * LOG2E)
    high = scaled.astype(BF16)
    low = (scaled - high.astype(F32)).astype(BF16)
    pos = lax.broadcasted_iota(jnp.int32, (16, seq_len), 1)
    row = lax.broadcasted_iota(jnp.int32, (16, seq_len), 0)
    for h in range(heads):
        rows = slice(h * HD, (h + 1) * HD)
        qa[h, 0:HD, :] = high[rows]
        qa[h, HD : 2 * HD, :] = low[rows]
        ka[h, 0:HD, :] = key[rows]
        ka[h, HD : 2 * HD, :] = key[rows]
    for i in range(span // seq_len):
        bad = (row == 0) & (pos >= lens[first + i])
        mask = jnp.where(bad, -1e9, 0.0).astype(BF16)
        for h in range(heads):
            ka[h, 2 * HD :, i * seq_len : (i + 1) * seq_len] = mask


def one_rows(qa):
    row = lax.broadcasted_iota(jnp.int32, (16, qa.shape[2]), 0)
    ones = jnp.where(row == 0, 1.0, 0.0).astype(BF16)
    for h in range(qa.shape[0]):
        qa[h, 2 * HD :, :] = ones


def slot_block(me, s):
    return lax.bitwise_xor(me[0], lax.bitwise_and(s, 3)) * 2 + lax.shift_right_logical(s, 2)


def attn_fwd_kernel(heads, short_blocks, me, lens_s, lens_l, x, w, b, proj, *refs):
    outs = refs[:8]
    lse, scr, qa, ka, bcol = refs[8:]
    k = pl.program_id(0)
    block = slot_block(me, k)
    width = heads * HD
    span = x.shape[1]

    @pl.when(k == 0)
    def _():
        t = jnp.broadcast_to(b[...], (8, 2 * width)).T
        bcol[:width] = t[:width]
        bcol[width : 2 * width] = jnp.zeros((width, 8), F32)
        bcol[2 * width :] = t[width:]
        one_rows(qa)

    proj[0] = (dot(w[...], x[...], 0, 0) + bcol[:, 0:1]).astype(BF16)

    def run(seq_len, lens, first):
        score_operands(
            heads, span, seq_len, lens, first, proj[0, :width], proj[0, width : 2 * width], qa, ka
        )
        items = [(i, h) for i in range(span // seq_len) for h in range(heads)]

        def score(i, h):
            cols = slice(i * seq_len, (i + 1) * seq_len)
            return dot(ka[h, :, cols], qa[h, :, cols], 0, 0)

        s = score(*items[0])
        for n, (i, h) in enumerate(items):
            later = score(*items[n + 1]) if n + 1 < len(items) else None
            cols = slice(i * seq_len, (i + 1) * seq_len)
            m = jnp.max(s, axis=0, keepdims=True)
            e = jnp.exp2(s - m)
            total = jnp.sum(e, axis=0, keepdims=True)
            val = proj[0, 2 * width + h * HD : 2 * width + (h + 1) * HD, cols]
            c = dot(val, e.astype(BF16), 1, 0) * (1.0 / total)
            scr[h * HD : (h + 1) * HD, cols] = c.astype(BF16)
            lse[0, h : h + 1, cols] = m + jnp.log2(total)
            s = later

    @pl.when(block < short_blocks)
    def _():
        run(LS, lens_s, block * (span // LS))

    @pl.when(block >= short_blocks)
    def _():
        run(LL, lens_l, (block - short_blocks) * (span // LL))

    for i, out in enumerate(outs):

        @pl.when(k == i)
        def _():
            out[0] = scr[...]
            if i % 4:
                out[1] = x[...]


def attn_fwd(me, lens_s, lens_l, x, w, b):
    width, tokens = x.shape
    span = tokens // 8
    heads = width // HD
    short_blocks = lens_s.shape[0] * LS // span
    fixed = lambda k, *_: (0, 0)
    parts = [(2 if k % 4 else 1, width, span) for k in range(8)]
    return pl.pallas_call(
        functools.partial(attn_fwd_kernel, heads, short_blocks),
        grid_spec=pltpu.PrefetchScalarGridSpec(
            num_scalar_prefetch=3,
            grid=(8,),
            in_specs=[
                pl.BlockSpec((width, span), lambda k, me, *_: (0, slot_block(me, k))),
                pl.BlockSpec(w.shape, fixed),
                pl.BlockSpec(b.shape, fixed),
            ],
            out_specs=[
                pl.BlockSpec((1, 3 * width, span), lambda k, *_: (k, 0, 0)),
                *[pl.BlockSpec(part, lambda k, *_: (0, 0, 0)) for part in parts],
                pl.BlockSpec((1, heads, span), lambda k, *_: (k, 0, 0)),
            ],
            scratch_shapes=[
                pltpu.VMEM((width, span), BF16),
                pltpu.VMEM((heads, 2 * HD + 16, span), BF16),
                pltpu.VMEM((heads, 2 * HD + 16, span), BF16),
                pltpu.VMEM((3 * width, 8), F32),
            ],
        ),
        out_shape=[
            jax.ShapeDtypeStruct((8, 3 * width, span), BF16),
            *[jax.ShapeDtypeStruct(part, BF16) for part in parts],
            jax.ShapeDtypeStruct((8, heads, span), F32),
        ],
        cost_estimate=COST(16.0),
        compiler_params=pltpu.CompilerParams(vmem_limit_bytes=VMEM_LIMIT),
        name="attn_fwd",
    )(me, lens_s, lens_l, x, w, b)


def attn_bwd_kernel(first, count, heads, short_blocks, first_call, split, *refs):
    me, parity, lens_s, lens_l, x, w, proj, lse = refs[:8]
    gs = refs[8 : 8 + count]
    refs = refs[8 + count :]
    if not first_call:
        acc_in, bias_in = refs[:2]
        refs = refs[3:]
    gin = refs[0]
    if split == 0:
        acc, bias = refs[1:3]
        refs = refs[3:]
    elif split == 1:
        out, bias = refs[1:3]
        acc = refs[-1]
        refs = refs[3:-1]
    else:
        keep, send, extra = refs[1:4]
        bias, acc = refs[-2:]
        refs = refs[4:-2]
    dproj, gsc, qa, ka = refs
    step = pl.program_id(0)
    block = slot_block(me, first + step)
    width = heads * HD
    span = x.shape[1]
    scale = HD**-0.5

    @pl.when(step == 0)
    def _():
        one_rows(qa)

    for i, g in enumerate(gs):

        @pl.when(step == i)
        def _():
            gsc[...] = g[...]

    def run(seq_len, lens, first):
        score_operands(
            heads, span, seq_len, lens, first, proj[0, :width], proj[0, width : 2 * width], qa, ka
        )
        items = [(i, h) for i in range(span // seq_len) for h in range(heads)]

        def score(i, h):
            cols = slice(i * seq_len, (i + 1) * seq_len)
            val = proj[0, 2 * width + h * HD : 2 * width + (h + 1) * HD, cols]
            go = gsc[0, h * HD : (h + 1) * HD, cols]
            return dot(ka[h, :, cols], qa[h, :, cols], 0, 0), dot(val, go, 0, 0)

        pair = score(*items[0])
        for n, (i, h) in enumerate(items):
            later = score(*items[n + 1]) if n + 1 < len(items) else None
            cols = slice(i * seq_len, (i + 1) * seq_len)
            rq, rk, rv = [slice(j * width + h * HD, j * width + (h + 1) * HD) for j in range(3)]
            q = proj[0, rq, cols]
            key = proj[0, rk, cols]
            go = gsc[0, h * HD : (h + 1) * HD, cols]
            s, gp = pair
            p = jnp.exp2(s - lse[0, h : h + 1, cols])
            inner = jnp.sum(p * gp, axis=0, keepdims=True)
            g = (p * (gp - inner)).astype(BF16)
            dproj[rq, cols] = (dot(key, g, 1, 0) * scale).astype(BF16)
            dproj[rk, cols] = (dot(q, g, 1, 1) * scale).astype(BF16)
            dproj[rv, cols] = dot(go, p.astype(BF16), 1, 1).astype(BF16)
            pair = later

    @pl.when(block < short_blocks)
    def _():
        run(LS, lens_s, block * (span // LS))

    @pl.when(block >= short_blocks)
    def _():
        run(LL, lens_l, (block - short_blocks) * (span // LL))

    gin[...] = dot(w[...], dproj[...], 1, 0) + gsc[1].astype(F32)
    part = dot(dproj[...], x[...], 1, 1)
    sums = dot(jnp.ones((8, span), BF16), dproj[...], 1, 1)

    @pl.when(step == 0)
    def _():
        if first_call:
            acc[...] = part
            bias[...] = sums
        else:
            acc[...] = acc_in[...] + part
            bias[...] = bias_in[...] + sums

    @pl.when(step > 0)
    def _():
        acc[...] += part
        bias[...] += sums

    if split == 1:

        @pl.when(step == count - 1)
        def _():
            rows = out.shape[1]
            for d in range(out.shape[0]):
                out[d] = acc[d * rows : (d + 1) * rows, :].astype(BF16)

    if split == 2:

        @pl.when(step == count - 1)
        def _():
            pairs, rows = keep.shape[:2]
            mine = parity[0]
            for d in range(pairs):
                a = pl.ds(pl.multiple_of((2 * d + mine) * rows, 8), rows)
                c = pl.ds(pl.multiple_of((2 * d + 1 - mine) * rows, 8), rows)
                keep[d] = acc[a, :].astype(BF16)
                send[d] = acc[c, :].astype(BF16)
            total = jnp.concatenate(
                [bias[:, i * width : (i + 1) * width] for i in range(3)], axis=0
            )
            extra[...] = total
            high = total.astype(BF16)
            send[pairs, :24] = high
            send[pairs, 24:48] = (total - high.astype(F32)).astype(BF16)


def attn_bwd(
    first, count, me, parity, lens_s, lens_l, x, w, proj, lse, g, carry, dp_count, split
):
    width, tokens = x.shape
    span = tokens // 8
    heads = width // HD
    short_blocks = lens_s.shape[0] * LS // span
    fixed = lambda k, *_: (0, 0)
    fixed3 = lambda k, *_: (0, 0, 0)
    here = lambda k, me, *_: (0, slot_block(me, first + k))
    slot = lambda k, *_: (first + k, 0, 0)
    first_call = carry is None
    acc_spec = pl.BlockSpec((3 * width, width), fixed)
    bias_spec = pl.BlockSpec((8, 3 * width), fixed)
    acc_shape = jax.ShapeDtypeStruct((3 * width, width), F32)
    bias_shape = jax.ShapeDtypeStruct((8, 3 * width), F32)
    mine = g[first : first + count]
    in_specs = [
        pl.BlockSpec((width, span), here),
        pl.BlockSpec(w.shape, fixed),
        pl.BlockSpec((1, 3 * width, span), slot),
        pl.BlockSpec((1, heads, span), slot),
    ] + [pl.BlockSpec((2, width, span), fixed3)] * len(mine)
    args = [x, w, proj, lse, *mine]
    aliases = {}
    if not first_call:
        gin, acc, bias = carry
        in_specs += [acc_spec, bias_spec, pl.BlockSpec(memory_space=pl.ANY)]
        args += [acc, bias, gin]
        aliases = {4 + len(args) - 1: 0}
    rows = 3 * width // dp_count
    scratch = []
    if split == 0:
        tail = [(acc_spec, acc_shape), (bias_spec, bias_shape)]
    elif split == 1:
        shape = (dp_count, rows, width)
        tail = [
            (pl.BlockSpec(shape, fixed3), jax.ShapeDtypeStruct(shape, BF16)),
            (bias_spec, bias_shape),
        ]
        scratch = [pltpu.VMEM(acc_shape.shape, F32)]
    else:
        keep = (dp_count // 2, rows, width)
        send = (dp_count // 2 + 1, rows, width)
        tail = [
            (pl.BlockSpec(keep, fixed3), jax.ShapeDtypeStruct(keep, BF16)),
            (pl.BlockSpec(send, fixed3), jax.ShapeDtypeStruct(send, BF16)),
            (pl.BlockSpec((24, width), fixed), jax.ShapeDtypeStruct((24, width), F32)),
        ]
        scratch = [pltpu.VMEM(bias_shape.shape, F32), pltpu.VMEM(acc_shape.shape, F32)]
    return pl.pallas_call(
        functools.partial(
            attn_bwd_kernel, first, count, heads, short_blocks, first_call, split
        ),
        grid_spec=pltpu.PrefetchScalarGridSpec(
            num_scalar_prefetch=4,
            grid=(count,),
            in_specs=in_specs,
            out_specs=[pl.BlockSpec((width, span), here)] + [t[0] for t in tail],
            scratch_shapes=[
                pltpu.VMEM((3 * width, span), BF16),
                pltpu.VMEM((2, width, span), BF16),
                pltpu.VMEM((heads, 2 * HD + 16, span), BF16),
                pltpu.VMEM((heads, 2 * HD + 16, span), BF16),
            ]
            + scratch,
        ),
        out_shape=[jax.ShapeDtypeStruct((width, tokens), F32)] + [t[1] for t in tail],
        input_output_aliases=aliases,
        cost_estimate=COST(4.0 * count),
        compiler_params=pltpu.CompilerParams(vmem_limit_bytes=VMEM_LIMIT),
        name=f"attn_bwd{first}",
    )(me, parity, lens_s, lens_l, *args)


def prep_kernel(w0, w1, w2, w3, *refs):
    params = refs[:6]
    owt, upt, dnt, upn, dnn, ub, cols, ow = refs[6:]
    weights = (w0, w1, w2, w3)
    model = owt.shape[0]
    width = model // 4

    def eye(n):
        a = lax.broadcasted_iota(jnp.int32, (n, n), 0)
        b = lax.broadcasted_iota(jnp.int32, (n, n), 1)
        return jnp.where(a == b, 1.0, 0.0).astype(BF16)

    big, small = eye(256), eye(width)
    for k, w in enumerate(weights):
        ks = slice(k * width, (k + 1) * width)
        ow[ks, :] = w[:width, :]
        for at in range(0, model, 256):
            lanes = slice(at, at + 256)
            for ref, first in ((upt, width), (dnt, 2 * width)):
                t = dot(big, w[first : first + width, lanes], 1, 1).astype(BF16)
                for g in range(4):
                    low, high = max(at, g * width), min(at + 256, (g + 1) * width)
                    if low < high:
                        start = k * width + low - g * width
                        ref[g, start : start + high - low, :] = t[low - at : high - at, :]
        bt = w[3 * width :, :].astype(F32).T
        ub[:, k : k + 1] = (bt[:, 2:3] + bt[:, 1:2]) + bt[:, 0:1]

    @pl.loop(0, model // 256)
    def _(i):
        at = pl.ds(pl.multiple_of(i * 256, 256), 256)
        owt[at, :] = dot(big, ow[:, at], 1, 1).astype(BF16)

    @pl.loop(0, 4)
    def _(g):
        upn[g] = dot(small, upt[g], 1, 1).astype(BF16)
        dnn[g] = dot(small, dnt[g], 1, 1).astype(BF16)

    for j, p in enumerate(params):
        cols[:, j : j + 1] = jnp.broadcast_to(p[...].reshape(1, model), (8, model)).T[:, 0:1]


def prep(weights, params):
    model = weights[0].shape[1]
    width = model // 4
    vmem = pl.BlockSpec(memory_space=pltpu.VMEM)
    shapes = [
        jax.ShapeDtypeStruct((model, model), BF16),
        jax.ShapeDtypeStruct((4, model, width), BF16),
        jax.ShapeDtypeStruct((4, model, width), BF16),
        jax.ShapeDtypeStruct((4, width, model), BF16),
        jax.ShapeDtypeStruct((4, width, model), BF16),
        jax.ShapeDtypeStruct((model, 8), F32),
        jax.ShapeDtypeStruct((model, 8), F32),
        jax.ShapeDtypeStruct((model, model), BF16),
    ]
    return pl.pallas_call(
        prep_kernel,
        in_specs=[vmem] * 10,
        out_specs=[vmem] * len(shapes),
        out_shape=shapes,
        cost_estimate=COST(4.0),
        compiler_params=pltpu.CompilerParams(vmem_limit_bytes=VMEM_LIMIT),
        name="prep",
    )(*weights, *params)


def mid_kernel(half, width, blocks, me, *refs):
    ctx, hid = refs[0:4], refs[4:8]
    og, ub, cols = refs[8:11]
    given = refs[11:17]
    at = 17
    if half:
        acc_hbm, vec_in = refs[at : at + 3], refs[at + 3]
        at += 5
    lo = refs[at]
    back = refs[at + 1 : at + 5]
    at += 5
    if half:
        keep, send, vec_out = refs[at : at + 3]
        at += 3
    else:
        acc_hbm, vec = refs[at : at + 3], refs[at + 3]
        at += 4
    (gow, gup, gdn, owt, upt, dnt, upn, dnn, ow) = refs[at : at + 9]
    at += 9
    (sums, act, slope, first, n1s, gps_s, cats, lows, sem, acc_sem) = refs[at : at + 10]
    if half:
        vec = refs[at + 10]
    accs = (gow, gup, gdn)
    step = pl.program_id(0)
    last = pl.num_programs(0) - 1
    model = 4 * width
    inv = 1.0 / model
    held = (owt, upt, dnn, dnt, upn, ow)

    def own(k):
        return pl.ds(pl.multiple_of(lax.bitwise_xor(me[0], k) * width, width), width)

    def fetch(i):
        return pltpu.make_async_copy(given[i], held[i], sem.at[i])

    def ready(i):
        @pl.when(step == 0)
        def _():
            fetch(i).wait()

    def acc_copy(i):
        if half:
            return pltpu.make_async_copy(acc_hbm[i], accs[i], acc_sem.at[i])
        return pltpu.make_async_copy(accs[i], acc_hbm[i], acc_sem.at[i])

    @pl.when(step == 0)
    def _():
        for i in range(6):
            fetch(i).start()
        if half:
            for i in range(3):
                acc_copy(i).start()
        row = lax.broadcasted_iota(jnp.int32, (16, TILE), 0)
        for g in range(4):
            lows[g, width:, :] = jnp.where(row == 0, 1.0, 0.0).astype(BF16)
        sums[...] = jnp.zeros_like(sums)

    def before(value):
        return value if half else jnp.where(step == 0, 0.0, value)

    def acc_ready(i):
        if half:

            @pl.when(step == 0)
            def _():
                acc_copy(i).wait()

    def acc_done(i):
        if not half:

            @pl.when(step == last)
            def _():
                acc_copy(i).start()

    def col(j):
        return cols[:, j : j + 1]

    def add_sum(j, value):
        sums[j] += sum(value[:, i : i + 128] for i in range(0, TILE, 128))

    for k in range(4):
        cats[k * width : (k + 1) * width, :] = ctx[k][0]
    ready(0)
    first[...] = dot(owt[...], cats[...], 1, 0) + col(0)
    for k in range(4):
        first[own(k), :] += hid[k][...].reshape(width, TILE).astype(F32)
    pre = first[...]
    cen = pre - jnp.sum(pre, axis=0, keepdims=True) * inv
    r1 = lax.rsqrt(jnp.sum(cen * cen, axis=0, keepdims=True) * inv + EPSILON)
    n1 = cen * r1
    n1s[...] = n1
    normed = n1 * col(1) + col(2)
    first[...] = normed
    low = normed.astype(BF16)
    for g in range(4):
        lows[g, :width, :] = low[g * width : (g + 1) * width, :]
    ready(1)
    ready(2)

    def pre_act(g):
        return dot(upt[g], lows[g, :width, :], 1, 0)

    later = pre_act(0)
    for g in range(4):
        rows = slice(g * width, (g + 1) * width)
        raw = later
        if g < 3:
            later = pre_act(g + 1)
        for k in range(4):
            units = slice(k * width, (k + 1) * width)
            pa = raw[units, :] + ub[rows, k : k + 1]
            phi, sl = gelu_parts(pa)
            act[g, units, :] = (pa * phi).astype(BF16)
            slope[g, units, :] = sl
        first[rows, :] += dot(dnn[g], act[g], 1, 0) + cols[rows, 3:4]
    pre = first[...]
    cen = pre - jnp.sum(pre, axis=0, keepdims=True) * inv
    r2 = lax.rsqrt(jnp.sum(cen * cen, axis=0, keepdims=True) * inv + EPSILON)
    n2 = cen * r2
    lo[...] = (n2 * col(4) + col(5)).astype(BF16).T
    ogt = og[...].T.astype(F32)
    add_sum(4, ogt * n2)
    add_sum(5, ogt)
    u = ogt * col(4)
    gps = r2 * (
        u
        - jnp.sum(u, axis=0, keepdims=True) * inv
        - n2 * (jnp.sum(u * n2, axis=0, keepdims=True) * inv)
    )
    add_sum(3, gps)
    gdl = gps.astype(BF16)
    gps_s[...] = gps
    ready(3)
    ready(4)
    acc_ready(1)
    acc_ready(2)

    def grad_act(g):
        return dot(dnt[g], gdl[g * width : (g + 1) * width, :], 1, 0)

    later = grad_act(0)
    for g in range(4):
        rows = slice(g * width, (g + 1) * width)
        raw = later
        if g < 3:
            later = grad_act(g + 1)
        gdn[g] = before(gdn[g]) + dot(act[g], gdl[rows, :], 1, 1)
        gpa = (raw * slope[g]).astype(BF16)
        gup[g] = before(gup[g]) + dot(gpa, lows[g], 1, 1)
        gps_s[rows, :] += dot(upn[g], gpa, 1, 0)
    acc_done(1)
    acc_done(2)
    gn = gps_s[...]
    n1 = n1s[...]
    add_sum(1, gn * n1)
    add_sum(2, gn)
    u = gn * col(1)
    gpf = r1 * (
        u
        - jnp.sum(u, axis=0, keepdims=True) * inv
        - n1 * (jnp.sum(u * n1, axis=0, keepdims=True) * inv)
    )
    gpl = gpf.astype(BF16)
    first[...] = gpl.astype(F32)
    add_sum(0, first[...])
    ready(5)
    acc_ready(0)
    gow[...] = before(gow[...]) + dot(gpl, cats[...], 1, 1)
    acc_done(0)
    for k in range(4):
        back[k][1] = first[own(k), :].astype(BF16)
        back[k][0] = dot(ow[k * width : (k + 1) * width, :], gpl, 1, 0).astype(BF16)

    @pl.when(step == last)
    def _():
        lane = lax.broadcasted_iota(jnp.int32, (1, 128), 1)
        total = vec_in[...] if half else jnp.zeros((model, 128), F32)
        for j in range(6):
            total += jnp.where(lane == j, jnp.sum(sums[j], axis=1, keepdims=True), 0.0)
        vec[...] = total
        if half:
            for g in range(4):
                for k in range(4):
                    vec[own(k), :] += jnp.where(
                        lane == 6 + g, gup[g, k * width : (k + 1) * width, width : width + 1], 0.0
                    )
            more = vec[...].T[:16]
            vec_out[...] = more
            part = width // blocks

            @pl.loop(0, 2)
            def _(far):
                for near in range(2):
                    dest = send if near else keep
                    units = pl.ds(pl.multiple_of((2 * far + near) * width, 8), width)
                    up_rows = pl.ds(pl.multiple_of(far * 3 * width, 16), width)
                    down_rows = pl.ds(pl.multiple_of((far * 3 + 1) * width, 16), width)
                    for g in range(4):
                        lanes = slice(g * width, (g + 1) * width)
                        dest[up_rows, lanes] = gup[g, units, :width].T.astype(BF16)
                        dest[down_rows, lanes] = gdn[g, units, :].T.astype(BF16)

            pairs = 2 if blocks > 1 else 1

            @pl.loop(0, blocks // pairs)
            def _(pair):
                for k in range(4):
                    dest = send if k % 2 else keep
                    base = ((k // 2) * 3 + 2) * width
                    units = slice(k * width, (k + 1) * width)
                    to = pl.ds(pl.multiple_of(base + pair * pairs * part, 16), pairs * part)
                    for g in range(4):
                        lanes = slice(g * width, (g + 1) * width)
                        rows = []
                        for i in range(pairs):
                            start = ((pair * pairs + i) * 4 + g) * part
                            rows.append(gow[pl.ds(pl.multiple_of(start, 8), part), units])
                        dest[to, lanes] = jnp.concatenate(rows, axis=0).astype(BF16)

            if blocks > 1:
                high = more.astype(BF16)
                send[6 * width : 6 * width + 16, :] = high
                send[6 * width + part : 6 * width + part + 16, :] = (
                    more - high.astype(F32)
                ).astype(BF16)
        else:
            for i in range(3):
                acc_copy(i).wait()


def mid(half, me, ctx, hid, og, ready, carry, blocks):
    width, span = ctx[0].shape[1:]
    model = 4 * width
    steps = span // TILE
    whole2 = lambda i, *_: (0, 0)
    ctx_tile = pl.BlockSpec((1, width, TILE), lambda i, *_: (0, 0, i))
    hid_own = pl.BlockSpec((width, TILE), lambda i, me: (0, (me[0] * 2 + half) * steps + i))
    hid_tile = pl.BlockSpec((1, width, TILE), lambda i, *_: (1, 0, i))
    back_tile = pl.BlockSpec((2, width, TILE), lambda i, *_: (0, 0, i))
    row_in = pl.BlockSpec((TILE, model), lambda i, *_: (half * steps + i, 0))
    hbm = pl.BlockSpec(memory_space=pl.ANY)
    column = pl.BlockSpec((model, 8), whole2)
    vec_spec = pl.BlockSpec((model, 128), whole2)
    owt, upt, dnt, upn, dnn, ub, cols, ow = ready
    in_specs = [ctx_tile] * 4 + [hid_own] + [hid_tile] * 3 + [row_in, column, column] + [hbm] * 6
    args = [*ctx, *hid, og, ub, cols, owt, upt, dnn, dnt, upn, ow]
    accs = [(model, model), (4, model, width + 16), (4, model, width)]
    piece = jax.ShapeDtypeStruct((2, width, span), BF16)
    scratch = [pltpu.VMEM(a, F32) for a in accs] + [
        pltpu.VMEM((model, model), BF16),
        pltpu.VMEM((4, model, width), BF16),
        pltpu.VMEM((4, model, width), BF16),
        pltpu.VMEM((4, width, model), BF16),
        pltpu.VMEM((4, width, model), BF16),
        pltpu.VMEM((model, model), BF16),
        pltpu.VMEM((6, model, 128), F32),
        pltpu.VMEM((4, model, TILE), BF16),
        pltpu.VMEM((4, model, TILE), F32),
        pltpu.VMEM((model, TILE), F32),
        pltpu.VMEM((model, TILE), F32),
        pltpu.VMEM((model, TILE), F32),
        pltpu.VMEM((model, TILE), BF16),
        pltpu.VMEM((4, width + 16, TILE), BF16),
        pltpu.SemaphoreType.DMA((6,)),
        pltpu.SemaphoreType.DMA((3,)),
    ]
    aliases = {}
    if half:
        in_specs += [hbm] * 3 + [vec_spec, hbm]
        aliases = {len(args) + 5: 0}
        args += list(carry)
        extra = 2 * (width // blocks) if blocks > 1 else 0
        rows = [6 * width, 6 * width + extra]
        tail_specs = [pl.BlockSpec((r, model), whole2) for r in rows + [16]]
        tail_shapes = [jax.ShapeDtypeStruct((r, model), BF16) for r in rows]
        tail_shapes += [jax.ShapeDtypeStruct((16, model), F32)]
        scratch += [pltpu.VMEM((model, 128), F32)]
    else:
        tail_specs = [hbm] * 3 + [vec_spec]
        tail_shapes = [jax.ShapeDtypeStruct(a, F32) for a in accs + [(model, 128)]]
    return pl.pallas_call(
        functools.partial(mid_kernel, half, width, blocks),
        grid_spec=pltpu.PrefetchScalarGridSpec(
            num_scalar_prefetch=1,
            grid=(steps,),
            in_specs=in_specs,
            out_specs=[row_in] + [back_tile] * 4
            + tail_specs,
            scratch_shapes=scratch,
        ),
        out_shape=[jax.ShapeDtypeStruct((2 * span, model), BF16)] + [piece] * 4 + tail_shapes,
        input_output_aliases=aliases,
        cost_estimate=COST(25.0),
        compiler_params=pltpu.CompilerParams(vmem_limit_bytes=VMEM_LIMIT),
        name=f"mid{half}",
    )(me, *args)


def combine_kernel(size, outer, inner, index, keep, recv, extra, kept, sent, extra_out):
    rows = extra.shape[0]
    more = extra[...] + (recv[size, :rows].astype(F32) + recv[size + 1, :rows].astype(F32))
    extra_out[...] = more
    hi = more.astype(BF16)
    sent[size // 2, :rows] = hi
    sent[size // 2 + 1, :rows] = (more - hi.astype(F32)).astype(BF16)
    mine = index[0]
    for o in range(outer):
        a = pl.ds((o * 2 + mine) * inner, inner)
        b = pl.ds((o * 2 + 1 - mine) * inner, inner)
        c = slice(o * inner, (o + 1) * inner)
        kept[c] = (keep[a].astype(F32) + recv[a].astype(F32)).astype(BF16)
        sent[c] = (keep[b].astype(F32) + recv[b].astype(F32)).astype(BF16)


def combine(index, keep, recv, extra, outer, inner, name):
    size, rows, lanes = keep.shape
    vmem = pl.BlockSpec(memory_space=pltpu.VMEM)
    shapes = [
        jax.ShapeDtypeStruct((size // 2, rows, lanes), BF16),
        jax.ShapeDtypeStruct((size // 2 + 2, rows, lanes), BF16),
        jax.ShapeDtypeStruct(extra.shape, F32),
    ]
    return pl.pallas_call(
        functools.partial(combine_kernel, size, outer, inner),
        in_specs=[pl.BlockSpec(memory_space=pltpu.SMEM)] + [vmem] * 3,
        out_specs=[vmem] * len(shapes),
        out_shape=shapes,
        cost_estimate=COST(1.0),
        compiler_params=pltpu.CompilerParams(vmem_limit_bytes=VMEM_LIMIT),
        name=name,
    )(index, keep, recv, extra)


def blend_kernel(joint, last, index, wk, wr, vec, qk, *refs):
    if not joint:
        qr, qb, refs = refs[0], refs[1], refs[2:]
    nw, rows, model = wk.shape
    nq, width = qk.shape[0], qk.shape[2]
    pitch = model // 3
    if joint:
        terms = wr[nw].astype(F32)
        more = vec[:12] + (terms[:12] + terms[12:24])
    else:
        more = vec[:12] + (wr[nw, :16].astype(F32) + wr[nw + 1, :16].astype(F32))[:12]
        bias = qb[...] + (qr[nq, :24].astype(F32) + qr[nq, 24:48].astype(F32))

    def wsum(i):
        return wk[i].astype(F32) + wr[i].astype(F32)

    def qsum(i, j):
        part = slice(j * rows, (j + 1) * rows)
        if joint:
            other = wr[nw + 1 + i, :, j * pitch : j * pitch + width]
        else:
            other = qr[i, part, :]
        return qk[i, part, :].astype(F32) + other.astype(F32)

    if last:
        gup, gdn, gow, gqkv, gqv, gub = refs[:6]
        vecs = refs[6:]
        gup[...] = wsum(0)
        gdn[...] = wsum(1)
        ow = wsum(2)
        quarter = model // 4
        gow[...] = jnp.concatenate(
            [ow[:, j * quarter : (j + 1) * quarter] for j in range(4)], axis=0
        ).T
        for j in range(3):
            gqkv[j * rows : (j + 1) * rows, :] = qsum(0, j)
        gqv[:, :width] = more[10:11, :width]
        gqv[:, width:] = more[10:11, 2 * pitch : 2 * pitch + width]
        own = vecs[0].shape[0]
        more = jnp.concatenate([more, jnp.zeros((4, model), F32)], axis=0)
        here = pltpu.roll(more, index[1], 1)
        for j, v in enumerate(vecs):
            v[...] = here[j, :own]
        here = pltpu.roll(more, index[2], 1)
        gub[...] = jnp.concatenate([here[6 + j, :quarter] for j in range(4)])
        return
    wkept, sent, vec_out, qkept = refs
    mine = index[0]
    vec_out[:12] = more
    vec_out[12:] = jnp.zeros((4, model), F32)
    if not joint:
        for j in range(3):
            vec_out[10:11, j * pitch : j * pitch + width] = bias[8 * j : 8 * j + 1]
    half = nw // 2
    more = vec_out[:12]
    hi = more.astype(BF16).astype(F32)
    sent[half, :24] = jnp.concatenate([hi, more - hi], axis=0).astype(BF16)
    for i in range(half):
        wkept[i] = wsum(2 * i + mine).astype(BF16)
        sent[i] = wsum(2 * i + 1 - mine).astype(BF16)
    at = half + 1
    for i in range(nq // 2):
        for j in range(3):
            qkept[i, j * rows : (j + 1) * rows, :] = qsum(2 * i + mine, j).astype(BF16)
            sent[at + i, :, j * pitch : j * pitch + width] = qsum(2 * i + 1 - mine, j).astype(BF16)


def blend(index, wk, wr, vec, qk, qr, qb, last, name):
    nw, rows, model = wk.shape
    nq, _, width = qk.shape
    vmem = pl.BlockSpec(memory_space=pltpu.VMEM)
    args = [wk, wr, vec, qk] + ([] if qr is None else [qr, qb])
    shape = jax.ShapeDtypeStruct
    if last:
        quarter = model // 4
        shapes = [
            shape((rows, model), F32),
            shape((rows, model), F32),
            shape((quarter, 4 * rows), F32),
            shape((3 * rows, width), F32),
            shape((1, 2 * width), F32),
            shape((model,), F32),
        ] + [shape((rows,), F32)] * 6
    else:
        shapes = [
            shape((nw // 2, rows, model), BF16),
            shape((nw // 2 + nq // 2 + 1, rows, model), BF16),
            shape(vec.shape, F32),
            shape((nq // 2, 3 * rows, width), BF16),
        ]
    return pl.pallas_call(
        functools.partial(blend_kernel, qr is None, last),
        in_specs=[pl.BlockSpec(memory_space=pltpu.SMEM)] + [vmem] * len(args),
        out_specs=[vmem] * len(shapes),
        out_shape=shapes,
        cost_estimate=COST(1.0),
        compiler_params=pltpu.CompilerParams(vmem_limit_bytes=VMEM_SMALL),
        name=name,
    )(index, *args)


def swap(value, axis, bit):
    count = lax.axis_size(axis)
    return lax.ppermute(value, axis, [(i, i ^ bit) for i in range(count)])


def to_chan(pieces):
    return [pieces[0]] + [swap(pieces[k], "chan", k) for k in range(1, 4)]


def gather_chan(value):
    near = swap(value, "chan", 1)
    far = swap(value, "chan", 2)
    return [value, near, far, swap(far, "chan", 1)]


def scatter_dp(pieces):
    index = lax.axis_index("dp")
    count, bit = pieces.shape[0], 1
    while count > 1:
        view = pieces.reshape((count // 2, 2) + pieces.shape[1:])
        digit = (index // bit) % 2
        mine = lax.dynamic_index_in_dim(view, digit, 1, keepdims=False).astype(F32)
        other = lax.dynamic_index_in_dim(view, 1 - digit, 1, keepdims=False)
        total = mine + swap(other, "dp", bit).astype(F32)
        count, bit = count // 2, bit * 2
        pieces = total if count == 1 else total.astype(pieces.dtype)
    return pieces[0]


def sum_dp(value):
    bit = 1
    while bit < lax.axis_size("dp"):
        value = value + swap(value, "dp", bit)
        bit *= 2
    return value


def pack_kernel(ow, up, dn, ub, weights):
    width = ow.shape[0]
    for i, w in enumerate((ow, up, dn)):
        weights[i * width : (i + 1) * width, :] = w[...]
    whole = jnp.broadcast_to(ub[...].reshape(1, -1), (16, ub.shape[0]))
    high = whole.astype(BF16)
    rest = whole - high.astype(F32)
    middle = rest.astype(BF16)
    low = (rest - middle.astype(F32)).astype(BF16)
    row = lax.broadcasted_iota(jnp.int32, whole.shape, 0)
    terms = jnp.where(
        row == 0,
        high.astype(F32),
        jnp.where(row == 1, middle.astype(F32), low.astype(F32)),
    )
    weights[3 * width :, :] = terms.astype(BF16)


def pack(ow, up, dn, ub):
    width, model = ow.shape
    vmem = pl.BlockSpec(memory_space=pltpu.VMEM)
    return pl.pallas_call(
        pack_kernel,
        in_specs=[vmem] * 4,
        out_specs=vmem,
        out_shape=jax.ShapeDtypeStruct((3 * width + 16, model), BF16),
        cost_estimate=COST(1.0),
        compiler_params=pltpu.CompilerParams(vmem_limit_bytes=VMEM_LIMIT),
        name="pack",
    )(ow, up, dn, ub)


def digit(value, b):
    return ((value >> b) & 1)[None]


def reduce_plain(keep, send, vec, dp_count):
    width, model = keep.shape[0] // 6, keep.shape[1]
    sections = 3
    keep = keep.reshape(2, 3, width, model)
    send = send[: 6 * width].reshape(2, 3, width, model)
    rows = width // dp_count
    keep = keep + swap(send, "chan", 1)
    keep = keep[0] + swap(keep[1], "chan", 2)
    if rows < 16:
        last = keep[2].reshape(width, 4, width).transpose(1, 0, 2).reshape(width, model)
        last = last.reshape(dp_count, 4, rows, width).transpose(0, 2, 1, 3)
        keep = jnp.stack([keep[0], keep[1], last.reshape(width, model)])
    keep = keep.reshape(sections, dp_count, rows, model).transpose(1, 0, 2, 3)
    vec = vec + swap(vec, "chan", 1)
    vec = sum_dp(vec + swap(vec, "chan", 2))
    return scatter_dp(keep), vec


def on_device(
    hidden_in,
    lengths_short,
    lengths_long,
    qkv_weight,
    qv_bias,
    out_weight,
    mixer_bias,
    first_gain,
    first_shift,
    up_weight,
    up_bias,
    down_weight,
    down_bias,
    second_gain,
    second_shift,
    out_grad,
):
    width, tokens = hidden_in.shape
    span = tokens // 8
    model = 4 * width
    dp_count = lax.axis_size("dp")
    chan = lax.axis_index("chan").astype(jnp.int32)
    dp = lax.axis_index("dp").astype(jnp.int32)
    me = chan[None]
    bar = lax.optimization_barrier
    fine = width // dp_count >= 16 and dp_count >= 4
    lengths = (lengths_short, lengths_long)
    w = qkv_weight[0]

    packed = pack(out_weight, up_weight, down_weight, up_bias)
    params = [mixer_bias, first_gain, first_shift, down_bias, second_gain, second_shift]
    far = swap(packed, "chan", 2)
    near = swap(packed, "chan", 1)
    x, _ = bar((hidden_in, packed))
    proj, *parts, lse = attn_fwd(me, *lengths, x, w, qv_bias)
    parts = [parts[:4], parts[4:]]
    far, near, parts = bar((far, near, parts))
    first = to_chan(parts[0])
    weights = [packed, near, far, swap(far, "chan", 1)]
    ready = prep(weights, params)
    second = to_chan(parts[1])
    blocks = dp_count if fine else 1
    hid = [hidden_in] + first[1:]
    lo, *rest = mid(0, me, first, hid, out_grad, ready, None, blocks)
    g0, carry = rest[:4], [*rest[4:], lo]
    g0, carry, second = bar((g0, carry, second))
    back0 = to_chan(g0)
    hid = [hidden_in] + second[1:]
    lo, *rest = mid(1, me, second, hid, out_grad, ready, carry, blocks)
    rest, back0 = bar((rest, back0))
    g1, (keep, send, vec) = rest[:4], rest[4:]
    recv = swap(send, "chan", 1)
    back = [*back0, *to_chan(g1)]
    parity = digit(dp, 0)

    def backward(start, count, x, carry, split):
        return attn_bwd(
            start,
            count,
            me,
            parity,
            *lengths,
            x,
            w,
            proj,
            lse,
            back,
            carry,
            dp_count,
            split,
        )

    if not fine:
        sums, vec = reduce_plain(keep, send, vec, dp_count)
        carry = backward(0, 5, hidden_in, None, 0)
        grad_input, gq, gbias = backward(5, 3, hidden_in, carry, 1)
        gq, gbias = scatter_dp(gq), sum_dp(gbias[0])
        own = width // dp_count
        mine = lax.dynamic_slice_in_dim(vec[:6], (dp * 4 + chan) * own, own, 1)
        mine = [mine[i] for i in range(6)]
        gub = lax.dynamic_slice_in_dim(vec[6:10], chan * width, width, 1).reshape(model)
        gup, gdn = sums[0], sums[1]
        gow = sums[2].reshape(-1, 4, width).transpose(1, 0, 2).reshape(model // dp_count, width).T
        gqv = jnp.concatenate([gbias[:width], gbias[2 * width :]])[None]
    else:
        rows = width // dp_count
        size = 6 * dp_count
        zero = jnp.zeros((1,), jnp.int32)
        recv = recv.reshape(size + 2, rows, model)
        keep = keep.reshape(size, rows, model)

        def stage(index, recv, chan_next, name):
            size = keep.shape[0]
            outer, inner = (1, size // 2) if chan_next else (size // 2, 1)
            return combine(index, keep, recv, vec, outer, inner, name)

        keep, send, vec = stage(parity, recv, False, "combine0")
        recv = swap(send, "dp", 1)
        x, keep = bar((hidden_in, keep))
        carry = backward(0, 5, x, None, 0)
        recv, carry = bar((recv, carry))
        keep, send, vec = stage(zero, recv, True, "combine1")
        recv = swap(send, "chan", 2)
        x, keep = bar((x, keep))
        grad_input, gk, gs, gbias = backward(5, 3, x, carry, 2)
        recv, gk, gs = bar((recv, gk, gs))
        grecv = swap(gs, "dp", 1)
        b = 1
        while b < dp_count.bit_length() - 1:
            keep, send, vec, gk = blend(
                digit(dp, b), keep, recv, vec, gk, grecv, gbias, False, f"blend{b}"
            )
            recv, grecv = swap(send, "dp", 1 << b), None
            b += 1
        index = jnp.stack(
            [
                jnp.zeros_like(dp),
                (model - (dp * 4 + chan) * rows) % model,
                (model - chan * width) % model,
            ]
        )
        gup, gdn, gow, gq, gqv, gub, *mine = blend(
            index, keep, recv, vec, gk, grecv, gbias, True, "blend"
        )
    return (
        lo,
        grad_input,
        gq.T[None],
        gqv,
        gow,
        mine[0],
        mine[1],
        mine[2],
        gup,
        gub,
        gdn,
        mine[3],
        mine[4],
        mine[5],
    )


def solution(mesh):
    in_specs = (
        P("chan", "dp"),
        P("dp"),
        P("dp"),
        P("chan", None, None),
        P("chan", None),
        P("chan", None),
        P(),
        P(),
        P(),
        P(None, "chan"),
        P("chan"),
        P(None, "chan"),
        P(),
        P(),
        P(),
        P(("dp", "chan"), None),
    )
    out_specs = (
        P(("dp", "chan"), None),
        P("chan", "dp"),
        P("chan", None, "dp"),
        P("chan", None),
        P("chan", "dp"),
        P(("dp", "chan")),
        P(("dp", "chan")),
        P(("dp", "chan")),
        P("dp", "chan"),
        P("chan"),
        P("dp", "chan"),
        P(("dp", "chan")),
        P(("dp", "chan")),
        P(("dp", "chan")),
    )
    return jax.shard_map(
        on_device, mesh=mesh, in_specs=in_specs, out_specs=out_specs, check_vma=False
    )
```

```python
import functools

import jax
import jax.numpy as jnp
from jax import lax
from jax.experimental import pallas as pl
from jax.experimental.pallas import tpu as pltpu
from jax.sharding import PartitionSpec as P

HD = 64
LS = 128
LL = 512
TILE = 256
EPSILON = 1e-06
LOG2E = 1.4426950408889634
F32 = jnp.float32
BF16 = jnp.bfloat16
VMEM_LIMIT = 67043328
VMEM_SMALL = 8388608


def COST(us):
    return pl.CostEstimate(
        flops=int(us * 1.0e9), bytes_accessed=int(us * 1.0e6), transcendentals=0
    )


def dot(a, b, ca, cb):
    return lax.dot_general(a, b, (((ca,), (cb,)), ((), ())), preferred_element_type=F32)


def gelu_parts(v):
    av = jnp.abs(v)
    t = 1.0 / (1.0 + (0.3275911 * 0.7071067811865476) * av)
    e = jnp.exp2((-0.5 * LOG2E) * (v * v))
    poly = t * (
        0.5 * 0.254829592
        + t
        * (
            0.5 * -0.284496736
            + t * (0.5 * 1.421413741 + t * (0.5 * -1.453152027 + t * (0.5 * 1.061405429)))
        )
    )
    tail = poly * e
    phi = jnp.where(v >= 0, 1.0 - tail, tail)
    return phi, phi + v * (0.3989422804014327 * e)


def score_operands(heads, span, seq_len, lens, first, q, key, qa, ka):
    width = heads * HD
    scaled = q.astype(F32) * (HD**-0.5 * LOG2E)
    high = scaled.astype(BF16)
    low = (scaled - high.astype(F32)).astype(BF16)
    pos = lax.broadcasted_iota(jnp.int32, (16, seq_len), 1)
    row = lax.broadcasted_iota(jnp.int32, (16, seq_len), 0)
    for h in range(heads):
        rows = slice(h * HD, (h + 1) * HD)
        qa[h, 0:HD, :] = high[rows]
        qa[h, HD : 2 * HD, :] = low[rows]
        ka[h, 0:HD, :] = key[rows]
        ka[h, HD : 2 * HD, :] = key[rows]
    for i in range(span // seq_len):
        bad = (row == 0) & (pos >= lens[first + i])
        mask = jnp.where(bad, -1e9, 0.0).astype(BF16)
        for h in range(heads):
            ka[h, 2 * HD :, i * seq_len : (i + 1) * seq_len] = mask


def one_rows(qa):
    row = lax.broadcasted_iota(jnp.int32, (16, qa.shape[2]), 0)
    ones = jnp.where(row == 0, 1.0, 0.0).astype(BF16)
    for h in range(qa.shape[0]):
        qa[h, 2 * HD :, :] = ones


def slot_block(me, s):
    return lax.bitwise_xor(me[0], lax.bitwise_and(s, 3)) * 2 + lax.shift_right_logical(s, 2)


def attn_fwd_kernel(heads, short_blocks, me, lens_s, lens_l, x, w, b, proj, *refs):
    outs = refs[:8]
    lse, scr, qa, ka, bcol = refs[8:]
    k = pl.program_id(0)
    block = slot_block(me, k)
    width = heads * HD
    span = x.shape[1]

    @pl.when(k == 0)
    def _():
        t = jnp.broadcast_to(b[...], (8, 2 * width)).T
        bcol[:width] = t[:width]
        bcol[width : 2 * width] = jnp.zeros((width, 8), F32)
        bcol[2 * width :] = t[width:]
        one_rows(qa)

    proj[0] = (dot(w[...], x[...], 0, 0) + bcol[:, 0:1]).astype(BF16)

    def run(seq_len, lens, first, together):
        score_operands(
            heads, span, seq_len, lens, first, proj[0, :width], proj[0, width : 2 * width], qa, ka
        )
        items = [(i, h) for i in range(span // seq_len) for h in range(heads)]
        groups = [items[n : n + together] for n in range(0, len(items), together)]

        def score(i, h):
            cols = slice(i * seq_len, (i + 1) * seq_len)
            return dot(ka[h, :, cols], qa[h, :, cols], 0, 0)

        scores = [score(*item) for item in groups[0]]
        for n, group in enumerate(groups):
            later = [score(*item) for item in groups[n + 1]] if n + 1 < len(groups) else None
            tops = [jnp.max(s, axis=0, keepdims=True) for s in scores]
            exps = [jnp.exp2(s - m) for s, m in zip(scores, tops)]
            sums = [jnp.sum(e, axis=0, keepdims=True) for e in exps]
            for (i, h), m, e, total in zip(group, tops, exps, sums):
                cols = slice(i * seq_len, (i + 1) * seq_len)
                val = proj[0, 2 * width + h * HD : 2 * width + (h + 1) * HD, cols]
                c = dot(val, e.astype(BF16), 1, 0) * (1.0 / total)
                scr[h * HD : (h + 1) * HD, cols] = c.astype(BF16)
                lse[0, h : h + 1, cols] = m + jnp.log2(total)
            scores = later

    @pl.when(block < short_blocks)
    def _():
        run(LS, lens_s, block * (span // LS), 6)

    @pl.when(block >= short_blocks)
    def _():
        run(LL, lens_l, (block - short_blocks) * (span // LL), 1)

    for i, out in enumerate(outs):

        @pl.when(k == i)
        def _():
            out[0] = scr[...]
            if i % 4:
                out[1] = x[...]


def attn_fwd(me, lens_s, lens_l, x, w, b):
    width, tokens = x.shape
    span = tokens // 8
    heads = width // HD
    short_blocks = lens_s.shape[0] * LS // span
    fixed = lambda k, *_: (0, 0)
    parts = [(2 if k % 4 else 1, width, span) for k in range(8)]
    return pl.pallas_call(
        functools.partial(attn_fwd_kernel, heads, short_blocks),
        grid_spec=pltpu.PrefetchScalarGridSpec(
            num_scalar_prefetch=3,
            grid=(8,),
            in_specs=[
                pl.BlockSpec((width, span), lambda k, me, *_: (0, slot_block(me, k))),
                pl.BlockSpec(w.shape, fixed),
                pl.BlockSpec(b.shape, fixed),
            ],
            out_specs=[
                pl.BlockSpec((1, 3 * width, span), lambda k, *_: (k, 0, 0)),
                *[pl.BlockSpec(part, lambda k, *_: (0, 0, 0)) for part in parts],
                pl.BlockSpec((1, heads, span), lambda k, *_: (k, 0, 0)),
            ],
            scratch_shapes=[
                pltpu.VMEM((width, span), BF16),
                pltpu.VMEM((heads, 2 * HD + 16, span), BF16),
                pltpu.VMEM((heads, 2 * HD + 16, span), BF16),
                pltpu.VMEM((3 * width, 8), F32),
            ],
        ),
        out_shape=[
            jax.ShapeDtypeStruct((8, 3 * width, span), BF16),
            *[jax.ShapeDtypeStruct(part, BF16) for part in parts],
            jax.ShapeDtypeStruct((8, heads, span), F32),
        ],
        cost_estimate=COST(16.0),
        compiler_params=pltpu.CompilerParams(vmem_limit_bytes=VMEM_LIMIT),
        name="attn_fwd",
    )(me, lens_s, lens_l, x, w, b)


def attn_bwd_kernel(first, count, heads, short_blocks, first_call, split, *refs):
    me, parity, lens_s, lens_l, x, w, proj, lse = refs[:8]
    gs = refs[8 : 8 + count]
    refs = refs[8 + count :]
    if not first_call:
        acc_in, bias_in = refs[:2]
        refs = refs[3:]
    gin = refs[0]
    if split == 0:
        acc, bias = refs[1:3]
        refs = refs[3:]
    elif split == 1:
        out, bias = refs[1:3]
        acc = refs[-1]
        refs = refs[3:-1]
    else:
        keep, send, extra = refs[1:4]
        bias, acc = refs[-2:]
        refs = refs[4:-2]
    dproj, gsc, qa, ka = refs
    step = pl.program_id(0)
    block = slot_block(me, first + step)
    width = heads * HD
    span = x.shape[1]
    scale = HD**-0.5

    @pl.when(step == 0)
    def _():
        one_rows(qa)

    for i, g in enumerate(gs):

        @pl.when(step == i)
        def _():
            gsc[...] = g[...]

    def run(seq_len, lens, first, together):
        score_operands(
            heads, span, seq_len, lens, first, proj[0, :width], proj[0, width : 2 * width], qa, ka
        )
        items = [(i, h) for i in range(span // seq_len) for h in range(heads)]
        groups = [items[n : n + together] for n in range(0, len(items), together)]

        def score(i, h):
            cols = slice(i * seq_len, (i + 1) * seq_len)
            val = proj[0, 2 * width + h * HD : 2 * width + (h + 1) * HD, cols]
            go = gsc[0, h * HD : (h + 1) * HD, cols]
            return dot(ka[h, :, cols], qa[h, :, cols], 0, 0), dot(val, go, 0, 0)

        pairs = [score(*item) for item in groups[0]]
        for n, group in enumerate(groups):
            later = [score(*item) for item in groups[n + 1]] if n + 1 < len(groups) else None
            ps = []
            for (i, h), (s, _) in zip(group, pairs):
                cols = slice(i * seq_len, (i + 1) * seq_len)
                ps.append(jnp.exp2(s - lse[0, h : h + 1, cols]))
            inner = [jnp.sum(p * gp, axis=0, keepdims=True) for p, (_, gp) in zip(ps, pairs)]
            gs = [(p * (gp - r)).astype(BF16) for p, (_, gp), r in zip(ps, pairs, inner)]
            for (i, h), p, g in zip(group, ps, gs):
                cols = slice(i * seq_len, (i + 1) * seq_len)
                rq, rk, rv = [slice(j * width + h * HD, j * width + (h + 1) * HD) for j in range(3)]
                go = gsc[0, h * HD : (h + 1) * HD, cols]
                dproj[rq, cols] = (dot(proj[0, rk, cols], g, 1, 0) * scale).astype(BF16)
                dproj[rk, cols] = (dot(proj[0, rq, cols], g, 1, 1) * scale).astype(BF16)
                dproj[rv, cols] = dot(go, p.astype(BF16), 1, 1).astype(BF16)
            pairs = later

    @pl.when(block < short_blocks)
    def _():
        run(LS, lens_s, block * (span // LS), 4)

    @pl.when(block >= short_blocks)
    def _():
        run(LL, lens_l, (block - short_blocks) * (span // LL), 1)

    gin[...] = dot(w[...], dproj[...], 1, 0) + gsc[1].astype(F32)
    part = dot(dproj[...], x[...], 1, 1)
    sums = dot(jnp.ones((8, span), BF16), dproj[...], 1, 1)

    @pl.when(step == 0)
    def _():
        if first_call:
            acc[...] = part
            bias[...] = sums
        else:
            acc[...] = acc_in[...] + part
            bias[...] = bias_in[...] + sums

    @pl.when(step > 0)
    def _():
        acc[...] += part
        bias[...] += sums

    if split == 1:

        @pl.when(step == count - 1)
        def _():
            rows = out.shape[1]
            for d in range(out.shape[0]):
                out[d] = acc[d * rows : (d + 1) * rows, :].astype(BF16)

    if split == 2:

        @pl.when(step == count - 1)
        def _():
            pairs, rows = keep.shape[:2]
            mine = parity[0]
            for d in range(pairs):
                a = pl.ds(pl.multiple_of((2 * d + mine) * rows, 8), rows)
                c = pl.ds(pl.multiple_of((2 * d + 1 - mine) * rows, 8), rows)
                keep[d] = acc[a, :].astype(BF16)
                send[d] = acc[c, :].astype(BF16)
            total = jnp.concatenate(
                [bias[:, i * width : (i + 1) * width] for i in range(3)], axis=0
            )
            extra[...] = total
            high = total.astype(BF16)
            send[pairs, :24] = high
            send[pairs, 24:48] = (total - high.astype(F32)).astype(BF16)


def attn_bwd(
    first, count, me, parity, lens_s, lens_l, x, w, proj, lse, g, carry, dp_count, split
):
    width, tokens = x.shape
    span = tokens // 8
    heads = width // HD
    short_blocks = lens_s.shape[0] * LS // span
    fixed = lambda k, *_: (0, 0)
    fixed3 = lambda k, *_: (0, 0, 0)
    here = lambda k, me, *_: (0, slot_block(me, first + k))
    slot = lambda k, *_: (first + k, 0, 0)
    first_call = carry is None
    acc_spec = pl.BlockSpec((3 * width, width), fixed)
    bias_spec = pl.BlockSpec((8, 3 * width), fixed)
    acc_shape = jax.ShapeDtypeStruct((3 * width, width), F32)
    bias_shape = jax.ShapeDtypeStruct((8, 3 * width), F32)
    mine = g[first : first + count]
    in_specs = [
        pl.BlockSpec((width, span), here),
        pl.BlockSpec(w.shape, fixed),
        pl.BlockSpec((1, 3 * width, span), slot),
        pl.BlockSpec((1, heads, span), slot),
    ] + [pl.BlockSpec((2, width, span), fixed3)] * len(mine)
    args = [x, w, proj, lse, *mine]
    aliases = {}
    if not first_call:
        gin, acc, bias = carry
        in_specs += [acc_spec, bias_spec, pl.BlockSpec(memory_space=pl.ANY)]
        args += [acc, bias, gin]
        aliases = {4 + len(args) - 1: 0}
    rows = 3 * width // dp_count
    scratch = []
    if split == 0:
        tail = [(acc_spec, acc_shape), (bias_spec, bias_shape)]
    elif split == 1:
        shape = (dp_count, rows, width)
        tail = [
            (pl.BlockSpec(shape, fixed3), jax.ShapeDtypeStruct(shape, BF16)),
            (bias_spec, bias_shape),
        ]
        scratch = [pltpu.VMEM(acc_shape.shape, F32)]
    else:
        keep = (dp_count // 2, rows, width)
        send = (dp_count // 2 + 1, rows, width)
        tail = [
            (pl.BlockSpec(keep, fixed3), jax.ShapeDtypeStruct(keep, BF16)),
            (pl.BlockSpec(send, fixed3), jax.ShapeDtypeStruct(send, BF16)),
            (pl.BlockSpec((24, width), fixed), jax.ShapeDtypeStruct((24, width), F32)),
        ]
        scratch = [pltpu.VMEM(bias_shape.shape, F32), pltpu.VMEM(acc_shape.shape, F32)]
    return pl.pallas_call(
        functools.partial(
            attn_bwd_kernel, first, count, heads, short_blocks, first_call, split
        ),
        grid_spec=pltpu.PrefetchScalarGridSpec(
            num_scalar_prefetch=4,
            grid=(count,),
            in_specs=in_specs,
            out_specs=[pl.BlockSpec((width, span), here)] + [t[0] for t in tail],
            scratch_shapes=[
                pltpu.VMEM((3 * width, span), BF16),
                pltpu.VMEM((2, width, span), BF16),
                pltpu.VMEM((heads, 2 * HD + 16, span), BF16),
                pltpu.VMEM((heads, 2 * HD + 16, span), BF16),
            ]
            + scratch,
        ),
        out_shape=[jax.ShapeDtypeStruct((width, tokens), F32)] + [t[1] for t in tail],
        input_output_aliases=aliases,
        cost_estimate=COST(4.0 * count),
        compiler_params=pltpu.CompilerParams(vmem_limit_bytes=VMEM_LIMIT),
        name=f"attn_bwd{first}",
    )(me, parity, lens_s, lens_l, *args)


def prep_kernel(w0, w1, w2, w3, *refs):
    params = refs[:6]
    owt, upt, dnt, upn, dnn, ub, cols, ow = refs[6:]
    weights = (w0, w1, w2, w3)
    model = owt.shape[0]
    width = model // 4

    def eye(n):
        a = lax.broadcasted_iota(jnp.int32, (n, n), 0)
        b = lax.broadcasted_iota(jnp.int32, (n, n), 1)
        return jnp.where(a == b, 1.0, 0.0).astype(BF16)

    big, small = eye(256), eye(width)
    for k, w in enumerate(weights):
        ks = slice(k * width, (k + 1) * width)
        ow[ks, :] = w[:width, :]
        for at in range(0, model, 256):
            lanes = slice(at, at + 256)
            for ref, first in ((upt, width), (dnt, 2 * width)):
                t = dot(big, w[first : first + width, lanes], 1, 1).astype(BF16)
                for g in range(4):
                    low, high = max(at, g * width), min(at + 256, (g + 1) * width)
                    if low < high:
                        start = k * width + low - g * width
                        ref[g, start : start + high - low, :] = t[low - at : high - at, :]
        bt = w[3 * width :, :].astype(F32).T
        ub[:, k : k + 1] = (bt[:, 2:3] + bt[:, 1:2]) + bt[:, 0:1]

    @pl.loop(0, model // 256)
    def _(i):
        at = pl.ds(pl.multiple_of(i * 256, 256), 256)
        owt[at, :] = dot(big, ow[:, at], 1, 1).astype(BF16)

    @pl.loop(0, 4)
    def _(g):
        upn[g] = dot(small, upt[g], 1, 1).astype(BF16)
        dnn[g] = dot(small, dnt[g], 1, 1).astype(BF16)

    for j, p in enumerate(params):
        cols[:, j : j + 1] = jnp.broadcast_to(p[...].reshape(1, model), (8, model)).T[:, 0:1]


def prep(weights, params):
    model = weights[0].shape[1]
    width = model // 4
    vmem = pl.BlockSpec(memory_space=pltpu.VMEM)
    shapes = [
        jax.ShapeDtypeStruct((model, model), BF16),
        jax.ShapeDtypeStruct((4, model, width), BF16),
        jax.ShapeDtypeStruct((4, model, width), BF16),
        jax.ShapeDtypeStruct((4, width, model), BF16),
        jax.ShapeDtypeStruct((4, width, model), BF16),
        jax.ShapeDtypeStruct((model, 8), F32),
        jax.ShapeDtypeStruct((model, 8), F32),
        jax.ShapeDtypeStruct((model, model), BF16),
    ]
    return pl.pallas_call(
        prep_kernel,
        in_specs=[vmem] * 10,
        out_specs=[vmem] * len(shapes),
        out_shape=shapes,
        cost_estimate=COST(4.0),
        compiler_params=pltpu.CompilerParams(vmem_limit_bytes=VMEM_LIMIT),
        name="prep",
    )(*weights, *params)


def mid_kernel(half, width, blocks, me, *refs):
    ctx, hid = refs[0:4], refs[4:8]
    og, ub, cols = refs[8:11]
    given = refs[11:17]
    at = 17
    if half:
        acc_hbm, vec_in = refs[at : at + 3], refs[at + 3]
        at += 5
    lo = refs[at]
    back = refs[at + 1 : at + 5]
    at += 5
    if half:
        keep, send, vec_out = refs[at : at + 3]
        at += 3
    else:
        acc_hbm, vec = refs[at : at + 3], refs[at + 3]
        at += 4
    (gow, gup, gdn, owt, upt, dnt, upn, dnn, ow) = refs[at : at + 9]
    at += 9
    (sums, act, slope, first, n1s, gps_s, cats, lows, sem, acc_sem) = refs[at : at + 10]
    if half:
        vec = refs[at + 10]
    accs = (gow, gup, gdn)
    step = pl.program_id(0)
    last = pl.num_programs(0) - 1
    model = 4 * width
    inv = 1.0 / model
    held = (owt, upt, dnn, dnt, upn, ow)

    def own(k):
        return pl.ds(pl.multiple_of(lax.bitwise_xor(me[0], k) * width, width), width)

    def fetch(i):
        return pltpu.make_async_copy(given[i], held[i], sem.at[i])

    def ready(i):
        @pl.when(step == 0)
        def _():
            fetch(i).wait()

    def acc_copy(i):
        if half:
            return pltpu.make_async_copy(acc_hbm[i], accs[i], acc_sem.at[i])
        return pltpu.make_async_copy(accs[i], acc_hbm[i], acc_sem.at[i])

    @pl.when(step == 0)
    def _():
        for i in range(6):
            fetch(i).start()
        if half:
            for i in range(3):
                acc_copy(i).start()
        row = lax.broadcasted_iota(jnp.int32, (16, TILE), 0)
        for g in range(4):
            lows[g, width:, :] = jnp.where(row == 0, 1.0, 0.0).astype(BF16)
        sums[...] = jnp.zeros_like(sums)

    def before(value):
        return value if half else jnp.where(step == 0, 0.0, value)

    def acc_ready(i):
        if half:

            @pl.when(step == 0)
            def _():
                acc_copy(i).wait()

    def acc_done(i):
        if not half:

            @pl.when(step == last)
            def _():
                acc_copy(i).start()

    def col(j):
        return cols[:, j : j + 1]

    def add_sum(j, value):
        sums[j] += sum(value[:, i : i + 128] for i in range(0, TILE, 128))

    for k in range(4):
        cats[k * width : (k + 1) * width, :] = ctx[k][0]
    ready(0)
    first[...] = dot(owt[...], cats[...], 1, 0) + col(0)
    for k in range(4):
        first[own(k), :] += hid[k][...].reshape(width, TILE).astype(F32)
    pre = first[...]
    cen = pre - jnp.sum(pre, axis=0, keepdims=True) * inv
    r1 = lax.rsqrt(jnp.sum(cen * cen, axis=0, keepdims=True) * inv + EPSILON)
    n1 = cen * r1
    n1s[...] = n1
    normed = n1 * col(1) + col(2)
    first[...] = normed
    low = normed.astype(BF16)
    for g in range(4):
        lows[g, :width, :] = low[g * width : (g + 1) * width, :]
    ready(1)
    ready(2)

    def pre_act(g):
        return dot(upt[g], lows[g, :width, :], 1, 0)

    later = pre_act(0)
    for g in range(4):
        rows = slice(g * width, (g + 1) * width)
        raw = later
        if g < 3:
            later = pre_act(g + 1)
        for k in range(4):
            units = slice(k * width, (k + 1) * width)
            pa = raw[units, :] + ub[rows, k : k + 1]
            phi, sl = gelu_parts(pa)
            act[g, units, :] = (pa * phi).astype(BF16)
            slope[g, units, :] = sl
        first[rows, :] += dot(dnn[g], act[g], 1, 0) + cols[rows, 3:4]
    pre = first[...]
    cen = pre - jnp.sum(pre, axis=0, keepdims=True) * inv
    r2 = lax.rsqrt(jnp.sum(cen * cen, axis=0, keepdims=True) * inv + EPSILON)
    n2 = cen * r2
    lo[...] = (n2 * col(4) + col(5)).astype(BF16).T
    ogt = og[...].T.astype(F32)
    add_sum(4, ogt * n2)
    add_sum(5, ogt)
    u = ogt * col(4)
    gps = r2 * (
        u
        - jnp.sum(u, axis=0, keepdims=True) * inv
        - n2 * (jnp.sum(u * n2, axis=0, keepdims=True) * inv)
    )
    add_sum(3, gps)
    gdl = gps.astype(BF16)
    gps_s[...] = gps
    ready(3)
    ready(4)
    acc_ready(1)
    acc_ready(2)

    def grad_act(g):
        return dot(dnt[g], gdl[g * width : (g + 1) * width, :], 1, 0)

    later = grad_act(0)
    for g in range(4):
        rows = slice(g * width, (g + 1) * width)
        raw = later
        if g < 3:
            later = grad_act(g + 1)
        gdn[g] = before(gdn[g]) + dot(act[g], gdl[rows, :], 1, 1)
        gpa = (raw * slope[g]).astype(BF16)
        gup[g] = before(gup[g]) + dot(gpa, lows[g], 1, 1)
        gps_s[rows, :] += dot(upn[g], gpa, 1, 0)
    acc_done(1)
    acc_done(2)
    gn = gps_s[...]
    n1 = n1s[...]
    add_sum(1, gn * n1)
    add_sum(2, gn)
    u = gn * col(1)
    gpf = r1 * (
        u
        - jnp.sum(u, axis=0, keepdims=True) * inv
        - n1 * (jnp.sum(u * n1, axis=0, keepdims=True) * inv)
    )
    gpl = gpf.astype(BF16)
    first[...] = gpl.astype(F32)
    add_sum(0, first[...])
    ready(5)
    acc_ready(0)
    gow[...] = before(gow[...]) + dot(gpl, cats[...], 1, 1)
    acc_done(0)
    for k in range(4):
        back[k][1] = first[own(k), :].astype(BF16)
        back[k][0] = dot(ow[k * width : (k + 1) * width, :], gpl, 1, 0).astype(BF16)

    @pl.when(step == last)
    def _():
        lane = lax.broadcasted_iota(jnp.int32, (1, 128), 1)
        total = vec_in[...] if half else jnp.zeros((model, 128), F32)
        for j in range(6):
            total += jnp.where(lane == j, jnp.sum(sums[j], axis=1, keepdims=True), 0.0)
        vec[...] = total
        if half:
            for g in range(4):
                for k in range(4):
                    vec[own(k), :] += jnp.where(
                        lane == 6 + g, gup[g, k * width : (k + 1) * width, width : width + 1], 0.0
                    )
            more = vec[...].T[:16]
            vec_out[...] = more
            part = width // blocks

            @pl.loop(0, 2)
            def _(far):
                for near in range(2):
                    dest = send if near else keep
                    units = pl.ds(pl.multiple_of((2 * far + near) * width, 8), width)
                    up_rows = pl.ds(pl.multiple_of(far * 3 * width, 16), width)
                    down_rows = pl.ds(pl.multiple_of((far * 3 + 1) * width, 16), width)
                    for g in range(4):
                        lanes = slice(g * width, (g + 1) * width)
                        dest[up_rows, lanes] = gup[g, units, :width].T.astype(BF16)
                        dest[down_rows, lanes] = gdn[g, units, :].T.astype(BF16)

            pairs = 2 if blocks > 1 else 1

            @pl.loop(0, blocks // pairs)
            def _(pair):
                for k in range(4):
                    dest = send if k % 2 else keep
                    base = ((k // 2) * 3 + 2) * width
                    units = slice(k * width, (k + 1) * width)
                    to = pl.ds(pl.multiple_of(base + pair * pairs * part, 16), pairs * part)
                    for g in range(4):
                        lanes = slice(g * width, (g + 1) * width)
                        rows = []
                        for i in range(pairs):
                            start = ((pair * pairs + i) * 4 + g) * part
                            rows.append(gow[pl.ds(pl.multiple_of(start, 8), part), units])
                        dest[to, lanes] = jnp.concatenate(rows, axis=0).astype(BF16)

            if blocks > 1:
                high = more.astype(BF16)
                send[6 * width : 6 * width + 16, :] = high
                send[6 * width + part : 6 * width + part + 16, :] = (
                    more - high.astype(F32)
                ).astype(BF16)
        else:
            for i in range(3):
                acc_copy(i).wait()


def mid(half, me, ctx, hid, og, ready, carry, blocks):
    width, span = ctx[0].shape[1:]
    model = 4 * width
    steps = span // TILE
    whole2 = lambda i, *_: (0, 0)
    ctx_tile = pl.BlockSpec((1, width, TILE), lambda i, *_: (0, 0, i))
    hid_own = pl.BlockSpec((width, TILE), lambda i, me: (0, (me[0] * 2 + half) * steps + i))
    hid_tile = pl.BlockSpec((1, width, TILE), lambda i, *_: (1, 0, i))
    back_tile = pl.BlockSpec((2, width, TILE), lambda i, *_: (0, 0, i))
    row_in = pl.BlockSpec((TILE, model), lambda i, *_: (half * steps + i, 0))
    hbm = pl.BlockSpec(memory_space=pl.ANY)
    column = pl.BlockSpec((model, 8), whole2)
    vec_spec = pl.BlockSpec((model, 128), whole2)
    owt, upt, dnt, upn, dnn, ub, cols, ow = ready
    in_specs = [ctx_tile] * 4 + [hid_own] + [hid_tile] * 3 + [row_in, column, column] + [hbm] * 6
    args = [*ctx, *hid, og, ub, cols, owt, upt, dnn, dnt, upn, ow]
    accs = [(model, model), (4, model, width + 16), (4, model, width)]
    piece = jax.ShapeDtypeStruct((2, width, span), BF16)
    scratch = [pltpu.VMEM(a, F32) for a in accs] + [
        pltpu.VMEM((model, model), BF16),
        pltpu.VMEM((4, model, width), BF16),
        pltpu.VMEM((4, model, width), BF16),
        pltpu.VMEM((4, width, model), BF16),
        pltpu.VMEM((4, width, model), BF16),
        pltpu.VMEM((model, model), BF16),
        pltpu.VMEM((6, model, 128), F32),
        pltpu.VMEM((4, model, TILE), BF16),
        pltpu.VMEM((4, model, TILE), F32),
        pltpu.VMEM((model, TILE), F32),
        pltpu.VMEM((model, TILE), F32),
        pltpu.VMEM((model, TILE), F32),
        pltpu.VMEM((model, TILE), BF16),
        pltpu.VMEM((4, width + 16, TILE), BF16),
        pltpu.SemaphoreType.DMA((6,)),
        pltpu.SemaphoreType.DMA((3,)),
    ]
    aliases = {}
    if half:
        in_specs += [hbm] * 3 + [vec_spec, hbm]
        aliases = {len(args) + 5: 0}
        args += list(carry)
        extra = 2 * (width // blocks) if blocks > 1 else 0
        rows = [6 * width, 6 * width + extra]
        tail_specs = [pl.BlockSpec((r, model), whole2) for r in rows + [16]]
        tail_shapes = [jax.ShapeDtypeStruct((r, model), BF16) for r in rows]
        tail_shapes += [jax.ShapeDtypeStruct((16, model), F32)]
        scratch += [pltpu.VMEM((model, 128), F32)]
    else:
        tail_specs = [hbm] * 3 + [vec_spec]
        tail_shapes = [jax.ShapeDtypeStruct(a, F32) for a in accs + [(model, 128)]]
    return pl.pallas_call(
        functools.partial(mid_kernel, half, width, blocks),
        grid_spec=pltpu.PrefetchScalarGridSpec(
            num_scalar_prefetch=1,
            grid=(steps,),
            in_specs=in_specs,
            out_specs=[row_in] + [back_tile] * 4
            + tail_specs,
            scratch_shapes=scratch,
        ),
        out_shape=[jax.ShapeDtypeStruct((2 * span, model), BF16)] + [piece] * 4 + tail_shapes,
        input_output_aliases=aliases,
        cost_estimate=COST(25.0),
        compiler_params=pltpu.CompilerParams(vmem_limit_bytes=VMEM_LIMIT),
        name=f"mid{half}",
    )(me, *args)


def combine_kernel(size, outer, inner, index, keep, recv, extra, kept, sent, extra_out):
    rows = extra.shape[0]
    more = extra[...] + (recv[size, :rows].astype(F32) + recv[size + 1, :rows].astype(F32))
    extra_out[...] = more
    hi = more.astype(BF16)
    sent[size // 2, :rows] = hi
    sent[size // 2 + 1, :rows] = (more - hi.astype(F32)).astype(BF16)
    mine = index[0]
    for o in range(outer):
        a = pl.ds((o * 2 + mine) * inner, inner)
        b = pl.ds((o * 2 + 1 - mine) * inner, inner)
        c = slice(o * inner, (o + 1) * inner)
        kept[c] = (keep[a].astype(F32) + recv[a].astype(F32)).astype(BF16)
        sent[c] = (keep[b].astype(F32) + recv[b].astype(F32)).astype(BF16)


def combine(index, keep, recv, extra, outer, inner, name):
    size, rows, lanes = keep.shape
    vmem = pl.BlockSpec(memory_space=pltpu.VMEM)
    shapes = [
        jax.ShapeDtypeStruct((size // 2, rows, lanes), BF16),
        jax.ShapeDtypeStruct((size // 2 + 2, rows, lanes), BF16),
        jax.ShapeDtypeStruct(extra.shape, F32),
    ]
    return pl.pallas_call(
        functools.partial(combine_kernel, size, outer, inner),
        in_specs=[pl.BlockSpec(memory_space=pltpu.SMEM)] + [vmem] * 3,
        out_specs=[vmem] * len(shapes),
        out_shape=shapes,
        cost_estimate=COST(1.0),
        compiler_params=pltpu.CompilerParams(vmem_limit_bytes=VMEM_LIMIT),
        name=name,
    )(index, keep, recv, extra)


def pulled(kernel, count, index, *refs):
    bufs, sem = refs[-count - 1 : -1], refs[-1]
    copies = [pltpu.make_async_copy(refs[i], bufs[i], sem.at[i]) for i in range(count)]
    for c in copies:
        c.start()
    for c in copies:
        c.wait()
    kernel(index, *bufs, *refs[count : -count - 1])


def pull_call(kernel, count, index, args, shapes, name):
    vmem = pl.BlockSpec(memory_space=pltpu.VMEM)
    return pl.pallas_call(
        functools.partial(pulled, kernel, count),
        in_specs=[pl.BlockSpec(memory_space=pltpu.SMEM)]
        + [pl.BlockSpec(memory_space=pltpu.HBM)] * count
        + [vmem] * (len(args) - count),
        out_specs=[vmem] * len(shapes),
        out_shape=shapes,
        scratch_shapes=[pltpu.VMEM(a.shape, a.dtype) for a in args[:count]]
        + [pltpu.SemaphoreType.DMA((count,))],
        cost_estimate=COST(1.0),
        compiler_params=pltpu.CompilerParams(vmem_limit_bytes=VMEM_SMALL),
        name=name,
    )(index, *args)


def combine_early(index, keep, recv, extra, name):
    size, rows, lanes = keep.shape
    shapes = [
        jax.ShapeDtypeStruct((size // 2, rows, lanes), BF16),
        jax.ShapeDtypeStruct((size // 2 + 2, rows, lanes), BF16),
        jax.ShapeDtypeStruct(extra.shape, F32),
    ]
    kernel = functools.partial(combine_kernel, size, size // 2, 1)
    return pull_call(kernel, 3, index, [keep, recv, extra], shapes, name)


def qkv_kernel(index, qk, qb, qr, kept, sent, qb_out):
    size = qk.shape[0]
    more = qb[...] + (qr[size, :24].astype(F32) + qr[size, 24:48].astype(F32))
    qb_out[...] = more
    hi = more.astype(BF16)
    sent[size // 2, :24] = hi
    sent[size // 2, 24:48] = (more - hi.astype(F32)).astype(BF16)
    mine = index[0]
    for i in range(size // 2):
        a, b = 2 * i + mine, 2 * i + 1 - mine
        kept[i] = (qk[a].astype(F32) + qr[a].astype(F32)).astype(BF16)
        sent[i] = (qk[b].astype(F32) + qr[b].astype(F32)).astype(BF16)


def qkv_stage(index, qk, qb, qr, name):
    size, rows, lanes = qk.shape
    shapes = [
        jax.ShapeDtypeStruct((size // 2, rows, lanes), BF16),
        jax.ShapeDtypeStruct((size // 2 + 1, rows, lanes), BF16),
        jax.ShapeDtypeStruct(qb.shape, F32),
    ]
    return pull_call(qkv_kernel, 2, index, [qk, qb, qr], shapes, name)


def blend_kernel(joint, last, index, wk, wr, vec, qk, *refs):
    if not joint:
        qr, qb, refs = refs[0], refs[1], refs[2:]
    nw, rows, model = wk.shape
    nq, width = qk.shape[0], qk.shape[2]
    pitch = model // 3
    if joint:
        terms = wr[nw].astype(F32)
        more = vec[:12] + (terms[:12] + terms[12:24])
    else:
        more = vec[:12] + (wr[nw, :16].astype(F32) + wr[nw + 1, :16].astype(F32))[:12]
        bias = qb[...] + (qr[nq, :24].astype(F32) + qr[nq, 24:48].astype(F32))

    def wsum(i):
        return wk[i].astype(F32) + wr[i].astype(F32)

    def qsum(i, j):
        part = slice(j * rows, (j + 1) * rows)
        if joint:
            other = wr[nw + 1 + i, :, j * pitch : j * pitch + width]
        else:
            other = qr[i, part, :]
        return qk[i, part, :].astype(F32) + other.astype(F32)

    if last:
        gup, gdn, gow, gqkv, gqv, gub = refs[:6]
        vecs = refs[6:]
        gup[...] = wsum(0)
        gdn[...] = wsum(1)
        ow = wsum(2)
        quarter = model // 4
        gow[...] = jnp.concatenate(
            [ow[:, j * quarter : (j + 1) * quarter] for j in range(4)], axis=0
        ).T
        for j in range(3):
            gqkv[j * rows : (j + 1) * rows, :] = qsum(0, j)
        gqv[:, :width] = more[10:11, :width]
        gqv[:, width:] = more[10:11, 2 * pitch : 2 * pitch + width]
        own = vecs[0].shape[0]
        more = jnp.concatenate([more, jnp.zeros((4, model), F32)], axis=0)
        here = pltpu.roll(more, index[1], 1)
        for j, v in enumerate(vecs):
            v[...] = here[j, :own]
        here = pltpu.roll(more, index[2], 1)
        gub[...] = jnp.concatenate([here[6 + j, :quarter] for j in range(4)])
        return
    wkept, sent, vec_out, qkept = refs
    mine = index[0]
    vec_out[:12] = more
    vec_out[12:] = jnp.zeros((4, model), F32)
    if not joint:
        for j in range(3):
            vec_out[10:11, j * pitch : j * pitch + width] = bias[8 * j : 8 * j + 1]
    half = nw // 2
    more = vec_out[:12]
    hi = more.astype(BF16).astype(F32)
    sent[half, :24] = jnp.concatenate([hi, more - hi], axis=0).astype(BF16)
    for i in range(half):
        wkept[i] = wsum(2 * i + mine).astype(BF16)
        sent[i] = wsum(2 * i + 1 - mine).astype(BF16)
    at = half + 1
    for i in range(nq // 2):
        for j in range(3):
            qkept[i, j * rows : (j + 1) * rows, :] = qsum(2 * i + mine, j).astype(BF16)
            sent[at + i, :, j * pitch : j * pitch + width] = qsum(2 * i + 1 - mine, j).astype(BF16)


def blend(index, wk, wr, vec, qk, qr, qb, last, name):
    nw, rows, model = wk.shape
    nq, _, width = qk.shape
    vmem = pl.BlockSpec(memory_space=pltpu.VMEM)
    args = [wk, wr, vec, qk] + ([] if qr is None else [qr, qb])
    shape = jax.ShapeDtypeStruct
    if last:
        quarter = model // 4
        shapes = [
            shape((rows, model), F32),
            shape((rows, model), F32),
            shape((quarter, 4 * rows), F32),
            shape((3 * rows, width), F32),
            shape((1, 2 * width), F32),
            shape((model,), F32),
        ] + [shape((rows,), F32)] * 6
    else:
        shapes = [
            shape((nw // 2, rows, model), BF16),
            shape((nw // 2 + nq // 2 + 1, rows, model), BF16),
            shape(vec.shape, F32),
            shape((nq // 2, 3 * rows, width), BF16),
        ]
    return pl.pallas_call(
        functools.partial(blend_kernel, qr is None, last),
        in_specs=[pl.BlockSpec(memory_space=pltpu.SMEM)] + [vmem] * len(args),
        out_specs=[vmem] * len(shapes),
        out_shape=shapes,
        cost_estimate=COST(1.0),
        compiler_params=pltpu.CompilerParams(vmem_limit_bytes=VMEM_SMALL),
        name=name,
    )(index, *args)


def swap(value, axis, bit):
    count = lax.axis_size(axis)
    return lax.ppermute(value, axis, [(i, i ^ bit) for i in range(count)])


def to_chan(pieces):
    return [pieces[0]] + [swap(pieces[k], "chan", k) for k in range(1, 4)]


def gather_chan(value):
    near = swap(value, "chan", 1)
    far = swap(value, "chan", 2)
    return [value, near, far, swap(far, "chan", 1)]


def scatter_dp(pieces):
    index = lax.axis_index("dp")
    count, bit = pieces.shape[0], 1
    while count > 1:
        view = pieces.reshape((count // 2, 2) + pieces.shape[1:])
        digit = (index // bit) % 2
        mine = lax.dynamic_index_in_dim(view, digit, 1, keepdims=False).astype(F32)
        other = lax.dynamic_index_in_dim(view, 1 - digit, 1, keepdims=False)
        total = mine + swap(other, "dp", bit).astype(F32)
        count, bit = count // 2, bit * 2
        pieces = total if count == 1 else total.astype(pieces.dtype)
    return pieces[0]


def sum_dp(value):
    bit = 1
    while bit < lax.axis_size("dp"):
        value = value + swap(value, "dp", bit)
        bit *= 2
    return value


def pack_kernel(ow, up, dn, ub, weights):
    width = ow.shape[0]
    for i, w in enumerate((ow, up, dn)):
        weights[i * width : (i + 1) * width, :] = w[...]
    whole = jnp.broadcast_to(ub[...].reshape(1, -1), (16, ub.shape[0]))
    high = whole.astype(BF16)
    rest = whole - high.astype(F32)
    middle = rest.astype(BF16)
    low = (rest - middle.astype(F32)).astype(BF16)
    row = lax.broadcasted_iota(jnp.int32, whole.shape, 0)
    terms = jnp.where(
        row == 0,
        high.astype(F32),
        jnp.where(row == 1, middle.astype(F32), low.astype(F32)),
    )
    weights[3 * width :, :] = terms.astype(BF16)


def pack(ow, up, dn, ub):
    width, model = ow.shape
    vmem = pl.BlockSpec(memory_space=pltpu.VMEM)
    return pl.pallas_call(
        pack_kernel,
        in_specs=[vmem] * 4,
        out_specs=vmem,
        out_shape=jax.ShapeDtypeStruct((3 * width + 16, model), BF16),
        cost_estimate=COST(1.0),
        compiler_params=pltpu.CompilerParams(vmem_limit_bytes=VMEM_LIMIT),
        name="pack",
    )(ow, up, dn, ub)


def digit(value, b):
    return ((value >> b) & 1)[None]


def reduce_plain(keep, send, vec, dp_count):
    width, model = keep.shape[0] // 6, keep.shape[1]
    sections = 3
    keep = keep.reshape(2, 3, width, model)
    send = send[: 6 * width].reshape(2, 3, width, model)
    rows = width // dp_count
    keep = keep + swap(send, "chan", 1)
    keep = keep[0] + swap(keep[1], "chan", 2)
    if rows < 16:
        last = keep[2].reshape(width, 4, width).transpose(1, 0, 2).reshape(width, model)
        last = last.reshape(dp_count, 4, rows, width).transpose(0, 2, 1, 3)
        keep = jnp.stack([keep[0], keep[1], last.reshape(width, model)])
    keep = keep.reshape(sections, dp_count, rows, model).transpose(1, 0, 2, 3)
    vec = vec + swap(vec, "chan", 1)
    vec = sum_dp(vec + swap(vec, "chan", 2))
    return scatter_dp(keep), vec


def on_device(
    hidden_in,
    lengths_short,
    lengths_long,
    qkv_weight,
    qv_bias,
    out_weight,
    mixer_bias,
    first_gain,
    first_shift,
    up_weight,
    up_bias,
    down_weight,
    down_bias,
    second_gain,
    second_shift,
    out_grad,
):
    width, tokens = hidden_in.shape
    span = tokens // 8
    model = 4 * width
    dp_count = lax.axis_size("dp")
    chan = lax.axis_index("chan").astype(jnp.int32)
    dp = lax.axis_index("dp").astype(jnp.int32)
    me = chan[None]
    bar = lax.optimization_barrier
    fine = width // dp_count >= 16 and dp_count >= 8
    lengths = (lengths_short, lengths_long)
    w = qkv_weight[0]

    packed = pack(out_weight, up_weight, down_weight, up_bias)
    params = [mixer_bias, first_gain, first_shift, down_bias, second_gain, second_shift]
    far = swap(packed, "chan", 2)
    near = swap(packed, "chan", 1)
    x, _ = bar((hidden_in, packed))
    proj, *parts, lse = attn_fwd(me, *lengths, x, w, qv_bias)
    parts = [parts[:4], parts[4:]]
    far, near, parts = bar((far, near, parts))
    first = to_chan(parts[0])
    weights = [packed, near, far, swap(far, "chan", 1)]
    ready = prep(weights, params)
    second = to_chan(parts[1])
    blocks = dp_count if fine else 1
    hid = [hidden_in] + first[1:]
    lo, *rest = mid(0, me, first, hid, out_grad, ready, None, blocks)
    g0, carry = rest[:4], [*rest[4:], lo]
    g0, carry, second = bar((g0, carry, second))
    back0 = to_chan(g0)
    hid = [hidden_in] + second[1:]
    lo, *rest = mid(1, me, second, hid, out_grad, ready, carry, blocks)
    rest, back0 = bar((rest, back0))
    g1, (keep, send, vec) = rest[:4], rest[4:]
    recv = swap(send, "chan", 1)
    back = [*back0, *to_chan(g1)]
    parity = digit(dp, 0)

    def backward(start, count, x, carry, split):
        return attn_bwd(
            start,
            count,
            me,
            parity,
            *lengths,
            x,
            w,
            proj,
            lse,
            back,
            carry,
            dp_count,
            split,
        )

    if not fine:
        sums, vec = reduce_plain(keep, send, vec, dp_count)
        carry = backward(0, 5, hidden_in, None, 0)
        grad_input, gq, gbias = backward(5, 3, hidden_in, carry, 1)
        gq, gbias = scatter_dp(gq), sum_dp(gbias[0])
        own = width // dp_count
        mine = lax.dynamic_slice_in_dim(vec[:6], (dp * 4 + chan) * own, own, 1)
        mine = [mine[i] for i in range(6)]
        gub = lax.dynamic_slice_in_dim(vec[6:10], chan * width, width, 1).reshape(model)
        gup, gdn = sums[0], sums[1]
        gow = sums[2].reshape(-1, 4, width).transpose(1, 0, 2).reshape(model // dp_count, width).T
        gqv = jnp.concatenate([gbias[:width], gbias[2 * width :]])[None]
    else:
        rows = width // dp_count
        size = 6 * dp_count
        zero = jnp.zeros((1,), jnp.int32)
        recv = recv.reshape(size + 2, rows, model)
        keep = keep.reshape(size, rows, model)

        def stage(index, recv, chan_next, name):
            size = keep.shape[0]
            outer, inner = (1, size // 2) if chan_next else (size // 2, 1)
            return combine(index, keep, recv, vec, outer, inner, name)

        keep, send, vec = stage(parity, recv, False, "combine0")
        recv = swap(send, "dp", 1)
        x, keep = bar((hidden_in, keep))
        carry = backward(0, 5, x, None, 0)
        recv, carry = bar((recv, carry))
        keep, send, vec = stage(zero, recv, True, "combine1")
        recv = swap(send, "chan", 2)
        x, keep = bar((x, keep))
        grad_input, gk, gs, gbias = backward(5, 3, x, carry, 2)
        recv, gk, gs = bar((recv, gk, gs))
        grecv = swap(gs, "dp", 1)
        second = digit(dp, 1)
        keep, send, vec = combine_early(second, keep, recv, vec, "combine2")
        recv = swap(send, "dp", 2)
        grecv, keep = bar((grecv, keep))
        gk, gs, gbias = qkv_stage(second, gk, gbias, grecv, "qkv2")
        grecv = swap(gs, "dp", 2)
        recv, gk = bar((recv, gk))
        b = 2
        while b < dp_count.bit_length() - 1:
            keep, send, vec, gk = blend(
                digit(dp, b), keep, recv, vec, gk, grecv, gbias, False, f"blend{b}"
            )
            recv, grecv = swap(send, "dp", 1 << b), None
            b += 1
        index = jnp.stack(
            [
                jnp.zeros_like(dp),
                (model - (dp * 4 + chan) * rows) % model,
                (model - chan * width) % model,
            ]
        )
        gup, gdn, gow, gq, gqv, gub, *mine = blend(
            index, keep, recv, vec, gk, grecv, gbias, True, "blend"
        )
    return (
        lo,
        grad_input,
        gq.T[None],
        gqv,
        gow,
        mine[0],
        mine[1],
        mine[2],
        gup,
        gub,
        gdn,
        mine[3],
        mine[4],
        mine[5],
    )


def solution(mesh):
    in_specs = (
        P("chan", "dp"),
        P("dp"),
        P("dp"),
        P("chan", None, None),
        P("chan", None),
        P("chan", None),
        P(),
        P(),
        P(),
        P(None, "chan"),
        P("chan"),
        P(None, "chan"),
        P(),
        P(),
        P(),
        P(("dp", "chan"), None),
    )
    out_specs = (
        P(("dp", "chan"), None),
        P("chan", "dp"),
        P("chan", None, "dp"),
        P("chan", None),
        P("chan", "dp"),
        P(("dp", "chan")),
        P(("dp", "chan")),
        P(("dp", "chan")),
        P("dp", "chan"),
        P("chan"),
        P("dp", "chan"),
        P(("dp", "chan")),
        P(("dp", "chan")),
        P(("dp", "chan")),
    )
    return jax.shard_map(
        on_device, mesh=mesh, in_specs=in_specs, out_specs=out_specs, check_vma=False
    )
```

```python
import functools

import jax
import jax.numpy as jnp
from jax import lax
from jax.experimental import pallas as pl
from jax.experimental.pallas import tpu as pltpu
from jax.sharding import PartitionSpec as P

HD = 64
LS = 128
LL = 512
TILE = 256
EPSILON = 1e-06
LOG2E = 1.4426950408889634
F32 = jnp.float32
BF16 = jnp.bfloat16
VMEM_LIMIT = 67043328
VMEM_SMALL = 8388608


def COST(us):
    return pl.CostEstimate(
        flops=int(us * 1.0e9), bytes_accessed=int(us * 1.0e6), transcendentals=0
    )


def dot(a, b, ca, cb):
    return lax.dot_general(a, b, (((ca,), (cb,)), ((), ())), preferred_element_type=F32)


def gelu_parts(v):
    av = jnp.abs(v)
    t = 1.0 / (1.0 + (0.3275911 * 0.7071067811865476) * av)
    e = jnp.exp2((-0.5 * LOG2E) * (v * v))
    poly = t * (
        0.5 * 0.254829592
        + t
        * (
            0.5 * -0.284496736
            + t * (0.5 * 1.421413741 + t * (0.5 * -1.453152027 + t * (0.5 * 1.061405429)))
        )
    )
    tail = poly * e
    phi = jnp.where(v >= 0, 1.0 - tail, tail)
    return phi, phi + v * (0.3989422804014327 * e)


def score_operands(heads, span, seq_len, lens, first, q, key, qa, ka):
    width = heads * HD
    scaled = q.astype(F32) * (HD**-0.5 * LOG2E)
    high = scaled.astype(BF16)
    low = (scaled - high.astype(F32)).astype(BF16)
    pos = lax.broadcasted_iota(jnp.int32, (16, seq_len), 1)
    row = lax.broadcasted_iota(jnp.int32, (16, seq_len), 0)
    for h in range(heads):
        rows = slice(h * HD, (h + 1) * HD)
        qa[h, 0:HD, :] = high[rows]
        qa[h, HD : 2 * HD, :] = low[rows]
        ka[h, 0:HD, :] = key[rows]
        ka[h, HD : 2 * HD, :] = key[rows]
    for i in range(span // seq_len):
        bad = (row == 0) & (pos >= lens[first + i])
        mask = jnp.where(bad, -1e9, 0.0).astype(BF16)
        for h in range(heads):
            ka[h, 2 * HD :, i * seq_len : (i + 1) * seq_len] = mask


def one_rows(qa):
    row = lax.broadcasted_iota(jnp.int32, (16, qa.shape[2]), 0)
    ones = jnp.where(row == 0, 1.0, 0.0).astype(BF16)
    for h in range(qa.shape[0]):
        qa[h, 2 * HD :, :] = ones


def slot_block(me, s):
    return lax.bitwise_xor(me[0], lax.bitwise_and(s, 3)) * 2 + lax.shift_right_logical(s, 2)


def attn_fwd_kernel(heads, short_blocks, me, lens_s, lens_l, x, w, b, proj, *refs):
    outs = refs[:8]
    lse, scr, qa, ka, bcol = refs[8:]
    k = pl.program_id(0)
    block = slot_block(me, k)
    width = heads * HD
    span = x.shape[1]

    @pl.when(k == 0)
    def _():
        t = jnp.broadcast_to(b[...], (8, 2 * width)).T
        bcol[:width] = t[:width]
        bcol[width : 2 * width] = jnp.zeros((width, 8), F32)
        bcol[2 * width :] = t[width:]
        one_rows(qa)

    proj[0] = (dot(w[...], x[...], 0, 0) + bcol[:, 0:1]).astype(BF16)

    def run(seq_len, lens, first, together):
        score_operands(
            heads, span, seq_len, lens, first, proj[0, :width], proj[0, width : 2 * width], qa, ka
        )
        items = [(i, h) for i in range(span // seq_len) for h in range(heads)]
        groups = [items[n : n + together] for n in range(0, len(items), together)]

        def score(i, h):
            cols = slice(i * seq_len, (i + 1) * seq_len)
            return dot(ka[h, :, cols], qa[h, :, cols], 0, 0)

        scores = [score(*item) for item in groups[0]]
        for n, group in enumerate(groups):
            later = [score(*item) for item in groups[n + 1]] if n + 1 < len(groups) else None
            tops = [jnp.max(s, axis=0, keepdims=True) for s in scores]
            exps = [jnp.exp2(s - m) for s, m in zip(scores, tops)]
            sums = [jnp.sum(e, axis=0, keepdims=True) for e in exps]
            for (i, h), m, e, total in zip(group, tops, exps, sums):
                cols = slice(i * seq_len, (i + 1) * seq_len)
                val = proj[0, 2 * width + h * HD : 2 * width + (h + 1) * HD, cols]
                c = dot(val, e.astype(BF16), 1, 0) * (1.0 / total)
                scr[h * HD : (h + 1) * HD, cols] = c.astype(BF16)
                lse[0, h : h + 1, cols] = m + jnp.log2(total)
            scores = later

    @pl.when(block < short_blocks)
    def _():
        run(LS, lens_s, block * (span // LS), 6)

    @pl.when(block >= short_blocks)
    def _():
        run(LL, lens_l, (block - short_blocks) * (span // LL), 1)

    for i, out in enumerate(outs):

        @pl.when(k == i)
        def _():
            out[0] = scr[...]
            if i % 4:
                out[1] = x[...]


def attn_fwd(me, lens_s, lens_l, x, w, b):
    width, tokens = x.shape
    span = tokens // 8
    heads = width // HD
    short_blocks = lens_s.shape[0] * LS // span
    fixed = lambda k, *_: (0, 0)
    parts = [(2 if k % 4 else 1, width, span) for k in range(8)]
    return pl.pallas_call(
        functools.partial(attn_fwd_kernel, heads, short_blocks),
        grid_spec=pltpu.PrefetchScalarGridSpec(
            num_scalar_prefetch=3,
            grid=(8,),
            in_specs=[
                pl.BlockSpec((width, span), lambda k, me, *_: (0, slot_block(me, k))),
                pl.BlockSpec(w.shape, fixed),
                pl.BlockSpec(b.shape, fixed),
            ],
            out_specs=[
                pl.BlockSpec((1, 3 * width, span), lambda k, *_: (k, 0, 0)),
                *[pl.BlockSpec(part, lambda k, *_: (0, 0, 0)) for part in parts],
                pl.BlockSpec((1, heads, span), lambda k, *_: (k, 0, 0)),
            ],
            scratch_shapes=[
                pltpu.VMEM((width, span), BF16),
                pltpu.VMEM((heads, 2 * HD + 16, span), BF16),
                pltpu.VMEM((heads, 2 * HD + 16, span), BF16),
                pltpu.VMEM((3 * width, 8), F32),
            ],
        ),
        out_shape=[
            jax.ShapeDtypeStruct((8, 3 * width, span), BF16),
            *[jax.ShapeDtypeStruct(part, BF16) for part in parts],
            jax.ShapeDtypeStruct((8, heads, span), F32),
        ],
        cost_estimate=COST(16.0),
        compiler_params=pltpu.CompilerParams(vmem_limit_bytes=VMEM_LIMIT),
        name="attn_fwd",
    )(me, lens_s, lens_l, x, w, b)


def attn_bwd_kernel(first, count, heads, short_blocks, first_call, split, *refs):
    me, parity, lens_s, lens_l, x, w, proj, lse = refs[:8]
    gs = refs[8 : 8 + count]
    refs = refs[8 + count :]
    if not first_call:
        acc_in, bias_in = refs[:2]
        refs = refs[3:]
    gin = refs[0]
    if split == 0:
        acc, bias = refs[1:3]
        refs = refs[3:]
    elif split == 1:
        out, bias = refs[1:3]
        acc = refs[-1]
        refs = refs[3:-1]
    else:
        keep, send, extra = refs[1:4]
        bias, acc = refs[-2:]
        refs = refs[4:-2]
    dproj, gsc, qa, ka = refs
    step = pl.program_id(0)
    block = slot_block(me, first + step)
    width = heads * HD
    span = x.shape[1]
    scale = HD**-0.5

    @pl.when(step == 0)
    def _():
        one_rows(qa)

    for i, g in enumerate(gs):

        @pl.when(step == i)
        def _():
            gsc[...] = g[...]

    def run(seq_len, lens, first, together):
        score_operands(
            heads, span, seq_len, lens, first, proj[0, :width], proj[0, width : 2 * width], qa, ka
        )
        items = [(i, h) for i in range(span // seq_len) for h in range(heads)]
        groups = [items[n : n + together] for n in range(0, len(items), together)]

        def score(i, h):
            cols = slice(i * seq_len, (i + 1) * seq_len)
            val = proj[0, 2 * width + h * HD : 2 * width + (h + 1) * HD, cols]
            go = gsc[0, h * HD : (h + 1) * HD, cols]
            return dot(ka[h, :, cols], qa[h, :, cols], 0, 0), dot(val, go, 0, 0)

        pairs = [score(*item) for item in groups[0]]
        for n, group in enumerate(groups):
            later = [score(*item) for item in groups[n + 1]] if n + 1 < len(groups) else None
            ps = []
            for (i, h), (s, _) in zip(group, pairs):
                cols = slice(i * seq_len, (i + 1) * seq_len)
                ps.append(jnp.exp2(s - lse[0, h : h + 1, cols]))
            inner = [jnp.sum(p * gp, axis=0, keepdims=True) for p, (_, gp) in zip(ps, pairs)]
            gs = [(p * (gp - r)).astype(BF16) for p, (_, gp), r in zip(ps, pairs, inner)]
            for (i, h), p, g in zip(group, ps, gs):
                cols = slice(i * seq_len, (i + 1) * seq_len)
                rq, rk, rv = [slice(j * width + h * HD, j * width + (h + 1) * HD) for j in range(3)]
                go = gsc[0, h * HD : (h + 1) * HD, cols]
                dproj[rq, cols] = (dot(proj[0, rk, cols], g, 1, 0) * scale).astype(BF16)
                dproj[rk, cols] = (dot(proj[0, rq, cols], g, 1, 1) * scale).astype(BF16)
                dproj[rv, cols] = dot(go, p.astype(BF16), 1, 1).astype(BF16)
            pairs = later

    @pl.when(block < short_blocks)
    def _():
        run(LS, lens_s, block * (span // LS), 4)

    @pl.when(block >= short_blocks)
    def _():
        run(LL, lens_l, (block - short_blocks) * (span // LL), 1)

    gin[...] = dot(w[...], dproj[...], 1, 0) + gsc[1].astype(F32)
    part = dot(dproj[...], x[...], 1, 1)
    sums = dot(jnp.ones((8, span), BF16), dproj[...], 1, 1)

    @pl.when(step == 0)
    def _():
        if first_call:
            acc[...] = part
            bias[...] = sums
        else:
            acc[...] = acc_in[...] + part
            bias[...] = bias_in[...] + sums

    @pl.when(step > 0)
    def _():
        acc[...] += part
        bias[...] += sums

    if split == 1:

        @pl.when(step == count - 1)
        def _():
            rows = out.shape[1]
            for d in range(out.shape[0]):
                out[d] = acc[d * rows : (d + 1) * rows, :].astype(BF16)

    if split == 2:

        @pl.when(step == count - 1)
        def _():
            pairs, rows = keep.shape[:2]
            mine = parity[0]
            for d in range(pairs):
                a = pl.ds(pl.multiple_of((2 * d + mine) * rows, 8), rows)
                c = pl.ds(pl.multiple_of((2 * d + 1 - mine) * rows, 8), rows)
                keep[d] = acc[a, :].astype(BF16)
                send[d] = acc[c, :].astype(BF16)
            total = jnp.concatenate(
                [bias[:, i * width : (i + 1) * width] for i in range(3)], axis=0
            )
            extra[...] = total
            high = total.astype(BF16)
            send[pairs, :24] = high
            send[pairs, 24:48] = (total - high.astype(F32)).astype(BF16)


def attn_bwd(
    first, count, me, parity, lens_s, lens_l, x, w, proj, lse, g, carry, dp_count, split
):
    width, tokens = x.shape
    span = tokens // 8
    heads = width // HD
    short_blocks = lens_s.shape[0] * LS // span
    fixed = lambda k, *_: (0, 0)
    fixed3 = lambda k, *_: (0, 0, 0)
    here = lambda k, me, *_: (0, slot_block(me, first + k))
    slot = lambda k, *_: (first + k, 0, 0)
    first_call = carry is None
    acc_spec = pl.BlockSpec((3 * width, width), fixed)
    bias_spec = pl.BlockSpec((8, 3 * width), fixed)
    acc_shape = jax.ShapeDtypeStruct((3 * width, width), F32)
    bias_shape = jax.ShapeDtypeStruct((8, 3 * width), F32)
    mine = g[first : first + count]
    in_specs = [
        pl.BlockSpec((width, span), here),
        pl.BlockSpec(w.shape, fixed),
        pl.BlockSpec((1, 3 * width, span), slot),
        pl.BlockSpec((1, heads, span), slot),
    ] + [pl.BlockSpec((2, width, span), fixed3)] * len(mine)
    args = [x, w, proj, lse, *mine]
    aliases = {}
    if not first_call:
        gin, acc, bias = carry
        in_specs += [acc_spec, bias_spec, pl.BlockSpec(memory_space=pl.ANY)]
        args += [acc, bias, gin]
        aliases = {4 + len(args) - 1: 0}
    rows = 3 * width // dp_count
    scratch = []
    if split == 0:
        tail = [(acc_spec, acc_shape), (bias_spec, bias_shape)]
    elif split == 1:
        shape = (dp_count, rows, width)
        tail = [
            (pl.BlockSpec(shape, fixed3), jax.ShapeDtypeStruct(shape, BF16)),
            (bias_spec, bias_shape),
        ]
        scratch = [pltpu.VMEM(acc_shape.shape, F32)]
    else:
        keep = (dp_count // 2, rows, width)
        send = (dp_count // 2 + 1, rows, width)
        tail = [
            (pl.BlockSpec(keep, fixed3), jax.ShapeDtypeStruct(keep, BF16)),
            (pl.BlockSpec(send, fixed3), jax.ShapeDtypeStruct(send, BF16)),
            (pl.BlockSpec((24, width), fixed), jax.ShapeDtypeStruct((24, width), F32)),
        ]
        scratch = [pltpu.VMEM(bias_shape.shape, F32), pltpu.VMEM(acc_shape.shape, F32)]
    return pl.pallas_call(
        functools.partial(
            attn_bwd_kernel, first, count, heads, short_blocks, first_call, split
        ),
        grid_spec=pltpu.PrefetchScalarGridSpec(
            num_scalar_prefetch=4,
            grid=(count,),
            in_specs=in_specs,
            out_specs=[pl.BlockSpec((width, span), here)] + [t[0] for t in tail],
            scratch_shapes=[
                pltpu.VMEM((3 * width, span), BF16),
                pltpu.VMEM((2, width, span), BF16),
                pltpu.VMEM((heads, 2 * HD + 16, span), BF16),
                pltpu.VMEM((heads, 2 * HD + 16, span), BF16),
            ]
            + scratch,
        ),
        out_shape=[jax.ShapeDtypeStruct((width, tokens), F32)] + [t[1] for t in tail],
        input_output_aliases=aliases,
        cost_estimate=COST(4.0 * count),
        compiler_params=pltpu.CompilerParams(vmem_limit_bytes=VMEM_LIMIT),
        name=f"attn_bwd{first}",
    )(me, parity, lens_s, lens_l, *args)


def prep_kernel(w0, w1, w2, w3, *refs):
    params = refs[:6]
    owt, upt, dnt, upn, dnn, ub, cols, ow = refs[6:]
    weights = (w0, w1, w2, w3)
    model = owt.shape[0]
    width = model // 4

    def eye(n):
        a = lax.broadcasted_iota(jnp.int32, (n, n), 0)
        b = lax.broadcasted_iota(jnp.int32, (n, n), 1)
        return jnp.where(a == b, 1.0, 0.0).astype(BF16)

    big, small = eye(256), eye(width)
    for k, w in enumerate(weights):
        ks = slice(k * width, (k + 1) * width)
        ow[ks, :] = w[:width, :]
        for at in range(0, model, 256):
            lanes = slice(at, at + 256)
            for ref, first in ((upt, width), (dnt, 2 * width)):
                t = dot(big, w[first : first + width, lanes], 1, 1).astype(BF16)
                for g in range(4):
                    low, high = max(at, g * width), min(at + 256, (g + 1) * width)
                    if low < high:
                        start = k * width + low - g * width
                        ref[g, start : start + high - low, :] = t[low - at : high - at, :]
        bt = w[3 * width :, :].astype(F32).T
        ub[:, k : k + 1] = (bt[:, 2:3] + bt[:, 1:2]) + bt[:, 0:1]

    @pl.loop(0, model // 256)
    def _(i):
        at = pl.ds(pl.multiple_of(i * 256, 256), 256)
        owt[at, :] = dot(big, ow[:, at], 1, 1).astype(BF16)

    @pl.loop(0, 4)
    def _(g):
        upn[g] = dot(small, upt[g], 1, 1).astype(BF16)
        dnn[g] = dot(small, dnt[g], 1, 1).astype(BF16)

    for j, p in enumerate(params):
        cols[:, j : j + 1] = jnp.broadcast_to(p[...].reshape(1, model), (8, model)).T[:, 0:1]


def prep(weights, params):
    model = weights[0].shape[1]
    width = model // 4
    vmem = pl.BlockSpec(memory_space=pltpu.VMEM)
    shapes = [
        jax.ShapeDtypeStruct((model, model), BF16),
        jax.ShapeDtypeStruct((4, model, width), BF16),
        jax.ShapeDtypeStruct((4, model, width), BF16),
        jax.ShapeDtypeStruct((4, width, model), BF16),
        jax.ShapeDtypeStruct((4, width, model), BF16),
        jax.ShapeDtypeStruct((model, 8), F32),
        jax.ShapeDtypeStruct((model, 8), F32),
        jax.ShapeDtypeStruct((model, model), BF16),
    ]
    return pl.pallas_call(
        prep_kernel,
        in_specs=[vmem] * 10,
        out_specs=[vmem] * len(shapes),
        out_shape=shapes,
        cost_estimate=COST(4.0),
        compiler_params=pltpu.CompilerParams(vmem_limit_bytes=VMEM_LIMIT),
        name="prep",
    )(*weights, *params)


def mid_kernel(half, width, blocks, me, *refs):
    ctx, hid = refs[0:4], refs[4:8]
    og, ub, cols = refs[8:11]
    given = refs[11:17]
    at = 17
    if half:
        acc_hbm, vec_in = refs[at : at + 3], refs[at + 3]
        at += 5
    lo = refs[at]
    back = refs[at + 1 : at + 5]
    at += 5
    if half:
        keep, send, vec_out = refs[at : at + 3]
        at += 3
    else:
        acc_hbm, vec = refs[at : at + 3], refs[at + 3]
        at += 4
    (gow, gup, gdn, owt, upt, dnt, upn, dnn, ow) = refs[at : at + 9]
    at += 9
    (sums, act, slope, first, n1s, gps_s, cats, lows, sem, acc_sem) = refs[at : at + 10]
    if half:
        vec = refs[at + 10]
    accs = (gow, gup, gdn)
    step = pl.program_id(0)
    last = pl.num_programs(0) - 1
    model = 4 * width
    inv = 1.0 / model
    held = (owt, upt, dnn, dnt, upn, ow)

    def own(k):
        return pl.ds(pl.multiple_of(lax.bitwise_xor(me[0], k) * width, width), width)

    def fetch(i):
        return pltpu.make_async_copy(given[i], held[i], sem.at[i])

    def ready(i):
        @pl.when(step == 0)
        def _():
            fetch(i).wait()

    def acc_copy(i):
        if half:
            return pltpu.make_async_copy(acc_hbm[i], accs[i], acc_sem.at[i])
        return pltpu.make_async_copy(accs[i], acc_hbm[i], acc_sem.at[i])

    @pl.when(step == 0)
    def _():
        for i in range(6):
            fetch(i).start()
        if half:
            for i in range(3):
                acc_copy(i).start()
        row = lax.broadcasted_iota(jnp.int32, (16, TILE), 0)
        for g in range(4):
            lows[g, width:, :] = jnp.where(row == 0, 1.0, 0.0).astype(BF16)
        sums[...] = jnp.zeros_like(sums)

    def before(value):
        return value if half else jnp.where(step == 0, 0.0, value)

    def acc_ready(i):
        if half:

            @pl.when(step == 0)
            def _():
                acc_copy(i).wait()

    def acc_done(i):
        if not half:

            @pl.when(step == last)
            def _():
                acc_copy(i).start()

    def col(j):
        return cols[:, j : j + 1]

    def add_sum(j, value):
        sums[j] += sum(value[:, i : i + 128] for i in range(0, TILE, 128))

    for k in range(4):
        cats[k * width : (k + 1) * width, :] = ctx[k][0]
    ready(0)
    first[...] = dot(owt[...], cats[...], 1, 0) + col(0)
    for k in range(4):
        first[own(k), :] += hid[k][...].reshape(width, TILE).astype(F32)
    pre = first[...]
    cen = pre - jnp.sum(pre, axis=0, keepdims=True) * inv
    r1 = lax.rsqrt(jnp.sum(cen * cen, axis=0, keepdims=True) * inv + EPSILON)
    n1 = cen * r1
    n1s[...] = n1
    normed = n1 * col(1) + col(2)
    first[...] = normed
    low = normed.astype(BF16)
    for g in range(4):
        lows[g, :width, :] = low[g * width : (g + 1) * width, :]
    ready(1)
    ready(2)

    def pre_act(g):
        return dot(upt[g], lows[g, :width, :], 1, 0)

    later = pre_act(0)
    for g in range(4):
        rows = slice(g * width, (g + 1) * width)
        raw = later
        if g < 3:
            later = pre_act(g + 1)
        for k in range(4):
            units = slice(k * width, (k + 1) * width)
            pa = raw[units, :] + ub[rows, k : k + 1]
            phi, sl = gelu_parts(pa)
            act[g, units, :] = (pa * phi).astype(BF16)
            slope[g, units, :] = sl
        first[rows, :] += dot(dnn[g], act[g], 1, 0) + cols[rows, 3:4]
    pre = first[...]
    cen = pre - jnp.sum(pre, axis=0, keepdims=True) * inv
    r2 = lax.rsqrt(jnp.sum(cen * cen, axis=0, keepdims=True) * inv + EPSILON)
    n2 = cen * r2
    lo[...] = (n2 * col(4) + col(5)).astype(BF16).T
    ogt = og[...].T.astype(F32)
    add_sum(4, ogt * n2)
    add_sum(5, ogt)
    u = ogt * col(4)
    gps = r2 * (
        u
        - jnp.sum(u, axis=0, keepdims=True) * inv
        - n2 * (jnp.sum(u * n2, axis=0, keepdims=True) * inv)
    )
    add_sum(3, gps)
    gdl = gps.astype(BF16)
    gps_s[...] = gps
    ready(3)
    ready(4)
    acc_ready(1)
    acc_ready(2)

    def grad_act(g):
        return dot(dnt[g], gdl[g * width : (g + 1) * width, :], 1, 0)

    later = grad_act(0)
    for g in range(4):
        rows = slice(g * width, (g + 1) * width)
        raw = later
        if g < 3:
            later = grad_act(g + 1)
        gdn[g] = before(gdn[g]) + dot(act[g], gdl[rows, :], 1, 1)
        gpa = (raw * slope[g]).astype(BF16)
        gup[g] = before(gup[g]) + dot(gpa, lows[g], 1, 1)
        gps_s[rows, :] += dot(upn[g], gpa, 1, 0)
    acc_done(1)
    acc_done(2)
    gn = gps_s[...]
    n1 = n1s[...]
    add_sum(1, gn * n1)
    add_sum(2, gn)
    u = gn * col(1)
    gpf = r1 * (
        u
        - jnp.sum(u, axis=0, keepdims=True) * inv
        - n1 * (jnp.sum(u * n1, axis=0, keepdims=True) * inv)
    )
    gpl = gpf.astype(BF16)
    first[...] = gpl.astype(F32)
    add_sum(0, first[...])
    ready(5)
    acc_ready(0)
    gow[...] = before(gow[...]) + dot(gpl, cats[...], 1, 1)
    acc_done(0)
    for k in range(4):
        back[k][1] = first[own(k), :].astype(BF16)
        back[k][0] = dot(ow[k * width : (k + 1) * width, :], gpl, 1, 0).astype(BF16)

    @pl.when(step == last)
    def _():
        lane = lax.broadcasted_iota(jnp.int32, (1, 128), 1)
        total = vec_in[...] if half else jnp.zeros((model, 128), F32)
        for j in range(6):
            total += jnp.where(lane == j, jnp.sum(sums[j], axis=1, keepdims=True), 0.0)
        vec[...] = total
        if half:
            for g in range(4):
                for k in range(4):
                    vec[own(k), :] += jnp.where(
                        lane == 6 + g, gup[g, k * width : (k + 1) * width, width : width + 1], 0.0
                    )
            more = vec[...].T[:16]
            vec_out[...] = more
            part = width // blocks

            @pl.loop(0, 2)
            def _(far):
                for near in range(2):
                    dest = send if near else keep
                    units = pl.ds(pl.multiple_of((2 * far + near) * width, 8), width)
                    up_rows = pl.ds(pl.multiple_of(far * 3 * width, 16), width)
                    down_rows = pl.ds(pl.multiple_of((far * 3 + 1) * width, 16), width)
                    for g in range(4):
                        lanes = slice(g * width, (g + 1) * width)
                        dest[up_rows, lanes] = gup[g, units, :width].T.astype(BF16)
                        dest[down_rows, lanes] = gdn[g, units, :].T.astype(BF16)

            pairs = 2 if blocks > 1 else 1

            @pl.loop(0, blocks // pairs)
            def _(pair):
                for k in range(4):
                    dest = send if k % 2 else keep
                    base = ((k // 2) * 3 + 2) * width
                    units = slice(k * width, (k + 1) * width)
                    to = pl.ds(pl.multiple_of(base + pair * pairs * part, 16), pairs * part)
                    for g in range(4):
                        lanes = slice(g * width, (g + 1) * width)
                        rows = []
                        for i in range(pairs):
                            start = ((pair * pairs + i) * 4 + g) * part
                            rows.append(gow[pl.ds(pl.multiple_of(start, 8), part), units])
                        dest[to, lanes] = jnp.concatenate(rows, axis=0).astype(BF16)

            if blocks > 1:
                high = more.astype(BF16)
                send[6 * width : 6 * width + 16, :] = high
                send[6 * width + part : 6 * width + part + 16, :] = (
                    more - high.astype(F32)
                ).astype(BF16)
        else:
            for i in range(3):
                acc_copy(i).wait()


def mid(half, me, ctx, hid, og, ready, carry, blocks):
    width, span = ctx[0].shape[1:]
    model = 4 * width
    steps = span // TILE
    whole2 = lambda i, *_: (0, 0)
    ctx_tile = pl.BlockSpec((1, width, TILE), lambda i, *_: (0, 0, i))
    hid_own = pl.BlockSpec((width, TILE), lambda i, me: (0, (me[0] * 2 + half) * steps + i))
    hid_tile = pl.BlockSpec((1, width, TILE), lambda i, *_: (1, 0, i))
    back_tile = pl.BlockSpec((2, width, TILE), lambda i, *_: (0, 0, i))
    row_in = pl.BlockSpec((TILE, model), lambda i, *_: (half * steps + i, 0))
    hbm = pl.BlockSpec(memory_space=pl.ANY)
    column = pl.BlockSpec((model, 8), whole2)
    vec_spec = pl.BlockSpec((model, 128), whole2)
    owt, upt, dnt, upn, dnn, ub, cols, ow = ready
    in_specs = [ctx_tile] * 4 + [hid_own] + [hid_tile] * 3 + [row_in, column, column] + [hbm] * 6
    args = [*ctx, *hid, og, ub, cols, owt, upt, dnn, dnt, upn, ow]
    accs = [(model, model), (4, model, width + 16), (4, model, width)]
    piece = jax.ShapeDtypeStruct((2, width, span), BF16)
    scratch = [pltpu.VMEM(a, F32) for a in accs] + [
        pltpu.VMEM((model, model), BF16),
        pltpu.VMEM((4, model, width), BF16),
        pltpu.VMEM((4, model, width), BF16),
        pltpu.VMEM((4, width, model), BF16),
        pltpu.VMEM((4, width, model), BF16),
        pltpu.VMEM((model, model), BF16),
        pltpu.VMEM((6, model, 128), F32),
        pltpu.VMEM((4, model, TILE), BF16),
        pltpu.VMEM((4, model, TILE), F32),
        pltpu.VMEM((model, TILE), F32),
        pltpu.VMEM((model, TILE), F32),
        pltpu.VMEM((model, TILE), F32),
        pltpu.VMEM((model, TILE), BF16),
        pltpu.VMEM((4, width + 16, TILE), BF16),
        pltpu.SemaphoreType.DMA((6,)),
        pltpu.SemaphoreType.DMA((3,)),
    ]
    aliases = {}
    if half:
        in_specs += [hbm] * 3 + [vec_spec, hbm]
        aliases = {len(args) + 5: 0}
        args += list(carry)
        extra = 2 * (width // blocks) if blocks > 1 else 0
        rows = [6 * width, 6 * width + extra]
        tail_specs = [pl.BlockSpec((r, model), whole2) for r in rows + [16]]
        tail_shapes = [jax.ShapeDtypeStruct((r, model), BF16) for r in rows]
        tail_shapes += [jax.ShapeDtypeStruct((16, model), F32)]
        scratch += [pltpu.VMEM((model, 128), F32)]
    else:
        tail_specs = [hbm] * 3 + [vec_spec]
        tail_shapes = [jax.ShapeDtypeStruct(a, F32) for a in accs + [(model, 128)]]
    return pl.pallas_call(
        functools.partial(mid_kernel, half, width, blocks),
        grid_spec=pltpu.PrefetchScalarGridSpec(
            num_scalar_prefetch=1,
            grid=(steps,),
            in_specs=in_specs,
            out_specs=[row_in] + [back_tile] * 4
            + tail_specs,
            scratch_shapes=scratch,
        ),
        out_shape=[jax.ShapeDtypeStruct((2 * span, model), BF16)] + [piece] * 4 + tail_shapes,
        input_output_aliases=aliases,
        cost_estimate=COST(25.0),
        compiler_params=pltpu.CompilerParams(vmem_limit_bytes=VMEM_LIMIT),
        name=f"mid{half}",
    )(me, *args)


def put_pair(ref, at, value):
    rows = value.shape[0]
    high = value.astype(BF16)
    ref[at, :rows] = high
    ref[at + 1, :rows] = (value - high.astype(F32)).astype(BF16)


def get_pair(ref, at, rows):
    return ref[at, :rows].astype(F32) + ref[at + 1, :rows].astype(F32)


def split_kernel(bit0, bit1, keep, recv, extra, kept, sent_y, sent_z, extra_out):
    size = keep.shape[0]
    per = size // 6
    half = per // 2
    more = extra[...] + get_pair(recv, size, extra.shape[0])
    extra_out[...] = more
    put_pair(sent_y, 4 * half, more)
    low, high = bit0[0], bit1[0]

    def total(i):
        return (keep[i].astype(F32) + recv[i].astype(F32)).astype(BF16)

    for k in range(2):
        for section in range(3):
            base = (k * 3 + section) * per
            for e in range(half):
                if section < 2:
                    mine, other = base + 2 * e + low, base + 2 * e + 1 - low
                    dest, at = sent_y, (k * 2 + section) * half + e
                else:
                    first = base + 4 * (e // 2) + e % 2
                    mine, other = first + 2 * high, first + 2 * (1 - high)
                    dest, at = sent_z, k * half + e
                kept[base // 2 + e] = total(mine)
                dest[at] = total(other)


def join_kernel(keep, recv_y, recv_z, extra, kept, sent, extra_out):
    half = keep.shape[0] // 6
    more = extra[...] + get_pair(recv_y, 4 * half, extra.shape[0])
    extra_out[...] = more
    put_pair(sent, 3 * half, more)
    for k in range(2):
        for section in range(3):
            for e in range(half):
                if section < 2:
                    other = recv_y[(k * 2 + section) * half + e]
                else:
                    other = recv_z[k * half + e]
                value = keep[(k * 3 + section) * half + e].astype(F32) + other.astype(F32)
                (sent if k else kept)[section * half + e] = value.astype(BF16)


def early_kernel(bit0, bit1, keep, recv, extra, kept, sent_z, sent_y, extra_out):
    size = keep.shape[0]
    half = size // 6
    more = extra[...] + get_pair(recv, size, extra.shape[0])
    extra_out[...] = more
    put_pair(sent_z, 2 * half, more)

    def total(i):
        return (keep[i].astype(F32) + recv[i].astype(F32)).astype(BF16)

    for section in range(3):
        mine = bit1[0] if section < 2 else bit0[0]
        for e in range(half):
            at = section * 2 * half + 2 * e
            kept[section * half + e] = total(at + mine)
            if section < 2:
                sent_z[section * half + e] = total(at + 1 - mine)
            else:
                sent_y[e] = total(at + 1 - mine)


def combine(kernel, bits, args, sizes, name):
    rows, lanes = args[0].shape[1:]
    vmem = pl.BlockSpec(memory_space=pltpu.VMEM)
    shapes = [jax.ShapeDtypeStruct((n, rows, lanes), BF16) for n in sizes]
    shapes.append(jax.ShapeDtypeStruct(args[-1].shape, F32))
    return pl.pallas_call(
        kernel,
        in_specs=[pl.BlockSpec(memory_space=pltpu.SMEM)] * len(bits) + [vmem] * len(args),
        out_specs=[vmem] * len(shapes),
        out_shape=shapes,
        cost_estimate=COST(1.0),
        compiler_params=pltpu.CompilerParams(vmem_limit_bytes=VMEM_LIMIT),
        name=name,
    )(*bits, *args)


def pulled(kernel, bits, count, *refs):
    bits, refs = refs[:bits], refs[bits:]
    bufs, sem = refs[-count - 1 : -1], refs[-1]
    copies = [pltpu.make_async_copy(refs[i], bufs[i], sem.at[i]) for i in range(count)]
    for c in copies:
        c.start()
    for c in copies:
        c.wait()
    kernel(*bits, *bufs, *refs[count : -count - 1])


def pull_call(kernel, count, bits, args, shapes, name):
    vmem = pl.BlockSpec(memory_space=pltpu.VMEM)
    return pl.pallas_call(
        functools.partial(pulled, kernel, len(bits), count),
        in_specs=[pl.BlockSpec(memory_space=pltpu.SMEM)] * len(bits)
        + [pl.BlockSpec(memory_space=pltpu.HBM)] * count
        + [vmem] * (len(args) - count),
        out_specs=[vmem] * len(shapes),
        out_shape=shapes,
        scratch_shapes=[pltpu.VMEM(a.shape, a.dtype) for a in args[:count]]
        + [pltpu.SemaphoreType.DMA((count,))],
        cost_estimate=COST(1.0),
        compiler_params=pltpu.CompilerParams(vmem_limit_bytes=VMEM_SMALL),
        name=name,
    )(*bits, *args)


def combine_early(bits, keep, recv, extra, name):
    size, rows, lanes = keep.shape
    half = size // 6
    shapes = [
        jax.ShapeDtypeStruct((3 * half, rows, lanes), BF16),
        jax.ShapeDtypeStruct((2 * half + 2, rows, lanes), BF16),
        jax.ShapeDtypeStruct((half, rows, lanes), BF16),
        jax.ShapeDtypeStruct(extra.shape, F32),
    ]
    return pull_call(early_kernel, 3, bits, [keep, recv, extra], shapes, name)


def qkv_kernel(index, qk, qb, qr, kept, sent, qb_out):
    size = qk.shape[0]
    more = qb[...] + (qr[size, :24].astype(F32) + qr[size, 24:48].astype(F32))
    qb_out[...] = more
    hi = more.astype(BF16)
    sent[size // 2, :24] = hi
    sent[size // 2, 24:48] = (more - hi.astype(F32)).astype(BF16)
    mine = index[0]
    for i in range(size // 2):
        a, b = 2 * i + mine, 2 * i + 1 - mine
        kept[i] = (qk[a].astype(F32) + qr[a].astype(F32)).astype(BF16)
        sent[i] = (qk[b].astype(F32) + qr[b].astype(F32)).astype(BF16)


def qkv_stage(index, qk, qb, qr, name):
    size, rows, lanes = qk.shape
    shapes = [
        jax.ShapeDtypeStruct((size // 2, rows, lanes), BF16),
        jax.ShapeDtypeStruct((size // 2 + 1, rows, lanes), BF16),
        jax.ShapeDtypeStruct(qb.shape, F32),
    ]
    return pull_call(qkv_kernel, 2, [index], [qk, qb, qr], shapes, name)


def blend_kernel(joint, last, index, wk, wr, vec, qk, *refs):
    if not joint:
        wy, qr, qb, refs = refs[0], refs[1], refs[2], refs[3:]
    nw, rows, model = wk.shape
    nq, width = qk.shape[0], qk.shape[2]
    pitch = model // 3
    if joint:
        terms = wr[nw].astype(F32)
        more = vec[:12] + (terms[:12] + terms[12:24])
    else:
        more = vec[:12] + get_pair(wr, wr.shape[0] - 2, 16)[:12]
        bias = qb[...] + (qr[nq, :24].astype(F32) + qr[nq, 24:48].astype(F32))

    def wsum(section, i):
        at = section * (nw // 3) + i
        other = wr[at] if joint or section < 2 else wy[i]
        return wk[at].astype(F32) + other.astype(F32)

    def qsum(i, j):
        part = slice(j * rows, (j + 1) * rows)
        if joint:
            other = wr[nw + 1 + i, :, j * pitch : j * pitch + width]
        else:
            other = qr[i, part, :]
        return qk[i, part, :].astype(F32) + other.astype(F32)

    if last:
        gup, gdn, gow, gqkv, gqv, gub = refs[:6]
        vecs = refs[6:]
        gup[...] = wsum(0, 0)
        gdn[...] = wsum(1, 0)
        ow = wsum(2, 0)
        quarter = model // 4
        gow[...] = jnp.concatenate(
            [ow[:, j * quarter : (j + 1) * quarter] for j in range(4)], axis=0
        ).T
        for j in range(3):
            gqkv[j * rows : (j + 1) * rows, :] = qsum(0, j)
        gqv[:, :width] = more[10:11, :width]
        gqv[:, width:] = more[10:11, 2 * pitch : 2 * pitch + width]
        own = vecs[0].shape[0]
        more = jnp.concatenate([more, jnp.zeros((4, model), F32)], axis=0)
        here = pltpu.roll(more, index[1], 1)
        for j, v in enumerate(vecs):
            v[...] = here[j, :own]
        here = pltpu.roll(more, index[2], 1)
        gub[...] = jnp.concatenate([here[6 + j, :quarter] for j in range(4)])
        return
    wkept, sent, vec_out, qkept = refs
    mine = index[0]
    vec_out[:12] = more
    vec_out[12:] = jnp.zeros((4, model), F32)
    if not joint:
        for j in range(3):
            vec_out[10:11, j * pitch : j * pitch + width] = bias[8 * j : 8 * j + 1]
    half = nw // 2
    more = vec_out[:12]
    hi = more.astype(BF16).astype(F32)
    sent[half, :24] = jnp.concatenate([hi, more - hi], axis=0).astype(BF16)
    for i in range(3):
        wkept[i] = wsum(i, mine).astype(BF16)
        sent[i] = wsum(i, 1 - mine).astype(BF16)
    at = half + 1
    for i in range(nq // 2):
        for j in range(3):
            qkept[i, j * rows : (j + 1) * rows, :] = qsum(2 * i + mine, j).astype(BF16)
            sent[at + i, :, j * pitch : j * pitch + width] = qsum(2 * i + 1 - mine, j).astype(BF16)


def blend(index, wk, wr, wy, vec, qk, qr, qb, last, name):
    nw, rows, model = wk.shape
    nq, _, width = qk.shape
    vmem = pl.BlockSpec(memory_space=pltpu.VMEM)
    args = [wk, wr, vec, qk] + ([] if qr is None else [wy, qr, qb])
    shape = jax.ShapeDtypeStruct
    if last:
        quarter = model // 4
        shapes = [
            shape((rows, model), F32),
            shape((rows, model), F32),
            shape((quarter, 4 * rows), F32),
            shape((3 * rows, width), F32),
            shape((1, 2 * width), F32),
            shape((model,), F32),
        ] + [shape((rows,), F32)] * 6
    else:
        shapes = [
            shape((nw // 2, rows, model), BF16),
            shape((nw // 2 + nq // 2 + 1, rows, model), BF16),
            shape(vec.shape, F32),
            shape((nq // 2, 3 * rows, width), BF16),
        ]
    return pl.pallas_call(
        functools.partial(blend_kernel, qr is None, last),
        in_specs=[pl.BlockSpec(memory_space=pltpu.SMEM)] + [vmem] * len(args),
        out_specs=[vmem] * len(shapes),
        out_shape=shapes,
        cost_estimate=COST(1.0),
        compiler_params=pltpu.CompilerParams(vmem_limit_bytes=VMEM_SMALL),
        name=name,
    )(index, *args)


def swap(value, axis, bit):
    count = lax.axis_size(axis)
    return lax.ppermute(value, axis, [(i, i ^ bit) for i in range(count)])


def to_chan(pieces):
    return [pieces[0]] + [swap(pieces[k], "chan", k) for k in range(1, 4)]


def gather_chan(value):
    near = swap(value, "chan", 1)
    far = swap(value, "chan", 2)
    return [value, near, far, swap(far, "chan", 1)]


def scatter_dp(pieces):
    index = lax.axis_index("dp")
    count, bit = pieces.shape[0], 1
    while count > 1:
        view = pieces.reshape((count // 2, 2) + pieces.shape[1:])
        digit = (index // bit) % 2
        mine = lax.dynamic_index_in_dim(view, digit, 1, keepdims=False).astype(F32)
        other = lax.dynamic_index_in_dim(view, 1 - digit, 1, keepdims=False)
        total = mine + swap(other, "dp", bit).astype(F32)
        count, bit = count // 2, bit * 2
        pieces = total if count == 1 else total.astype(pieces.dtype)
    return pieces[0]


def sum_dp(value):
    bit = 1
    while bit < lax.axis_size("dp"):
        value = value + swap(value, "dp", bit)
        bit *= 2
    return value


def pack_kernel(ow, up, dn, ub, weights):
    width = ow.shape[0]
    for i, w in enumerate((ow, up, dn)):
        weights[i * width : (i + 1) * width, :] = w[...]
    whole = jnp.broadcast_to(ub[...].reshape(1, -1), (16, ub.shape[0]))
    high = whole.astype(BF16)
    rest = whole - high.astype(F32)
    middle = rest.astype(BF16)
    low = (rest - middle.astype(F32)).astype(BF16)
    row = lax.broadcasted_iota(jnp.int32, whole.shape, 0)
    terms = jnp.where(
        row == 0,
        high.astype(F32),
        jnp.where(row == 1, middle.astype(F32), low.astype(F32)),
    )
    weights[3 * width :, :] = terms.astype(BF16)


def pack(ow, up, dn, ub):
    width, model = ow.shape
    vmem = pl.BlockSpec(memory_space=pltpu.VMEM)
    return pl.pallas_call(
        pack_kernel,
        in_specs=[vmem] * 4,
        out_specs=vmem,
        out_shape=jax.ShapeDtypeStruct((3 * width + 16, model), BF16),
        cost_estimate=COST(1.0),
        compiler_params=pltpu.CompilerParams(vmem_limit_bytes=VMEM_LIMIT),
        name="pack",
    )(ow, up, dn, ub)


def digit(value, b):
    return ((value >> b) & 1)[None]


def reduce_plain(keep, send, vec, dp_count):
    width, model = keep.shape[0] // 6, keep.shape[1]
    sections = 3
    keep = keep.reshape(2, 3, width, model)
    send = send[: 6 * width].reshape(2, 3, width, model)
    rows = width // dp_count
    keep = keep + swap(send, "chan", 1)
    keep = keep[0] + swap(keep[1], "chan", 2)
    if rows < 16:
        last = keep[2].reshape(width, 4, width).transpose(1, 0, 2).reshape(width, model)
        last = last.reshape(dp_count, 4, rows, width).transpose(0, 2, 1, 3)
        keep = jnp.stack([keep[0], keep[1], last.reshape(width, model)])
    keep = keep.reshape(sections, dp_count, rows, model).transpose(1, 0, 2, 3)
    vec = vec + swap(vec, "chan", 1)
    vec = sum_dp(vec + swap(vec, "chan", 2))
    return scatter_dp(keep), vec


def on_device(
    hidden_in,
    lengths_short,
    lengths_long,
    qkv_weight,
    qv_bias,
    out_weight,
    mixer_bias,
    first_gain,
    first_shift,
    up_weight,
    up_bias,
    down_weight,
    down_bias,
    second_gain,
    second_shift,
    out_grad,
):
    width, tokens = hidden_in.shape
    span = tokens // 8
    model = 4 * width
    dp_count = lax.axis_size("dp")
    chan = lax.axis_index("chan").astype(jnp.int32)
    dp = lax.axis_index("dp").astype(jnp.int32)
    me = chan[None]
    bar = lax.optimization_barrier
    fine = width // dp_count >= 16 and dp_count == 8
    lengths = (lengths_short, lengths_long)
    w = qkv_weight[0]

    packed = pack(out_weight, up_weight, down_weight, up_bias)
    params = [mixer_bias, first_gain, first_shift, down_bias, second_gain, second_shift]
    far = swap(packed, "chan", 2)
    near = swap(packed, "chan", 1)
    x, _ = bar((hidden_in, packed))
    proj, *parts, lse = attn_fwd(me, *lengths, x, w, qv_bias)
    parts = [parts[:4], parts[4:]]
    far, near, parts = bar((far, near, parts))
    first = to_chan(parts[0])
    weights = [packed, near, far, swap(far, "chan", 1)]
    ready = prep(weights, params)
    second = to_chan(parts[1])
    blocks = dp_count if fine else 1
    hid = [hidden_in] + first[1:]
    lo, *rest = mid(0, me, first, hid, out_grad, ready, None, blocks)
    g0, carry = rest[:4], [*rest[4:], lo]
    g0, carry, second = bar((g0, carry, second))
    back0 = to_chan(g0)
    hid = [hidden_in] + second[1:]
    lo, *rest = mid(1, me, second, hid, out_grad, ready, carry, blocks)
    rest, back0 = bar((rest, back0))
    g1, (keep, send, vec) = rest[:4], rest[4:]
    recv = swap(send, "chan", 1)
    back = [*back0, *to_chan(g1)]
    parity = digit(dp, 0)

    def backward(start, count, x, carry, split):
        return attn_bwd(
            start,
            count,
            me,
            parity,
            *lengths,
            x,
            w,
            proj,
            lse,
            back,
            carry,
            dp_count,
            split,
        )

    if not fine:
        sums, vec = reduce_plain(keep, send, vec, dp_count)
        carry = backward(0, 5, hidden_in, None, 0)
        grad_input, gq, gbias = backward(5, 3, hidden_in, carry, 1)
        gq, gbias = scatter_dp(gq), sum_dp(gbias[0])
        own = width // dp_count
        mine = lax.dynamic_slice_in_dim(vec[:6], (dp * 4 + chan) * own, own, 1)
        mine = [mine[i] for i in range(6)]
        gub = lax.dynamic_slice_in_dim(vec[6:10], chan * width, width, 1).reshape(model)
        gup, gdn = sums[0], sums[1]
        gow = sums[2].reshape(-1, 4, width).transpose(1, 0, 2).reshape(model // dp_count, width).T
        gqv = jnp.concatenate([gbias[:width], gbias[2 * width :]])[None]
    else:
        rows = width // dp_count
        size = 6 * dp_count
        recv = recv.reshape(size + 2, rows, model)
        keep = keep.reshape(size, rows, model)

        bits = [parity, digit(dp, 1)]
        keep, send_y, send_z, vec = combine(
            split_kernel, bits, [keep, recv, vec], [24, 18, 8], "combine0"
        )
        recv_y, recv_z = swap(send_y, "dp", 1), swap(send_z, "dp", 2)
        x, keep = bar((hidden_in, keep))
        carry = backward(0, 5, x, None, 0)
        recv_y, recv_z, carry = bar((recv_y, recv_z, carry))
        keep, send, vec = combine(
            join_kernel, [], [keep, recv_y, recv_z, vec], [12, 14], "combine1"
        )
        recv = swap(send, "chan", 2)
        x, keep = bar((x, keep))
        grad_input, gk, gs, gbias = backward(5, 3, x, carry, 2)
        recv, gk, gs = bar((recv, gk, gs))
        grecv = swap(gs, "dp", 1)
        keep, send_z, send_y, vec = combine_early(bits, keep, recv, vec, "combine2")
        recv_z, recv_y = swap(send_z, "dp", 2), swap(send_y, "dp", 1)
        grecv, keep = bar((grecv, keep))
        gk, gs, gbias = qkv_stage(bits[1], gk, gbias, grecv, "qkv2")
        grecv = swap(gs, "dp", 2)
        recv_z, recv_y, gk = bar((recv_z, recv_y, gk))
        keep, send, vec, gk = blend(
            digit(dp, 2), keep, recv_z, recv_y, vec, gk, grecv, gbias, False, "blend2"
        )
        recv = swap(send, "dp", 4)
        index = jnp.stack(
            [
                jnp.zeros_like(dp),
                (model - (dp * 4 + chan) * rows) % model,
                (model - chan * width) % model,
            ]
        )
        gup, gdn, gow, gq, gqv, gub, *mine = blend(
            index, keep, recv, None, vec, gk, None, None, True, "blend"
        )
    return (
        lo,
        grad_input,
        gq.T[None],
        gqv,
        gow,
        mine[0],
        mine[1],
        mine[2],
        gup,
        gub,
        gdn,
        mine[3],
        mine[4],
        mine[5],
    )


def solution(mesh):
    in_specs = (
        P("chan", "dp"),
        P("dp"),
        P("dp"),
        P("chan", None, None),
        P("chan", None),
        P("chan", None),
        P(),
        P(),
        P(),
        P(None, "chan"),
        P("chan"),
        P(None, "chan"),
        P(),
        P(),
        P(),
        P(("dp", "chan"), None),
    )
    out_specs = (
        P(("dp", "chan"), None),
        P("chan", "dp"),
        P("chan", None, "dp"),
        P("chan", None),
        P("chan", "dp"),
        P(("dp", "chan")),
        P(("dp", "chan")),
        P(("dp", "chan")),
        P("dp", "chan"),
        P("chan"),
        P("dp", "chan"),
        P(("dp", "chan")),
        P(("dp", "chan")),
        P(("dp", "chan")),
    )
    return jax.shard_map(
        on_device, mesh=mesh, in_specs=in_specs, out_specs=out_specs, check_vma=False
    )
```

```python
import functools

import jax
import jax.numpy as jnp
from jax import lax
from jax.experimental import pallas as pl
from jax.experimental.pallas import tpu as pltpu
from jax.sharding import PartitionSpec as P

HD = 64
LS = 128
LL = 512
TILE = 256
EPSILON = 1e-06
LOG2E = 1.4426950408889634
F32 = jnp.float32
BF16 = jnp.bfloat16
VMEM_LIMIT = 67043328
VMEM_SMALL = 8388608


def COST(us):
    return pl.CostEstimate(
        flops=int(us * 1.0e9), bytes_accessed=int(us * 1.0e6), transcendentals=0
    )


def dot(a, b, ca, cb):
    return lax.dot_general(a, b, (((ca,), (cb,)), ((), ())), preferred_element_type=F32)


def gelu_parts(v):
    av = jnp.abs(v)
    t = 1.0 / (1.0 + (0.3275911 * 0.7071067811865476) * av)
    e = jnp.exp2((-0.5 * LOG2E) * (v * v))
    poly = t * (
        0.5 * 0.254829592
        + t
        * (
            0.5 * -0.284496736
            + t * (0.5 * 1.421413741 + t * (0.5 * -1.453152027 + t * (0.5 * 1.061405429)))
        )
    )
    tail = poly * e
    phi = jnp.where(v >= 0, 1.0 - tail, tail)
    return phi, phi + v * (0.3989422804014327 * e)


def score_operands(heads, span, seq_len, lens, first, q, key, qa, ka):
    width = heads * HD
    scaled = q.astype(F32) * (HD**-0.5 * LOG2E)
    high = scaled.astype(BF16)
    low = (scaled - high.astype(F32)).astype(BF16)
    pos = lax.broadcasted_iota(jnp.int32, (16, seq_len), 1)
    row = lax.broadcasted_iota(jnp.int32, (16, seq_len), 0)
    for h in range(heads):
        rows = slice(h * HD, (h + 1) * HD)
        qa[h, 0:HD, :] = high[rows]
        qa[h, HD : 2 * HD, :] = low[rows]
        ka[h, 0:HD, :] = key[rows]
        ka[h, HD : 2 * HD, :] = key[rows]
    for i in range(span // seq_len):
        bad = (row == 0) & (pos >= lens[first + i])
        mask = jnp.where(bad, -1e9, 0.0).astype(BF16)
        for h in range(heads):
            ka[h, 2 * HD :, i * seq_len : (i + 1) * seq_len] = mask


def one_rows(qa):
    row = lax.broadcasted_iota(jnp.int32, (16, qa.shape[2]), 0)
    ones = jnp.where(row == 0, 1.0, 0.0).astype(BF16)
    for h in range(qa.shape[0]):
        qa[h, 2 * HD :, :] = ones


def slot_block(me, s):
    return lax.bitwise_xor(me[0], lax.bitwise_and(s, 3)) * 2 + lax.shift_right_logical(s, 2)


def attn_fwd_kernel(heads, short_blocks, me, lens_s, lens_l, x, w, b, proj, *refs):
    outs = refs[:8]
    lse, scr, qa, ka, bcol = refs[8:]
    k = pl.program_id(0)
    block = slot_block(me, k)
    width = heads * HD
    span = x.shape[1]

    @pl.when(k == 0)
    def _():
        t = jnp.broadcast_to(b[...], (8, 2 * width)).T
        bcol[:width] = t[:width]
        bcol[width : 2 * width] = jnp.zeros((width, 8), F32)
        bcol[2 * width :] = t[width:]
        one_rows(qa)

    proj[0] = (dot(w[...], x[...], 0, 0) + bcol[:, 0:1]).astype(BF16)

    def run(seq_len, lens, first, together):
        score_operands(
            heads, span, seq_len, lens, first, proj[0, :width], proj[0, width : 2 * width], qa, ka
        )
        items = [(i, h) for i in range(span // seq_len) for h in range(heads)]
        groups = [items[n : n + together] for n in range(0, len(items), together)]

        def score(i, h):
            cols = slice(i * seq_len, (i + 1) * seq_len)
            return dot(ka[h, :, cols], qa[h, :, cols], 0, 0)

        scores = [score(*item) for item in groups[0]]
        for n, group in enumerate(groups):
            later = [score(*item) for item in groups[n + 1]] if n + 1 < len(groups) else None
            tops = [jnp.max(s, axis=0, keepdims=True) for s in scores]
            exps = [jnp.exp2(s - m) for s, m in zip(scores, tops)]
            sums = [jnp.sum(e, axis=0, keepdims=True) for e in exps]
            for (i, h), m, e, total in zip(group, tops, exps, sums):
                cols = slice(i * seq_len, (i + 1) * seq_len)
                val = proj[0, 2 * width + h * HD : 2 * width + (h + 1) * HD, cols]
                c = dot(val, e.astype(BF16), 1, 0) * (1.0 / total)
                scr[h * HD : (h + 1) * HD, cols] = c.astype(BF16)
                lse[0, h : h + 1, cols] = m + jnp.log2(total)
            scores = later

    @pl.when(block < short_blocks)
    def _():
        run(LS, lens_s, block * (span // LS), 6)

    @pl.when(block >= short_blocks)
    def _():
        run(LL, lens_l, (block - short_blocks) * (span // LL), 1)

    for i, out in enumerate(outs):

        @pl.when(k == i)
        def _():
            out[0] = scr[...]
            if i % 4:
                out[1] = x[...]


def attn_fwd(me, lens_s, lens_l, x, w, b):
    width, tokens = x.shape
    span = tokens // 8
    heads = width // HD
    short_blocks = lens_s.shape[0] * LS // span
    fixed = lambda k, *_: (0, 0)
    parts = [(2 if k % 4 else 1, width, span) for k in range(8)]
    return pl.pallas_call(
        functools.partial(attn_fwd_kernel, heads, short_blocks),
        grid_spec=pltpu.PrefetchScalarGridSpec(
            num_scalar_prefetch=3,
            grid=(8,),
            in_specs=[
                pl.BlockSpec((width, span), lambda k, me, *_: (0, slot_block(me, k))),
                pl.BlockSpec(w.shape, fixed),
                pl.BlockSpec(b.shape, fixed),
            ],
            out_specs=[
                pl.BlockSpec((1, 3 * width, span), lambda k, *_: (k, 0, 0)),
                *[pl.BlockSpec(part, lambda k, *_: (0, 0, 0)) for part in parts],
                pl.BlockSpec((1, heads, span), lambda k, *_: (k, 0, 0)),
            ],
            scratch_shapes=[
                pltpu.VMEM((width, span), BF16),
                pltpu.VMEM((heads, 2 * HD + 16, span), BF16),
                pltpu.VMEM((heads, 2 * HD + 16, span), BF16),
                pltpu.VMEM((3 * width, 8), F32),
            ],
        ),
        out_shape=[
            jax.ShapeDtypeStruct((8, 3 * width, span), BF16),
            *[jax.ShapeDtypeStruct(part, BF16) for part in parts],
            jax.ShapeDtypeStruct((8, heads, span), F32),
        ],
        cost_estimate=COST(16.0),
        compiler_params=pltpu.CompilerParams(vmem_limit_bytes=VMEM_LIMIT),
        name="attn_fwd",
    )(me, lens_s, lens_l, x, w, b)


def attn_bwd_kernel(first, count, heads, short_blocks, first_call, split, *refs):
    me, parity, lens_s, lens_l, x, w, proj, lse = refs[:8]
    gs = refs[8 : 8 + count]
    refs = refs[8 + count :]
    if not first_call:
        acc_in, bias_in = refs[:2]
        refs = refs[3:]
    gin = refs[0]
    if split == 0:
        acc, bias = refs[1:3]
        refs = refs[3:]
    elif split == 1:
        out, bias = refs[1:3]
        acc = refs[-1]
        refs = refs[3:-1]
    else:
        keep, send, extra = refs[1:4]
        bias, acc = refs[-2:]
        refs = refs[4:-2]
    dproj, gsc, qa, ka = refs
    step = pl.program_id(0)
    block = slot_block(me, first + step)
    width = heads * HD
    span = x.shape[1]
    scale = HD**-0.5

    @pl.when(step == 0)
    def _():
        one_rows(qa)

    for i, g in enumerate(gs):

        @pl.when(step == i)
        def _():
            gsc[...] = g[...]

    def run(seq_len, lens, first, together):
        score_operands(
            heads, span, seq_len, lens, first, proj[0, :width], proj[0, width : 2 * width], qa, ka
        )
        items = [(i, h) for i in range(span // seq_len) for h in range(heads)]
        groups = [items[n : n + together] for n in range(0, len(items), together)]

        def score(i, h):
            cols = slice(i * seq_len, (i + 1) * seq_len)
            val = proj[0, 2 * width + h * HD : 2 * width + (h + 1) * HD, cols]
            go = gsc[0, h * HD : (h + 1) * HD, cols]
            return dot(ka[h, :, cols], qa[h, :, cols], 0, 0), dot(val, go, 0, 0)

        pairs = [score(*item) for item in groups[0]]
        for n, group in enumerate(groups):
            later = [score(*item) for item in groups[n + 1]] if n + 1 < len(groups) else None
            ps = []
            for (i, h), (s, _) in zip(group, pairs):
                cols = slice(i * seq_len, (i + 1) * seq_len)
                ps.append(jnp.exp2(s - lse[0, h : h + 1, cols]))
            inner = [jnp.sum(p * gp, axis=0, keepdims=True) for p, (_, gp) in zip(ps, pairs)]
            gs = [(p * (gp - r)).astype(BF16) for p, (_, gp), r in zip(ps, pairs, inner)]
            for (i, h), p, g in zip(group, ps, gs):
                cols = slice(i * seq_len, (i + 1) * seq_len)
                rq, rk, rv = [slice(j * width + h * HD, j * width + (h + 1) * HD) for j in range(3)]
                go = gsc[0, h * HD : (h + 1) * HD, cols]
                dproj[rq, cols] = (dot(proj[0, rk, cols], g, 1, 0) * scale).astype(BF16)
                dproj[rk, cols] = (dot(proj[0, rq, cols], g, 1, 1) * scale).astype(BF16)
                dproj[rv, cols] = dot(go, p.astype(BF16), 1, 1).astype(BF16)
            pairs = later

    @pl.when(block < short_blocks)
    def _():
        run(LS, lens_s, block * (span // LS), 4)

    @pl.when(block >= short_blocks)
    def _():
        run(LL, lens_l, (block - short_blocks) * (span // LL), 1)

    gin[...] = dot(w[...], dproj[...], 1, 0) + gsc[1].astype(F32)
    part = dot(dproj[...], x[...], 1, 1)
    sums = dot(jnp.ones((8, span), BF16), dproj[...], 1, 1)

    @pl.when(step == 0)
    def _():
        if first_call:
            acc[...] = part
            bias[...] = sums
        else:
            acc[...] = acc_in[...] + part
            bias[...] = bias_in[...] + sums

    @pl.when(step > 0)
    def _():
        acc[...] += part
        bias[...] += sums

    if split == 1:

        @pl.when(step == count - 1)
        def _():
            rows = out.shape[1]
            for d in range(out.shape[0]):
                out[d] = acc[d * rows : (d + 1) * rows, :].astype(BF16)

    if split == 2:

        @pl.when(step == count - 1)
        def _():
            pairs, rows = keep.shape[:2]
            mine = parity[0]
            for d in range(pairs):
                a = pl.ds(pl.multiple_of((2 * d + mine) * rows, 8), rows)
                c = pl.ds(pl.multiple_of((2 * d + 1 - mine) * rows, 8), rows)
                keep[d] = acc[a, :].astype(BF16)
                send[d] = acc[c, :].astype(BF16)
            total = jnp.concatenate(
                [bias[:, i * width : (i + 1) * width] for i in range(3)], axis=0
            )
            extra[...] = total
            high = total.astype(BF16)
            send[pairs, :24] = high
            send[pairs, 24:48] = (total - high.astype(F32)).astype(BF16)


def attn_bwd(
    first, count, me, parity, lens_s, lens_l, x, w, proj, lse, g, carry, dp_count, split
):
    width, tokens = x.shape
    span = tokens // 8
    heads = width // HD
    short_blocks = lens_s.shape[0] * LS // span
    fixed = lambda k, *_: (0, 0)
    fixed3 = lambda k, *_: (0, 0, 0)
    here = lambda k, me, *_: (0, slot_block(me, first + k))
    slot = lambda k, *_: (first + k, 0, 0)
    first_call = carry is None
    acc_spec = pl.BlockSpec((3 * width, width), fixed)
    bias_spec = pl.BlockSpec((8, 3 * width), fixed)
    acc_shape = jax.ShapeDtypeStruct((3 * width, width), F32)
    bias_shape = jax.ShapeDtypeStruct((8, 3 * width), F32)
    mine = g[first : first + count]
    in_specs = [
        pl.BlockSpec((width, span), here),
        pl.BlockSpec(w.shape, fixed),
        pl.BlockSpec((1, 3 * width, span), slot),
        pl.BlockSpec((1, heads, span), slot),
    ] + [pl.BlockSpec((2, width, span), fixed3)] * len(mine)
    args = [x, w, proj, lse, *mine]
    aliases = {}
    if not first_call:
        gin, acc, bias = carry
        in_specs += [acc_spec, bias_spec, pl.BlockSpec(memory_space=pl.ANY)]
        args += [acc, bias, gin]
        aliases = {4 + len(args) - 1: 0}
    rows = 3 * width // dp_count
    scratch = []
    if split == 0:
        tail = [(acc_spec, acc_shape), (bias_spec, bias_shape)]
    elif split == 1:
        shape = (dp_count, rows, width)
        tail = [
            (pl.BlockSpec(shape, fixed3), jax.ShapeDtypeStruct(shape, BF16)),
            (bias_spec, bias_shape),
        ]
        scratch = [pltpu.VMEM(acc_shape.shape, F32)]
    else:
        keep = (dp_count // 2, rows, width)
        send = (dp_count // 2 + 1, rows, width)
        tail = [
            (pl.BlockSpec(keep, fixed3), jax.ShapeDtypeStruct(keep, BF16)),
            (pl.BlockSpec(send, fixed3), jax.ShapeDtypeStruct(send, BF16)),
            (pl.BlockSpec((24, width), fixed), jax.ShapeDtypeStruct((24, width), F32)),
        ]
        scratch = [pltpu.VMEM(bias_shape.shape, F32), pltpu.VMEM(acc_shape.shape, F32)]
    return pl.pallas_call(
        functools.partial(
            attn_bwd_kernel, first, count, heads, short_blocks, first_call, split
        ),
        grid_spec=pltpu.PrefetchScalarGridSpec(
            num_scalar_prefetch=4,
            grid=(count,),
            in_specs=in_specs,
            out_specs=[pl.BlockSpec((width, span), here)] + [t[0] for t in tail],
            scratch_shapes=[
                pltpu.VMEM((3 * width, span), BF16),
                pltpu.VMEM((2, width, span), BF16),
                pltpu.VMEM((heads, 2 * HD + 16, span), BF16),
                pltpu.VMEM((heads, 2 * HD + 16, span), BF16),
            ]
            + scratch,
        ),
        out_shape=[jax.ShapeDtypeStruct((width, tokens), F32)] + [t[1] for t in tail],
        input_output_aliases=aliases,
        cost_estimate=COST(4.0 * count),
        compiler_params=pltpu.CompilerParams(vmem_limit_bytes=VMEM_LIMIT),
        name=f"attn_bwd{first}",
    )(me, parity, lens_s, lens_l, *args)


def prep_kernel(w0, w1, w2, w3, *refs):
    params = refs[:6]
    owt, upt, dnt, upn, dnn, ub, cols, ow = refs[6:]
    weights = (w0, w1, w2, w3)
    model = owt.shape[0]
    width = model // 4

    def eye(n):
        a = lax.broadcasted_iota(jnp.int32, (n, n), 0)
        b = lax.broadcasted_iota(jnp.int32, (n, n), 1)
        return jnp.where(a == b, 1.0, 0.0).astype(BF16)

    big, small = eye(256), eye(width)
    for k, w in enumerate(weights):
        ks = slice(k * width, (k + 1) * width)
        ow[ks, :] = w[:width, :]
        for at in range(0, model, 256):
            lanes = slice(at, at + 256)
            for ref, first in ((upt, width), (dnt, 2 * width)):
                t = dot(big, w[first : first + width, lanes], 1, 1).astype(BF16)
                for g in range(4):
                    low, high = max(at, g * width), min(at + 256, (g + 1) * width)
                    if low < high:
                        start = k * width + low - g * width
                        ref[g, start : start + high - low, :] = t[low - at : high - at, :]
        bt = w[3 * width :, :].astype(F32).T
        ub[:, k : k + 1] = (bt[:, 2:3] + bt[:, 1:2]) + bt[:, 0:1]

    @pl.loop(0, model // 256)
    def _(i):
        at = pl.ds(pl.multiple_of(i * 256, 256), 256)
        owt[at, :] = dot(big, ow[:, at], 1, 1).astype(BF16)

    @pl.loop(0, 4)
    def _(g):
        upn[g] = dot(small, upt[g], 1, 1).astype(BF16)
        dnn[g] = dot(small, dnt[g], 1, 1).astype(BF16)

    for j, p in enumerate(params):
        cols[:, j : j + 1] = jnp.broadcast_to(p[...].reshape(1, model), (8, model)).T[:, 0:1]


def prep(weights, params):
    model = weights[0].shape[1]
    width = model // 4
    vmem = pl.BlockSpec(memory_space=pltpu.VMEM)
    shapes = [
        jax.ShapeDtypeStruct((model, model), BF16),
        jax.ShapeDtypeStruct((4, model, width), BF16),
        jax.ShapeDtypeStruct((4, model, width), BF16),
        jax.ShapeDtypeStruct((4, width, model), BF16),
        jax.ShapeDtypeStruct((4, width, model), BF16),
        jax.ShapeDtypeStruct((model, 8), F32),
        jax.ShapeDtypeStruct((model, 8), F32),
        jax.ShapeDtypeStruct((model, model), BF16),
    ]
    return pl.pallas_call(
        prep_kernel,
        in_specs=[vmem] * 10,
        out_specs=[vmem] * len(shapes),
        out_shape=shapes,
        cost_estimate=COST(4.0),
        compiler_params=pltpu.CompilerParams(vmem_limit_bytes=VMEM_LIMIT),
        name="prep",
    )(*weights, *params)


def mid_kernel(half, width, blocks, me, *refs):
    ctx, hid = refs[0:4], refs[4:8]
    og, ub, cols = refs[8:11]
    given = refs[11:17]
    at = 17
    if half:
        acc_hbm, vec_in = refs[at : at + 3], refs[at + 3]
        at += 5
    lo = refs[at]
    back = refs[at + 1 : at + 5]
    at += 5
    if half:
        keep, send, vec_out = refs[at : at + 3]
        at += 3
    else:
        acc_hbm, vec = refs[at : at + 3], refs[at + 3]
        at += 4
    (gow, gup, gdn, owt, upt, dnt, upn, dnn, ow) = refs[at : at + 9]
    at += 9
    (sums, act, slope, first, n1s, gps_s, cats, lows, sem, acc_sem) = refs[at : at + 10]
    if half:
        vec = refs[at + 10]
    accs = (gow, gup, gdn)
    step = pl.program_id(0)
    last = pl.num_programs(0) - 1
    model = 4 * width
    inv = 1.0 / model
    held = (owt, upt, dnn, dnt, upn, ow)

    def own(k):
        return pl.ds(pl.multiple_of(lax.bitwise_xor(me[0], k) * width, width), width)

    def fetch(i):
        return pltpu.make_async_copy(given[i], held[i], sem.at[i])

    def ready(i):
        @pl.when(step == 0)
        def _():
            fetch(i).wait()

    def acc_copy(i):
        if half:
            return pltpu.make_async_copy(acc_hbm[i], accs[i], acc_sem.at[i])
        return pltpu.make_async_copy(accs[i], acc_hbm[i], acc_sem.at[i])

    @pl.when(step == 0)
    def _():
        for i in range(6):
            fetch(i).start()
        if half:
            for i in range(3):
                acc_copy(i).start()
        row = lax.broadcasted_iota(jnp.int32, (16, TILE), 0)
        for g in range(4):
            lows[g, width:, :] = jnp.where(row == 0, 1.0, 0.0).astype(BF16)
        sums[...] = jnp.zeros_like(sums)

    def before(value):
        return value if half else jnp.where(step == 0, 0.0, value)

    def acc_ready(i):
        if half:

            @pl.when(step == 0)
            def _():
                acc_copy(i).wait()

    def acc_done(i):
        if not half:

            @pl.when(step == last)
            def _():
                acc_copy(i).start()

    def col(j):
        return cols[:, j : j + 1]

    def add_sum(j, value):
        sums[j] += sum(value[:, i : i + 128] for i in range(0, TILE, 128))

    for k in range(4):
        cats[k * width : (k + 1) * width, :] = ctx[k][0]
    ready(0)
    first[...] = dot(owt[...], cats[...], 1, 0) + col(0)
    for k in range(4):
        first[own(k), :] += hid[k][...].reshape(width, TILE).astype(F32)
    pre = first[...]
    cen = pre - jnp.sum(pre, axis=0, keepdims=True) * inv
    r1 = lax.rsqrt(jnp.sum(cen * cen, axis=0, keepdims=True) * inv + EPSILON)
    n1 = cen * r1
    n1s[...] = n1
    normed = n1 * col(1) + col(2)
    first[...] = normed
    low = normed.astype(BF16)
    for g in range(4):
        lows[g, :width, :] = low[g * width : (g + 1) * width, :]
    ready(1)
    ready(2)

    def pre_act(g):
        return dot(upt[g], lows[g, :width, :], 1, 0)

    later = pre_act(0)
    for g in range(4):
        rows = slice(g * width, (g + 1) * width)
        raw = later
        if g < 3:
            later = pre_act(g + 1)
        for k in range(4):
            units = slice(k * width, (k + 1) * width)
            pa = raw[units, :] + ub[rows, k : k + 1]
            phi, sl = gelu_parts(pa)
            act[g, units, :] = (pa * phi).astype(BF16)
            slope[g, units, :] = sl
        first[rows, :] += dot(dnn[g], act[g], 1, 0) + cols[rows, 3:4]
    pre = first[...]
    cen = pre - jnp.sum(pre, axis=0, keepdims=True) * inv
    r2 = lax.rsqrt(jnp.sum(cen * cen, axis=0, keepdims=True) * inv + EPSILON)
    n2 = cen * r2
    lo[...] = (n2 * col(4) + col(5)).astype(BF16).T
    ogt = og[...].T.astype(F32)
    add_sum(4, ogt * n2)
    add_sum(5, ogt)
    u = ogt * col(4)
    gps = r2 * (
        u
        - jnp.sum(u, axis=0, keepdims=True) * inv
        - n2 * (jnp.sum(u * n2, axis=0, keepdims=True) * inv)
    )
    add_sum(3, gps)
    gdl = gps.astype(BF16)
    gps_s[...] = gps
    ready(3)
    ready(4)
    acc_ready(1)
    acc_ready(2)

    def grad_act(g):
        return dot(dnt[g], gdl[g * width : (g + 1) * width, :], 1, 0)

    later = grad_act(0)
    for g in range(4):
        rows = slice(g * width, (g + 1) * width)
        raw = later
        if g < 3:
            later = grad_act(g + 1)
        gdn[g] = before(gdn[g]) + dot(act[g], gdl[rows, :], 1, 1)
        gpa = (raw * slope[g]).astype(BF16)
        gup[g] = before(gup[g]) + dot(gpa, lows[g], 1, 1)
        gps_s[rows, :] += dot(upn[g], gpa, 1, 0)
    acc_done(1)
    acc_done(2)
    gn = gps_s[...]
    n1 = n1s[...]
    add_sum(1, gn * n1)
    add_sum(2, gn)
    u = gn * col(1)
    gpf = r1 * (
        u
        - jnp.sum(u, axis=0, keepdims=True) * inv
        - n1 * (jnp.sum(u * n1, axis=0, keepdims=True) * inv)
    )
    gpl = gpf.astype(BF16)
    first[...] = gpl.astype(F32)
    add_sum(0, first[...])
    ready(5)
    acc_ready(0)
    gow[...] = before(gow[...]) + dot(gpl, cats[...], 1, 1)
    acc_done(0)
    for k in range(4):
        back[k][1] = first[own(k), :].astype(BF16)
        back[k][0] = dot(ow[k * width : (k + 1) * width, :], gpl, 1, 0).astype(BF16)

    @pl.when(step == last)
    def _():
        lane = lax.broadcasted_iota(jnp.int32, (1, 128), 1)
        total = vec_in[...] if half else jnp.zeros((model, 128), F32)
        for j in range(6):
            total += jnp.where(lane == j, jnp.sum(sums[j], axis=1, keepdims=True), 0.0)
        vec[...] = total
        if half:
            for g in range(4):
                for k in range(4):
                    vec[own(k), :] += jnp.where(
                        lane == 6 + g, gup[g, k * width : (k + 1) * width, width : width + 1], 0.0
                    )
            more = vec[...].T[:16]
            vec_out[...] = more
            part = width // blocks

            @pl.loop(0, 2)
            def _(far):
                for near in range(2):
                    dest = send if near else keep
                    units = pl.ds(pl.multiple_of((2 * far + near) * width, 8), width)
                    up_rows = pl.ds(pl.multiple_of(far * 3 * width, 16), width)
                    down_rows = pl.ds(pl.multiple_of((far * 3 + 1) * width, 16), width)
                    for g in range(4):
                        lanes = slice(g * width, (g + 1) * width)
                        dest[up_rows, lanes] = gup[g, units, :width].T.astype(BF16)
                        dest[down_rows, lanes] = gdn[g, units, :].T.astype(BF16)

            pairs = 2 if blocks > 1 else 1

            @pl.loop(0, blocks // pairs)
            def _(pair):
                for k in range(4):
                    dest = send if k % 2 else keep
                    base = ((k // 2) * 3 + 2) * width
                    units = slice(k * width, (k + 1) * width)
                    to = pl.ds(pl.multiple_of(base + pair * pairs * part, 16), pairs * part)
                    for g in range(4):
                        lanes = slice(g * width, (g + 1) * width)
                        rows = []
                        for i in range(pairs):
                            start = ((pair * pairs + i) * 4 + g) * part
                            rows.append(gow[pl.ds(pl.multiple_of(start, 8), part), units])
                        dest[to, lanes] = jnp.concatenate(rows, axis=0).astype(BF16)

            if blocks > 1:
                high = more.astype(BF16)
                send[6 * width : 6 * width + 16, :] = high
                send[6 * width + part : 6 * width + part + 16, :] = (
                    more - high.astype(F32)
                ).astype(BF16)
        else:
            for i in range(3):
                acc_copy(i).wait()


def mid(half, me, ctx, hid, og, ready, carry, blocks):
    width, span = ctx[0].shape[1:]
    model = 4 * width
    steps = span // TILE
    whole2 = lambda i, *_: (0, 0)
    ctx_tile = pl.BlockSpec((1, width, TILE), lambda i, *_: (0, 0, i))
    hid_own = pl.BlockSpec((width, TILE), lambda i, me: (0, (me[0] * 2 + half) * steps + i))
    hid_tile = pl.BlockSpec((1, width, TILE), lambda i, *_: (1, 0, i))
    back_tile = pl.BlockSpec((2, width, TILE), lambda i, *_: (0, 0, i))
    row_in = pl.BlockSpec((TILE, model), lambda i, *_: (half * steps + i, 0))
    hbm = pl.BlockSpec(memory_space=pl.ANY)
    column = pl.BlockSpec((model, 8), whole2)
    vec_spec = pl.BlockSpec((model, 128), whole2)
    owt, upt, dnt, upn, dnn, ub, cols, ow = ready
    in_specs = [ctx_tile] * 4 + [hid_own] + [hid_tile] * 3 + [row_in, column, column] + [hbm] * 6
    args = [*ctx, *hid, og, ub, cols, owt, upt, dnn, dnt, upn, ow]
    accs = [(model, model), (4, model, width + 16), (4, model, width)]
    piece = jax.ShapeDtypeStruct((2, width, span), BF16)
    scratch = [pltpu.VMEM(a, F32) for a in accs] + [
        pltpu.VMEM((model, model), BF16),
        pltpu.VMEM((4, model, width), BF16),
        pltpu.VMEM((4, model, width), BF16),
        pltpu.VMEM((4, width, model), BF16),
        pltpu.VMEM((4, width, model), BF16),
        pltpu.VMEM((model, model), BF16),
        pltpu.VMEM((6, model, 128), F32),
        pltpu.VMEM((4, model, TILE), BF16),
        pltpu.VMEM((4, model, TILE), F32),
        pltpu.VMEM((model, TILE), F32),
        pltpu.VMEM((model, TILE), F32),
        pltpu.VMEM((model, TILE), F32),
        pltpu.VMEM((model, TILE), BF16),
        pltpu.VMEM((4, width + 16, TILE), BF16),
        pltpu.SemaphoreType.DMA((6,)),
        pltpu.SemaphoreType.DMA((3,)),
    ]
    aliases = {}
    if half:
        in_specs += [hbm] * 3 + [vec_spec, hbm]
        aliases = {len(args) + 5: 0}
        args += list(carry)
        extra = 2 * (width // blocks) if blocks > 1 else 0
        rows = [6 * width, 6 * width + extra]
        tail_specs = [pl.BlockSpec((r, model), whole2) for r in rows + [16]]
        tail_shapes = [jax.ShapeDtypeStruct((r, model), BF16) for r in rows]
        tail_shapes += [jax.ShapeDtypeStruct((16, model), F32)]
        scratch += [pltpu.VMEM((model, 128), F32)]
    else:
        tail_specs = [hbm] * 3 + [vec_spec]
        tail_shapes = [jax.ShapeDtypeStruct(a, F32) for a in accs + [(model, 128)]]
    return pl.pallas_call(
        functools.partial(mid_kernel, half, width, blocks),
        grid_spec=pltpu.PrefetchScalarGridSpec(
            num_scalar_prefetch=1,
            grid=(steps,),
            in_specs=in_specs,
            out_specs=[row_in] + [back_tile] * 4
            + tail_specs,
            scratch_shapes=scratch,
        ),
        out_shape=[jax.ShapeDtypeStruct((2 * span, model), BF16)] + [piece] * 4 + tail_shapes,
        input_output_aliases=aliases,
        cost_estimate=COST(25.0),
        compiler_params=pltpu.CompilerParams(vmem_limit_bytes=VMEM_LIMIT),
        name=f"mid{half}",
    )(me, *args)


def put_pair(ref, at, value):
    rows = value.shape[0]
    high = value.astype(BF16)
    ref[at, :rows] = high
    ref[at + 1, :rows] = (value - high.astype(F32)).astype(BF16)


def get_pair(ref, at, rows):
    return ref[at, :rows].astype(F32) + ref[at + 1, :rows].astype(F32)


def split_kernel(bit0, bit1, keep, recv, pair, extra, kept, sent_y, sent_z, extra_out):
    per = keep.shape[0] // 3
    half = per // 2
    rows = extra.shape[0]
    more = extra[...] + get_pair(pair, 0, rows)
    extra_out[...] = more
    high = more.astype(BF16).astype(F32)
    term = jnp.where(pl.program_id(0) == 0, high, more - high)
    sent_y[2 * half, :rows] = term.astype(BF16)
    low, far = bit0[0], bit1[0]

    def total(i):
        return (keep[i].astype(F32) + recv[i].astype(F32)).astype(BF16)

    for section in range(3):
        base = section * per
        for e in range(half):
            if section < 2:
                mine, other = base + 2 * e + low, base + 2 * e + 1 - low
                dest, at = sent_y, section * half + e
            else:
                first = base + 4 * (e // 2) + e % 2
                mine, other = first + 2 * far, first + 2 * (1 - far)
                dest, at = sent_z, e
            kept[section * half + e] = total(mine)
            dest[at] = total(other)


def split(bits, keep, recv, extra, name):
    size, rows, lanes = keep.shape
    half = size // 12
    smem = pl.BlockSpec(memory_space=pltpu.SMEM)
    step = lambda n: pl.BlockSpec((n, rows, lanes), lambda k: (k, 0, 0))
    whole = pl.BlockSpec(extra.shape, lambda k: (0, 0))
    sizes = [3 * half, 2 * half + 1, half]
    return pl.pallas_call(
        split_kernel,
        grid=(2,),
        in_specs=[
            smem,
            smem,
            step(size // 2),
            step(size // 2),
            pl.BlockSpec((2, rows, lanes), lambda k: (size // 2, 0, 0)),
            whole,
        ],
        out_specs=[step(n) for n in sizes] + [whole],
        out_shape=[jax.ShapeDtypeStruct((2 * n, rows, lanes), BF16) for n in sizes]
        + [jax.ShapeDtypeStruct(extra.shape, F32)],
        cost_estimate=COST(1.0),
        compiler_params=pltpu.CompilerParams(vmem_limit_bytes=VMEM_LIMIT),
        name=name,
    )(*bits, keep, recv, recv, extra)


def join_kernel(keep, recv_y, recv_z, extra, kept, sent, extra_out):
    half = keep.shape[0] // 6
    rows, part = extra.shape[0], 2 * half + 1
    terms = [recv_y[k * part + 2 * half, :rows].astype(F32) for k in range(2)]
    more = extra[...] + (terms[0] + terms[1])
    extra_out[...] = more
    put_pair(sent, 3 * half, more)
    for k in range(2):
        for section in range(3):
            for e in range(half):
                if section < 2:
                    other = recv_y[k * part + section * half + e]
                else:
                    other = recv_z[k * half + e]
                value = keep[(k * 3 + section) * half + e].astype(F32) + other.astype(F32)
                (sent if k else kept)[section * half + e] = value.astype(BF16)


def early_kernel(bit0, bit1, keep, recv, extra, kept, sent_z, sent_y, extra_out):
    size = keep.shape[0]
    half = size // 6
    more = extra[...] + get_pair(recv, size, extra.shape[0])
    extra_out[...] = more
    put_pair(sent_z, 2 * half, more)

    def total(i):
        return (keep[i].astype(F32) + recv[i].astype(F32)).astype(BF16)

    for section in range(3):
        mine = bit1[0] if section < 2 else bit0[0]
        for e in range(half):
            at = section * 2 * half + 2 * e
            kept[section * half + e] = total(at + mine)
            if section < 2:
                sent_z[section * half + e] = total(at + 1 - mine)
            else:
                sent_y[e] = total(at + 1 - mine)


def combine(kernel, bits, args, sizes, name):
    rows, lanes = args[0].shape[1:]
    vmem = pl.BlockSpec(memory_space=pltpu.VMEM)
    shapes = [jax.ShapeDtypeStruct((n, rows, lanes), BF16) for n in sizes]
    shapes.append(jax.ShapeDtypeStruct(args[-1].shape, F32))
    return pl.pallas_call(
        kernel,
        in_specs=[pl.BlockSpec(memory_space=pltpu.SMEM)] * len(bits) + [vmem] * len(args),
        out_specs=[vmem] * len(shapes),
        out_shape=shapes,
        cost_estimate=COST(1.0),
        compiler_params=pltpu.CompilerParams(vmem_limit_bytes=VMEM_LIMIT),
        name=name,
    )(*bits, *args)


def pulled(kernel, bits, count, *refs):
    bits, refs = refs[:bits], refs[bits:]
    bufs, sem = refs[-count - 1 : -1], refs[-1]
    copies = [pltpu.make_async_copy(refs[i], bufs[i], sem.at[i]) for i in range(count)]
    for c in copies:
        c.start()
    for c in copies:
        c.wait()
    kernel(*bits, *bufs, *refs[count : -count - 1])


def pull_call(kernel, count, bits, args, shapes, name):
    vmem = pl.BlockSpec(memory_space=pltpu.VMEM)
    return pl.pallas_call(
        functools.partial(pulled, kernel, len(bits), count),
        in_specs=[pl.BlockSpec(memory_space=pltpu.SMEM)] * len(bits)
        + [pl.BlockSpec(memory_space=pltpu.HBM)] * count
        + [vmem] * (len(args) - count),
        out_specs=[vmem] * len(shapes),
        out_shape=shapes,
        scratch_shapes=[pltpu.VMEM(a.shape, a.dtype) for a in args[:count]]
        + [pltpu.SemaphoreType.DMA((count,))],
        cost_estimate=COST(1.0),
        compiler_params=pltpu.CompilerParams(vmem_limit_bytes=VMEM_SMALL),
        name=name,
    )(*bits, *args)


def combine_early(bits, keep, recv, extra, name):
    size, rows, lanes = keep.shape
    half = size // 6
    shapes = [
        jax.ShapeDtypeStruct((3 * half, rows, lanes), BF16),
        jax.ShapeDtypeStruct((2 * half + 2, rows, lanes), BF16),
        jax.ShapeDtypeStruct((half, rows, lanes), BF16),
        jax.ShapeDtypeStruct(extra.shape, F32),
    ]
    return pull_call(early_kernel, 3, bits, [keep, recv, extra], shapes, name)


def qkv_kernel(index, qk, qb, qr, kept, sent, qb_out):
    size = qk.shape[0]
    more = qb[...] + (qr[size, :24].astype(F32) + qr[size, 24:48].astype(F32))
    qb_out[...] = more
    hi = more.astype(BF16)
    sent[size // 2, :24] = hi
    sent[size // 2, 24:48] = (more - hi.astype(F32)).astype(BF16)
    mine = index[0]
    for i in range(size // 2):
        a, b = 2 * i + mine, 2 * i + 1 - mine
        kept[i] = (qk[a].astype(F32) + qr[a].astype(F32)).astype(BF16)
        sent[i] = (qk[b].astype(F32) + qr[b].astype(F32)).astype(BF16)


def qkv_stage(index, qk, qb, qr, name):
    size, rows, lanes = qk.shape
    shapes = [
        jax.ShapeDtypeStruct((size // 2, rows, lanes), BF16),
        jax.ShapeDtypeStruct((size // 2 + 1, rows, lanes), BF16),
        jax.ShapeDtypeStruct(qb.shape, F32),
    ]
    return pull_call(qkv_kernel, 2, [index], [qk, qb, qr], shapes, name)


def blend_kernel(joint, last, index, wk, wr, vec, qk, *refs):
    if not joint:
        wy, qr, qb, refs = refs[0], refs[1], refs[2], refs[3:]
    nw, rows, model = wk.shape
    nq, width = qk.shape[0], qk.shape[2]
    pitch = model // 3
    if joint:
        terms = wr[nw].astype(F32)
        more = vec[:12] + (terms[:12] + terms[12:24])
    else:
        more = vec[:12] + get_pair(wr, wr.shape[0] - 2, 16)[:12]
        bias = qb[...] + (qr[nq, :24].astype(F32) + qr[nq, 24:48].astype(F32))

    def wsum(section, i):
        at = section * (nw // 3) + i
        other = wr[at] if joint or section < 2 else wy[i]
        return wk[at].astype(F32) + other.astype(F32)

    def qsum(i, j):
        part = slice(j * rows, (j + 1) * rows)
        if joint:
            other = wr[nw + 1 + i, :, j * pitch : j * pitch + width]
        else:
            other = qr[i, part, :]
        return qk[i, part, :].astype(F32) + other.astype(F32)

    if last:
        gup, gdn, gow, gqkv, gqv, gub = refs[:6]
        vecs = refs[6:]
        gup[...] = wsum(0, 0)
        gdn[...] = wsum(1, 0)
        ow = wsum(2, 0)
        quarter = model // 4
        gow[...] = jnp.concatenate(
            [ow[:, j * quarter : (j + 1) * quarter] for j in range(4)], axis=0
        ).T
        for j in range(3):
            gqkv[j * rows : (j + 1) * rows, :] = qsum(0, j)
        gqv[:, :width] = more[10:11, :width]
        gqv[:, width:] = more[10:11, 2 * pitch : 2 * pitch + width]
        own = vecs[0].shape[0]
        more = jnp.concatenate([more, jnp.zeros((4, model), F32)], axis=0)
        here = pltpu.roll(more, index[1], 1)
        for j, v in enumerate(vecs):
            v[...] = here[j, :own]
        here = pltpu.roll(more, index[2], 1)
        gub[...] = jnp.concatenate([here[6 + j, :quarter] for j in range(4)])
        return
    wkept, sent, vec_out, qkept = refs
    mine = index[0]
    vec_out[:12] = more
    vec_out[12:] = jnp.zeros((4, model), F32)
    if not joint:
        for j in range(3):
            vec_out[10:11, j * pitch : j * pitch + width] = bias[8 * j : 8 * j + 1]
    half = nw // 2
    more = vec_out[:12]
    hi = more.astype(BF16).astype(F32)
    sent[half, :24] = jnp.concatenate([hi, more - hi], axis=0).astype(BF16)
    for i in range(3):
        wkept[i] = wsum(i, mine).astype(BF16)
        sent[i] = wsum(i, 1 - mine).astype(BF16)
    at = half + 1
    for i in range(nq // 2):
        for j in range(3):
            qkept[i, j * rows : (j + 1) * rows, :] = qsum(2 * i + mine, j).astype(BF16)
            sent[at + i, :, j * pitch : j * pitch + width] = qsum(2 * i + 1 - mine, j).astype(BF16)


def blend(index, wk, wr, wy, vec, qk, qr, qb, last, name):
    nw, rows, model = wk.shape
    nq, _, width = qk.shape
    vmem = pl.BlockSpec(memory_space=pltpu.VMEM)
    args = [wk, wr, vec, qk] + ([] if qr is None else [wy, qr, qb])
    shape = jax.ShapeDtypeStruct
    if last:
        quarter = model // 4
        shapes = [
            shape((rows, model), F32),
            shape((rows, model), F32),
            shape((quarter, 4 * rows), F32),
            shape((3 * rows, width), F32),
            shape((1, 2 * width), F32),
            shape((model,), F32),
        ] + [shape((rows,), F32)] * 6
    else:
        shapes = [
            shape((nw // 2, rows, model), BF16),
            shape((nw // 2 + nq // 2 + 1, rows, model), BF16),
            shape(vec.shape, F32),
            shape((nq // 2, 3 * rows, width), BF16),
        ]
    return pl.pallas_call(
        functools.partial(blend_kernel, qr is None, last),
        in_specs=[pl.BlockSpec(memory_space=pltpu.SMEM)] + [vmem] * len(args),
        out_specs=[vmem] * len(shapes),
        out_shape=shapes,
        cost_estimate=COST(1.0),
        compiler_params=pltpu.CompilerParams(vmem_limit_bytes=VMEM_SMALL),
        name=name,
    )(index, *args)


def swap(value, axis, bit):
    count = lax.axis_size(axis)
    return lax.ppermute(value, axis, [(i, i ^ bit) for i in range(count)])


def to_chan(pieces):
    return [pieces[0]] + [swap(pieces[k], "chan", k) for k in range(1, 4)]


def gather_chan(value):
    near = swap(value, "chan", 1)
    far = swap(value, "chan", 2)
    return [value, near, far, swap(far, "chan", 1)]


def scatter_dp(pieces):
    index = lax.axis_index("dp")
    count, bit = pieces.shape[0], 1
    while count > 1:
        view = pieces.reshape((count // 2, 2) + pieces.shape[1:])
        digit = (index // bit) % 2
        mine = lax.dynamic_index_in_dim(view, digit, 1, keepdims=False).astype(F32)
        other = lax.dynamic_index_in_dim(view, 1 - digit, 1, keepdims=False)
        total = mine + swap(other, "dp", bit).astype(F32)
        count, bit = count // 2, bit * 2
        pieces = total if count == 1 else total.astype(pieces.dtype)
    return pieces[0]


def sum_dp(value):
    bit = 1
    while bit < lax.axis_size("dp"):
        value = value + swap(value, "dp", bit)
        bit *= 2
    return value


def pack_kernel(ow, up, dn, ub, weights):
    width = ow.shape[0]
    for i, w in enumerate((ow, up, dn)):
        weights[i * width : (i + 1) * width, :] = w[...]
    whole = jnp.broadcast_to(ub[...].reshape(1, -1), (16, ub.shape[0]))
    high = whole.astype(BF16)
    rest = whole - high.astype(F32)
    middle = rest.astype(BF16)
    low = (rest - middle.astype(F32)).astype(BF16)
    row = lax.broadcasted_iota(jnp.int32, whole.shape, 0)
    terms = jnp.where(
        row == 0,
        high.astype(F32),
        jnp.where(row == 1, middle.astype(F32), low.astype(F32)),
    )
    weights[3 * width :, :] = terms.astype(BF16)


def pack(ow, up, dn, ub):
    width, model = ow.shape
    vmem = pl.BlockSpec(memory_space=pltpu.VMEM)
    return pl.pallas_call(
        pack_kernel,
        in_specs=[vmem] * 4,
        out_specs=vmem,
        out_shape=jax.ShapeDtypeStruct((3 * width + 16, model), BF16),
        cost_estimate=COST(1.0),
        compiler_params=pltpu.CompilerParams(vmem_limit_bytes=VMEM_LIMIT),
        name="pack",
    )(ow, up, dn, ub)


def digit(value, b):
    return ((value >> b) & 1)[None]


def reduce_plain(keep, send, vec, dp_count):
    width, model = keep.shape[0] // 6, keep.shape[1]
    sections = 3
    keep = keep.reshape(2, 3, width, model)
    send = send[: 6 * width].reshape(2, 3, width, model)
    rows = width // dp_count
    keep = keep + swap(send, "chan", 1)
    keep = keep[0] + swap(keep[1], "chan", 2)
    if rows < 16:
        last = keep[2].reshape(width, 4, width).transpose(1, 0, 2).reshape(width, model)
        last = last.reshape(dp_count, 4, rows, width).transpose(0, 2, 1, 3)
        keep = jnp.stack([keep[0], keep[1], last.reshape(width, model)])
    keep = keep.reshape(sections, dp_count, rows, model).transpose(1, 0, 2, 3)
    vec = vec + swap(vec, "chan", 1)
    vec = sum_dp(vec + swap(vec, "chan", 2))
    return scatter_dp(keep), vec


def on_device(
    hidden_in,
    lengths_short,
    lengths_long,
    qkv_weight,
    qv_bias,
    out_weight,
    mixer_bias,
    first_gain,
    first_shift,
    up_weight,
    up_bias,
    down_weight,
    down_bias,
    second_gain,
    second_shift,
    out_grad,
):
    width, tokens = hidden_in.shape
    span = tokens // 8
    model = 4 * width
    dp_count = lax.axis_size("dp")
    chan = lax.axis_index("chan").astype(jnp.int32)
    dp = lax.axis_index("dp").astype(jnp.int32)
    me = chan[None]
    bar = lax.optimization_barrier
    fine = width // dp_count >= 16 and dp_count == 8
    lengths = (lengths_short, lengths_long)
    w = qkv_weight[0]

    packed = pack(out_weight, up_weight, down_weight, up_bias)
    params = [mixer_bias, first_gain, first_shift, down_bias, second_gain, second_shift]
    far = swap(packed, "chan", 2)
    near = swap(packed, "chan", 1)
    x, _ = bar((hidden_in, packed))
    proj, *parts, lse = attn_fwd(me, *lengths, x, w, qv_bias)
    parts = [parts[:4], parts[4:]]
    far, near, parts = bar((far, near, parts))
    first = to_chan(parts[0])
    weights = [packed, near, far, swap(far, "chan", 1)]
    ready = prep(weights, params)
    second = to_chan(parts[1])
    blocks = dp_count if fine else 1
    hid = [hidden_in] + first[1:]
    lo, *rest = mid(0, me, first, hid, out_grad, ready, None, blocks)
    g0, carry = rest[:4], [*rest[4:], lo]
    g0, carry, second = bar((g0, carry, second))
    back0 = to_chan(g0)
    hid = [hidden_in] + second[1:]
    lo, *rest = mid(1, me, second, hid, out_grad, ready, carry, blocks)
    rest, back0 = bar((rest, back0))
    g1, (keep, send, vec) = rest[:4], rest[4:]
    recv = swap(send, "chan", 1)
    back = [*back0, *to_chan(g1)]
    parity = digit(dp, 0)

    def backward(start, count, x, carry, split):
        return attn_bwd(
            start,
            count,
            me,
            parity,
            *lengths,
            x,
            w,
            proj,
            lse,
            back,
            carry,
            dp_count,
            split,
        )

    if not fine:
        sums, vec = reduce_plain(keep, send, vec, dp_count)
        carry = backward(0, 5, hidden_in, None, 0)
        grad_input, gq, gbias = backward(5, 3, hidden_in, carry, 1)
        gq, gbias = scatter_dp(gq), sum_dp(gbias[0])
        own = width // dp_count
        mine = lax.dynamic_slice_in_dim(vec[:6], (dp * 4 + chan) * own, own, 1)
        mine = [mine[i] for i in range(6)]
        gub = lax.dynamic_slice_in_dim(vec[6:10], chan * width, width, 1).reshape(model)
        gup, gdn = sums[0], sums[1]
        gow = sums[2].reshape(-1, 4, width).transpose(1, 0, 2).reshape(model // dp_count, width).T
        gqv = jnp.concatenate([gbias[:width], gbias[2 * width :]])[None]
    else:
        rows = width // dp_count
        size = 6 * dp_count
        recv = recv.reshape(size + 2, rows, model)
        keep = keep.reshape(size, rows, model)

        bits = [parity, digit(dp, 1)]
        keep, send_y, send_z, vec = split(bits, keep, recv, vec, "combine0")
        recv_y, recv_z = swap(send_y, "dp", 1), swap(send_z, "dp", 2)
        x, keep = bar((hidden_in, keep))
        carry = backward(0, 5, x, None, 0)
        recv_y, recv_z, carry = bar((recv_y, recv_z, carry))
        keep, send, vec = combine(
            join_kernel, [], [keep, recv_y, recv_z, vec], [12, 14], "combine1"
        )
        recv = swap(send, "chan", 2)
        x, keep = bar((x, keep))
        grad_input, gk, gs, gbias = backward(5, 3, x, carry, 2)
        recv, gk, gs = bar((recv, gk, gs))
        grecv = swap(gs, "dp", 1)
        keep, send_z, send_y, vec = combine_early(bits, keep, recv, vec, "combine2")
        recv_z, recv_y = swap(send_z, "dp", 2), swap(send_y, "dp", 1)
        grecv, keep = bar((grecv, keep))
        gk, gs, gbias = qkv_stage(bits[1], gk, gbias, grecv, "qkv2")
        grecv = swap(gs, "dp", 2)
        recv_z, recv_y, gk = bar((recv_z, recv_y, gk))
        keep, send, vec, gk = blend(
            digit(dp, 2), keep, recv_z, recv_y, vec, gk, grecv, gbias, False, "blend2"
        )
        recv = swap(send, "dp", 4)
        index = jnp.stack(
            [
                jnp.zeros_like(dp),
                (model - (dp * 4 + chan) * rows) % model,
                (model - chan * width) % model,
            ]
        )
        gup, gdn, gow, gq, gqv, gub, *mine = blend(
            index, keep, recv, None, vec, gk, None, None, True, "blend"
        )
    return (
        lo,
        grad_input,
        gq.T[None],
        gqv,
        gow,
        mine[0],
        mine[1],
        mine[2],
        gup,
        gub,
        gdn,
        mine[3],
        mine[4],
        mine[5],
    )


def solution(mesh):
    in_specs = (
        P("chan", "dp"),
        P("dp"),
        P("dp"),
        P("chan", None, None),
        P("chan", None),
        P("chan", None),
        P(),
        P(),
        P(),
        P(None, "chan"),
        P("chan"),
        P(None, "chan"),
        P(),
        P(),
        P(),
        P(("dp", "chan"), None),
    )
    out_specs = (
        P(("dp", "chan"), None),
        P("chan", "dp"),
        P("chan", None, "dp"),
        P("chan", None),
        P("chan", "dp"),
        P(("dp", "chan")),
        P(("dp", "chan")),
        P(("dp", "chan")),
        P("dp", "chan"),
        P("chan"),
        P("dp", "chan"),
        P(("dp", "chan")),
        P(("dp", "chan")),
        P(("dp", "chan")),
    )
    return jax.shard_map(
        on_device, mesh=mesh, in_specs=in_specs, out_specs=out_specs, check_vma=False
    )
```
